256 devices in a mesh: ens: 2 (over x_lo), sx: 16 (over x_hi, y, core), sy: 8 (over z).
Axes of the slice: x: 4 (x_hi: 2, x_lo: 2; x = x_hi * 2 + x_lo), y: 4, z: 8, core: 2. Of those that a mesh axis runs over, the one named last changes fastest.
Arguments:
- snapshots: bfloat16 [4, 4, 128, 512, 512], P('ens', None, 'sx', 'sy'), may hold values from -6 to 6
- coefficients: bfloat16 [4, 256, 512], P('ens'), may hold values from -0.125 to 0.125
- modes: bfloat16 [4, 128, 512, 256], P(None, 'sx', 'sy'), may hold values from -12 to 12
Outputs:
- new_modes: bfloat16 [4, 128, 512, 256], P(None, 'sx', 'sy')
- gram: float32 [256, 256], replicated
- proj: float32 [4, 256, 512], P('ens')
The draws below stay inside these ranges and needn't reach their ends.
All inputs are finite; a program needn't handle non-finite values.
Results may differ from the reference program's by a relative error of at most 0.005.
Values may be sent and summed in bfloat16 or wider, within the bound.
No kernel may reach another device: no remote copies, remote signals or barrier semaphores. Data moves between devices by JAX's collectives and lax.ppermute only.
A program may use at most 64 MiB of HBM per device.

```python
import math
import jax
import jax.numpy as jnp
from jax import lax

R = 256
SNAPS = 512
LEV = 4
ENS = 4
NX = 128
NY = 512


def draw_modes(key, part):
    first, second, third = jax.random.split(key, 3)
    base = jnp.clip(jax.random.normal(first, (LEV, NX, NY, R), jnp.float32), -5.0, 5.0)
    column_scale = jnp.exp(jax.random.uniform(second, (R,), jnp.float32, math.log(0.05), math.log(2.0)))
    rough = jax.random.uniform(third, (LEV, NX, NY, 1), jnp.float32, 0.6, 1.4)
    rising = 1.0 + 2.0 * jnp.arange(NX, dtype=jnp.float32) / max(NX - 1, 1)
    values = base * column_scale[None, None, None, :] * rough * rising[None, :, None, None]
    return jnp.clip(values, -12.0, 12.0).astype(jnp.bfloat16)


def steps_of(rng, shape, pieces, least, top_value):
    loudness, own = 1.0, jax.random.fold_in(rng, 6)
    for axis_at, shards_of in pieces:
        steps = jnp.exp(jax.random.uniform(jax.random.fold_in(own, axis_at), (shards_of,), jnp.float32, least / len(pieces), top_value / len(pieces)))
        loudness = loudness * jnp.repeat(steps, shape[axis_at] // shards_of).reshape([-1 if axis == axis_at else 1 for axis in range(len(shape))])
    return loudness


def scatter_about(stream_key, shape, spread, reach, shards=(), kind=jnp.bfloat16):
    gain = steps_of(stream_key, shape, shards, -0.22, 0.18) if shards else 1.0
    result = jax.random.normal(stream_key, shape, jnp.float32) * spread * gain
    return jnp.minimum(jnp.maximum(result, -reach), reach).astype(kind)


def setup_inputs(seed: int = 0) -> dict:
    seeds = jax.random.split(jax.random.key(seed), 4)
    return {
        "snapshots": scatter_about(seeds[0], (ENS, LEV, NX, NY, SNAPS), 1.0, 6.0, ((0, 2), (2, 16), (3, 8))),
        "coefficients": scatter_about(seeds[1], (ENS, R, SNAPS), (ENS * SNAPS) ** -0.5, 0.125, ((0, 2),)),
        "modes": draw_modes(jax.random.fold_in(seeds[3], 71), 0),
    }


ETA = 0.25
LAM = 0.5
TAU = 0.4

def laplace(field):
    padded = jnp.pad(field, ((0, 0), (1, 1), (1, 1), (0, 0)))
    beside_all = padded[:, 2:, 1:-1] + padded[:, :-2, 1:-1] + padded[:, 1:-1, 2:] + padded[:, 1:-1, :-2]
    return 4.0 * field - beside_all

def reference(snapshots, coefficients, modes):
    cells = LEV * NX * NY
    flat_modes = modes.reshape(cells, R)
    gradient = jnp.zeros((cells, R), jnp.float32)
    for member in range(ENS):
        series = snapshots[member].reshape(cells, SNAPS)
        fitted = jnp.dot(flat_modes, coefficients[member], preferred_element_type=jnp.float32)
        misfit = (fitted - series.astype(jnp.float32)).astype(jnp.bfloat16)
        gradient = gradient + jnp.dot(misfit, coefficients[member].T, preferred_element_type=jnp.float32)
    bent = laplace(modes.astype(jnp.float32)).reshape(cells, R)
    moved = (flat_modes.astype(jnp.float32) - ETA * (gradient + LAM * bent)).astype(jnp.bfloat16)
    moved_f = moved.astype(jnp.float32)
    squares = lax.optimization_barrier(jnp.sum(moved_f * moved_f, axis=0))
    shrink = jnp.maximum(0.0, 1.0 - TAU / jnp.sqrt(squares / cells + 1e-06))
    new_modes = (moved_f * shrink[None, :]).astype(jnp.bfloat16).reshape(LEV, NX, NY, R)
    raw_gram = jnp.dot(moved.T, moved, preferred_element_type=jnp.float32)
    gram = shrink[:, None] * raw_gram * shrink[None, :] / cells
    projected = []
    for member in range(ENS):
        series = snapshots[member].reshape(cells, SNAPS)
        raw_proj = jnp.dot(moved.T, series, preferred_element_type=jnp.float32)
        projected.append(shrink[:, None] * raw_proj / math.sqrt(cells))
    return (new_modes, gram, jnp.stack(projected))
```

```python
import functools
import math

import jax
import jax.numpy as jnp
from jax import lax
from jax.experimental import pallas as pl
from jax.experimental.pallas import tpu as pltpu
from jax.sharding import Mesh, PartitionSpec as P

ETA = 0.25
LAM = 0.5
TAU = 0.4

F32 = jnp.float32
BF16 = jnp.bfloat16
VMEM_LIMIT = 48 * 1024 * 1024
PARAMS = pltpu.CompilerParams(vmem_limit_bytes=VMEM_LIMIT)

GROUP = ("xh", "y", "z")
SHARES = 64
PROJ_ROWS = 16
SHARE_ROWS = 24


def dot_t(a, b):
    return lax.dot_general(a, b, (((0,), (0,)), ((), ())), preferred_element_type=F32)


def grad_kernel(m_ref, c_ref, x_ref, g_ref):
    members = c_ref.shape[0]
    acc = None
    for e in range(members):
        fitted = jnp.dot(m_ref[...], c_ref[e], preferred_element_type=F32)
        misfit = (fitted - x_ref[e].astype(F32)).astype(BF16)
        term = lax.dot_general(misfit, c_ref[e], (((1,), (1,)), ((), ())), preferred_element_type=F32)
        acc = term if acc is None else acc + term
    g_ref[...] = acc.astype(BF16)


def grad_level(flat_modes, coefficients, series, level, cells):
    members, _, frames = series.shape
    width = flat_modes.shape[1]
    return pl.pallas_call(
        grad_kernel,
        grid=(1,),
        in_specs=[
            pl.BlockSpec((cells, width), lambda i: (level, 0)),
            pl.BlockSpec(coefficients.shape, lambda i: (0, 0, 0)),
            pl.BlockSpec((members, cells, frames), lambda i: (0, level, 0)),
        ],
        out_specs=pl.BlockSpec((cells, width), lambda i: (0, 0)),
        out_shape=jax.ShapeDtypeStruct((cells, width), BF16),
        compiler_params=PARAMS,
        cost_estimate=pl.CostEstimate(
            flops=4 * members * cells * frames * width,
            bytes_accessed=2 * cells * (2 * width + members * frames) + 2 * members * width * frames,
            transcendentals=0,
        ),
    )(flat_modes, coefficients, series)


def moved_of(level, m_ref, xlo_ref, xhi_ref, zlo_ref, zhi_ref, own_ref, got_ref):
    rows_x, rows_y, width = m_ref.shape
    f = m_ref[...].astype(F32)
    up = jnp.concatenate([xlo_ref[...].astype(F32), f[:-1]], axis=0)
    down = jnp.concatenate([f[1:], xhi_ref[...].astype(F32)], axis=0)
    at = lax.broadcasted_iota(jnp.int32, (rows_x, rows_y, width), 1)
    zlo = zlo_ref[level * rows_x : (level + 1) * rows_x, :].astype(F32)
    zhi = zhi_ref[level * rows_x : (level + 1) * rows_x, :].astype(F32)
    left = jnp.where(at == 0, jnp.broadcast_to(zlo[:, None, :], f.shape), pltpu.roll(f, 1, 1))
    right = jnp.where(
        at == rows_y - 1, jnp.broadcast_to(zhi[:, None, :], f.shape), pltpu.roll(f, rows_y - 1, 1)
    )
    bent = 4.0 * f - (down + up + right + left)
    cells = rows_x * rows_y
    grad = own_ref[...].astype(F32) + got_ref[...].astype(F32)
    return (f.reshape(cells, width) - ETA * (grad + LAM * bent.reshape(cells, width))).astype(BF16)


def emit_share(out_ref, half, proj_ref, gram_ref, squares_ref, tmp_ref):
    members, width, frames = proj_ref.shape
    per = width // PROJ_ROWS
    for tb in range(frames // 256):
        for m in range(members):
            at = pl.multiple_of((half * (frames // 256) + tb) * 128, 128)
            block = proj_ref[m, :, pl.ds(at, 128)]
            first = (tb * members + m) * per
            out_ref[first : first + per, 0:PROJ_ROWS, :] = block.reshape(per, PROJ_ROWS, 128).astype(BF16)
    gram = gram_ref[:, pl.ds(pl.multiple_of(half * 128, 128), 128)]
    for q in range(4):
        tmp_ref[:, q, :] = gram[q * SHARES : (q + 1) * SHARES, :]
    for k in range(2):
        part = squares_ref[0:1, k * 128 : (k + 1) * 128]
        high = part.astype(BF16).astype(F32)
        tmp_ref[:, 4 + k, :] = jnp.broadcast_to(high, (SHARES, 128))
        tmp_ref[:, 6 + k, :] = jnp.broadcast_to(part - high, (SHARES, 128))
    out_ref[:, PROJ_ROWS:SHARE_ROWS, :] = tmp_ref[...].astype(BF16)


def step_kernel(level, first, last, *refs):
    (core_ref, m_ref, xlo_ref, xhi_ref, zlo_ref, zhi_ref, own_ref, got_ref, x_ref), refs = refs[:9], refs[9:]
    if not first:
        (proj_in, gram_in, squares_in), refs = refs[:3], refs[3:]
    if last:
        moved_ref, keep_ref, send_ref, proj_ref, gram_ref, squares_ref, tmp_ref = refs
    else:
        moved_ref, proj_ref, gram_ref, squares_ref = refs
    moved = moved_of(level, m_ref, xlo_ref, xhi_ref, zlo_ref, zhi_ref, own_ref, got_ref)
    moved_ref[...] = moved
    members = x_ref.shape[0]
    wide = moved.astype(F32)
    squares = jnp.sum(wide * wide, axis=0, keepdims=True)
    gram = dot_t(moved, moved)
    squares_ref[...] = squares if first else squares_in[...] + squares
    gram_ref[...] = gram if first else gram_in[...] + gram
    for e in range(members):
        proj = dot_t(moved, x_ref[e])
        proj_ref[e] = proj if first else proj_in[e] + proj
    if last:
        core = core_ref[0]
        emit_share(keep_ref, core, proj_ref, gram_ref, squares_ref, tmp_ref)
        emit_share(send_ref, 1 - core, proj_ref, gram_ref, squares_ref, tmp_ref)


def step_level(level, levels, core, modes, halos, own, got, series, carry):
    members, total, frames = series.shape
    _, rows_x, rows_y, width = modes.shape
    cells = rows_x * rows_y
    first, last = level == 0, level == levels - 1
    xlo, xhi, zlo, zhi = halos
    whole = lambda a: pl.BlockSpec(a.shape, lambda i, c: (0,) * len(a.shape))
    in_specs = [
        pl.BlockSpec((None, rows_x, rows_y, width), lambda i, c: (level, 0, 0, 0)),
        pl.BlockSpec((None, 1, rows_y, width), lambda i, c: (level, 0, 0, 0)),
        pl.BlockSpec((None, 1, rows_y, width), lambda i, c: (level, 0, 0, 0)),
        whole(zlo),
        whole(zhi),
        whole(own),
        whole(got),
        pl.BlockSpec((members, cells, frames), lambda i, c: (0, level, 0)),
    ]
    args = [modes, xlo, xhi, zlo, zhi, own, got, series]
    if not first:
        in_specs += [whole(a) for a in carry]
        args += list(carry)
    sums = [
        jax.ShapeDtypeStruct((members, width, frames), F32),
        jax.ShapeDtypeStruct((width, width), F32),
        jax.ShapeDtypeStruct((1, width), F32),
    ]
    outs = [jax.ShapeDtypeStruct((cells, width), BF16)]
    scratch = []
    if last:
        share = jax.ShapeDtypeStruct((SHARES, SHARE_ROWS, 128), BF16)
        outs += [share, share]
        scratch = [pltpu.VMEM(s.shape, F32) for s in sums] + [pltpu.VMEM((SHARES, 8, 128), F32)]
    else:
        outs += sums
    return pl.pallas_call(
        functools.partial(step_kernel, level, first, last),
        grid_spec=pltpu.PrefetchScalarGridSpec(
            num_scalar_prefetch=1,
            grid=(1,),
            in_specs=in_specs,
            out_specs=[whole(o) for o in outs],
            scratch_shapes=scratch,
        ),
        out_shape=outs,
        compiler_params=PARAMS,
        cost_estimate=pl.CostEstimate(
            flops=2 * cells * width * (width + members * frames),
            bytes_accessed=2 * cells * (4 * width + members * frames),
            transcendentals=0,
        ),
    )(core, *args)


def join_kernel(keep_ref, got_ref, out_ref):
    out_ref[:, 0:PROJ_ROWS, :] = (
        keep_ref[:, 0:PROJ_ROWS, :].astype(F32) + got_ref[:, 0:PROJ_ROWS, :].astype(F32)
    ).astype(BF16)
    tail = keep_ref[:, PROJ_ROWS:SHARE_ROWS, :].astype(F32) + got_ref[:, PROJ_ROWS:SHARE_ROWS, :].astype(F32)
    row = lax.broadcasted_iota(jnp.int32, tail.shape, 1)
    total = tail + pltpu.roll(tail, 6, 1)
    high = total.astype(BF16).astype(F32)
    low = pltpu.roll(total - high, 2, 1)
    out_ref[:, PROJ_ROWS:SHARE_ROWS, :] = jnp.where(
        row < 4, tail, jnp.where(row < 6, high, low)
    ).astype(BF16)


def reduce_kernel(total_cells, at_ref, in_ref, out_ref, shrink_ref, column_ref):
    core, share = at_ref[0], at_ref[1]
    total = jnp.sum(in_ref[...].astype(F32), axis=0)
    squares = total[20:22, :] + total[22:24, :]
    shrink = jnp.maximum(0.0, 1.0 - TAU / jnp.sqrt(squares / total_cells + 1e-06))
    shrink_ref[...] = shrink
    for k in range(2):
        column_ref[k * 128 : (k + 1) * 128, :] = jnp.broadcast_to(shrink[k : k + 1, :], (128, 128)).T
    per = column_ref.shape[0] // PROJ_ROWS
    at = pl.multiple_of(lax.rem(share, per) * PROJ_ROWS, PROJ_ROWS)
    proj = column_ref[pl.ds(at, PROJ_ROWS), :] * total[0:PROJ_ROWS, :] / math.sqrt(total_cells)
    rows = jnp.concatenate([column_ref[pl.ds(share + q * SHARES, 1), :] for q in range(4)], axis=0)
    lanes = jnp.where(core == 0, shrink[0:1, :], shrink[1:2, :])
    gram = rows * total[16:20, :] * lanes / total_cells
    tail = jnp.concatenate([gram, jnp.zeros((4, 128), F32)], axis=0)
    mine = jnp.concatenate([proj, tail], axis=0).astype(BF16)
    out_ref[...] = jnp.broadcast_to(mine[None], out_ref.shape)


def scale_kernel(shrink_ref, *refs):
    out_ref = refs[-1]
    for level, m_ref in enumerate(refs[:-1]):
        for k in range(2):
            lanes = slice(k * 128, (k + 1) * 128)
            out_ref[level, :, lanes] = (m_ref[:, lanes].astype(F32) * shrink_ref[k : k + 1, :]).astype(BF16)


def final_kernel(core_ref, own_ref, got_ref, proj_ref, gram_ref, tmp_ref):
    core = core_ref[0]
    members, width, frames = proj_ref.shape
    per = width // PROJ_ROWS
    for ref, half in ((own_ref, core), (got_ref, 1 - core)):
        for tb in range(frames // 256):
            for m in range(members):
                at = pl.multiple_of((half * (frames // 256) + tb) * 128, 128)
                first = (tb * members + m) * per
                proj_ref[m, :, pl.ds(at, 128)] = (
                    ref[first : first + per, 0:PROJ_ROWS, :].astype(F32).reshape(width, 128)
                )
        tmp_ref[...] = ref[:, PROJ_ROWS:SHARE_ROWS, :].astype(F32)
        for q in range(4):
            gram_ref[q * SHARES : (q + 1) * SHARES, pl.ds(pl.multiple_of(half * 128, 128), 128)] = tmp_ref[:, q, :]


VM = pl.BlockSpec(memory_space=pltpu.VMEM)
SM = pl.BlockSpec(memory_space=pltpu.SMEM)


def local(snapshots, coefficients, modes):
    members, levels, rows_x, rows_y, frames = snapshots.shape
    width = modes.shape[3]
    cells = rows_x * rows_y
    local_cells = levels * cells
    sx_axes = ("xh", "y", "c")
    n_sx, n_z = lax.axis_size(sx_axes), lax.axis_size("z")
    total_cells = local_cells * n_sx * n_z
    core = lax.axis_index("c").astype(jnp.int32)
    share = lax.axis_index(GROUP).astype(jnp.int32)
    flat_modes = modes.reshape(local_cells, width)
    series = snapshots.reshape(members, local_cells, frames)

    swap = [(0, 1), (1, 0)]
    own, got = [], []
    for level in range(levels):
        g = grad_level(flat_modes, coefficients, series, level, cells)
        own.append(g)
        got.append(lax.ppermute(g, "ens", swap))

    def shifts(n):
        up = [(i, i + 1) for i in range(n - 1)]
        return up, [(j, i) for i, j in up]

    up, down = shifts(n_sx)
    xlo = lax.ppermute(modes[:, rows_x - 1 :], sx_axes, up)
    xhi = lax.ppermute(modes[:, :1], sx_axes, down)
    up, down = shifts(n_z)
    zlo = lax.ppermute(modes[:, :, rows_y - 1].reshape(levels * rows_x, width), "z", up)
    zhi = lax.ppermute(modes[:, :, 0].reshape(levels * rows_x, width), "z", down)
    halos = (xlo, xhi, zlo, zhi)

    moved, carry = [], None
    for level in range(levels):
        m, *carry = step_level(
            level, levels, core.reshape(1), modes, halos, own[level], got[level], series, carry
        )
        moved.append(m)
    keep, send = carry

    share_shape = jax.ShapeDtypeStruct((SHARES, SHARE_ROWS, 128), BF16)
    other = lax.ppermute(send, "c", swap)
    joined = pl.pallas_call(
        join_kernel, in_specs=[VM, VM], out_specs=VM, out_shape=share_shape, compiler_params=PARAMS
    )(keep, other)
    parts = lax.all_to_all(joined, GROUP, 0, 0)
    spread, shrink = pl.pallas_call(
        functools.partial(reduce_kernel, total_cells),
        in_specs=[SM, VM],
        out_specs=[VM, VM],
        out_shape=[share_shape, jax.ShapeDtypeStruct((2, 128), F32)],
        scratch_shapes=[pltpu.VMEM((width, 128), F32)],
        compiler_params=PARAMS,
    )(jnp.stack([core, share]), parts)
    half = lax.all_to_all(spread, GROUP, 0, 0)
    new_modes = pl.pallas_call(
        scale_kernel,
        in_specs=[VM] * (1 + levels),
        out_specs=VM,
        out_shape=jax.ShapeDtypeStruct((levels, cells, width), BF16),
        compiler_params=PARAMS,
    )(shrink, *moved).reshape(modes.shape)
    other_half = lax.ppermute(half, "c", swap)
    projected, gram = pl.pallas_call(
        final_kernel,
        in_specs=[SM, VM, VM],
        out_specs=[VM, VM],
        out_shape=[
            jax.ShapeDtypeStruct((members, width, frames), F32),
            jax.ShapeDtypeStruct((width, width), F32),
        ],
        scratch_shapes=[pltpu.VMEM((SHARES, 8, 128), F32)],
        compiler_params=PARAMS,
    )(core.reshape(1), half, other_half)
    return (new_modes, gram, projected)


def solution(mesh):
    ens, n_sx, n_sy = (mesh.shape[a] for a in ("ens", "sx", "sy"))
    fine = Mesh(mesh.devices.reshape(ens, 2, n_sx // 4, 2, n_sy), ("ens", "xh", "y", "c", "z"))
    sx = ("xh", "y", "c")
    in_specs = (P("ens", None, sx, "z", None), P("ens", None, None), P(None, sx, "z", None))
    out_specs = (P(None, sx, "z", None), P(), P("ens", None, None))
    return jax.shard_map(local, mesh=fine, in_specs=in_specs, out_specs=out_specs, check_vma=False)
```

```python
import functools
import math

import jax
import jax.numpy as jnp
from jax import lax
from jax.experimental import pallas as pl
from jax.experimental.pallas import tpu as pltpu
from jax.sharding import Mesh, PartitionSpec as P

ETA = 0.25
LAM = 0.5
TAU = 0.4

F32 = jnp.float32
BF16 = jnp.bfloat16
VMEM_LIMIT = 40 * 1024 * 1024
PARAMS = pltpu.CompilerParams(vmem_limit_bytes=VMEM_LIMIT)

SX = ("xh", "y", "c")
PLANE = ("xh", "y")
PARTS = 8
PROJ_ROWS = 128
GRAM_ROWS = 32
SUM_ROWS = PROJ_ROWS + GRAM_ROWS
PART_ROWS = SUM_ROWS + 8

VM = pl.BlockSpec(memory_space=pltpu.VMEM)
SM = pl.BlockSpec(memory_space=pltpu.SMEM)
HBM = pl.BlockSpec(memory_space=pltpu.HBM)


def gradient(m, coefficients, series):
    acc = None
    for e in range(len(coefficients)):
        c = coefficients[e]()
        fitted = jnp.dot(m, c, preferred_element_type=F32)
        misfit = (fitted - series[e]().astype(F32)).astype(BF16)
        term = lax.dot_general(misfit, c, (((1,), (1,)), ((), ())), preferred_element_type=F32)
        acc = term if acc is None else acc + term
    return acc.astype(BF16)


def first_grad_kernel(cells, m_hbm, c_hbm, x_hbm, g_ref, m_ref, c_ref, x_ref, sems):
    members = c_ref.shape[0]
    rows = pl.ds(0, cells)
    copies = [pltpu.make_async_copy(m_hbm.at[rows], m_ref, sems.at[0])]
    for e in range(members):
        copies.append(pltpu.make_async_copy(c_hbm.at[e], c_ref.at[e], sems.at[1 + 2 * e]))
        copies.append(pltpu.make_async_copy(x_hbm.at[e, rows], x_ref.at[e], sems.at[2 + 2 * e]))
    for copy in copies:
        copy.start()
    copies[0].wait()

    def ready(copy, ref, e):
        def load():
            copy.wait()
            return ref[e]

        return load

    g_ref[...] = gradient(
        m_ref[...],
        [ready(copies[1 + 2 * e], c_ref, e) for e in range(members)],
        [ready(copies[2 + 2 * e], x_ref, e) for e in range(members)],
    )


def grad_kernel(level, m_ref, c_ref, x_ref, g_ref):
    cells = g_ref.shape[0]
    members = c_ref.shape[0]
    rows = slice(level * cells, (level + 1) * cells)

    def part(ref, *at):
        return lambda: ref[at]

    g_ref[...] = gradient(
        m_ref[rows, :],
        [part(c_ref, e) for e in range(members)],
        [part(x_ref, e, rows) for e in range(members)],
    )


def grad_level(flat_modes, coefficients, series, level, cells):
    members, _, frames = series.shape
    width = flat_modes.shape[1]
    if level == 0:
        kernel, specs = functools.partial(first_grad_kernel, cells), [HBM, HBM, HBM]
        scratch = [
            pltpu.VMEM((cells, width), BF16),
            pltpu.VMEM(coefficients.shape, BF16),
            pltpu.VMEM((members, cells, frames), BF16),
            pltpu.SemaphoreType.DMA((1 + 2 * members,)),
        ]
    else:
        kernel, specs, scratch = functools.partial(grad_kernel, level), [VM, VM, VM], []
    return pl.pallas_call(
        kernel,
        in_specs=specs,
        out_specs=VM,
        out_shape=jax.ShapeDtypeStruct((cells, width), BF16),
        scratch_shapes=scratch,
        compiler_params=PARAMS,
        cost_estimate=pl.CostEstimate(
            flops=4 * members * cells * frames * width,
            bytes_accessed=2 * cells * (2 * width + members * frames) + 2 * members * width * frames,
            transcendentals=0,
        ),
    )(flat_modes, coefficients, series)


def moved_of(level, at_ref, m_ref, xa_ref, xb_ref, za_ref, zb_ref, own_ref, got_ref):
    _, rows_x, rows_y, width = m_ref.shape
    f = m_ref[level].astype(F32)
    lower = at_ref[0] == 0
    even = at_ref[1] == 0
    xa, xb = xa_ref[level].astype(F32), xb_ref[level].astype(F32)
    rows = slice(level * rows_x, (level + 1) * rows_x)
    za, zb = za_ref[rows, :].astype(F32), zb_ref[rows, :].astype(F32)
    up = jnp.concatenate([jnp.where(lower, xb, xa), f[:-1]], axis=0)
    down = jnp.concatenate([f[1:], jnp.where(lower, xa, xb)], axis=0)
    at = lax.broadcasted_iota(jnp.int32, (rows_x, rows_y, width), 1)
    zlo = jnp.broadcast_to(jnp.where(even, zb, za)[:, None, :], f.shape)
    zhi = jnp.broadcast_to(jnp.where(even, za, zb)[:, None, :], f.shape)
    left = jnp.where(at == 0, zlo, pltpu.roll(f, 1, 1))
    right = jnp.where(at == rows_y - 1, zhi, pltpu.roll(f, rows_y - 1, 1))
    bent = 4.0 * f - (down + up + right + left)
    cells = rows_x * rows_y
    grad = own_ref[...].astype(F32) + got_ref[...].astype(F32)
    return (f.reshape(cells, width) - ETA * (grad + LAM * bent.reshape(cells, width))).astype(BF16)


def split_squares(squares, rows):
    high = squares.astype(BF16).astype(F32)
    return jnp.concatenate([high, squares - high, jnp.zeros((rows - 4, 128), F32)], axis=0)


def emit(out_ref, half, proj_ref, gram_ref, squares):
    members = proj_ref.shape[0]
    for j in range(PARTS):
        tb, m, r = j // 4, (j // 2) % members, j % 2
        at = pl.multiple_of((half * 2 + tb) * 128, 128)
        block = proj_ref[m, r * 128 : (r + 1) * 128, pl.ds(at, 128)]
        out_ref[j, 0:PROJ_ROWS, :] = block.astype(BF16)
        at = pl.multiple_of(half * 128, 128)
        block = gram_ref[j * GRAM_ROWS : (j + 1) * GRAM_ROWS, pl.ds(at, 128)]
        out_ref[j, PROJ_ROWS:SUM_ROWS, :] = block.astype(BF16)
        out_ref[j, SUM_ROWS:PART_ROWS, :] = squares


def step_kernel(level, first, last, *refs):
    inputs, refs = refs[:8], refs[8:]
    x_ref, refs = refs[0], refs[1:]
    if not first:
        (proj_in, gram_in, squares_in), refs = refs[:3], refs[3:]
    if last:
        moved_ref, keep_ref, send_ref, proj_ref, gram_ref = refs
    else:
        moved_ref, proj_ref, gram_ref, squares_ref = refs
    moved = moved_of(level, *inputs)
    moved_ref[...] = moved
    cells = moved.shape[0]
    rows = slice(level * cells, (level + 1) * cells)
    wide = moved.astype(F32)
    squares = jnp.sum(wide * wide, axis=0, keepdims=True)
    if not first:
        squares = squares + squares_in[...]
    turned = moved.T
    gram = jnp.dot(turned, moved, preferred_element_type=F32)
    gram_ref[...] = gram if first else gram_in[...] + gram
    for e in range(x_ref.shape[0]):
        proj = jnp.dot(turned, x_ref[e, rows, :], preferred_element_type=F32)
        proj_ref[e] = proj if first else proj_in[e] + proj
    if last:
        core = inputs[0][0]
        pair = jnp.concatenate([squares[:, 0:128], squares[:, 128:256]], axis=0)
        packed = split_squares(pair, 8).astype(BF16)
        emit(send_ref, 1 - core, proj_ref, gram_ref, packed)
        emit(keep_ref, core, proj_ref, gram_ref, packed)
    else:
        squares_ref[...] = squares


def step_level(level, levels, place, modes, halos, own, got, series, carry):
    members, _, frames = series.shape
    _, rows_x, rows_y, width = modes.shape
    cells = rows_x * rows_y
    first, last = level == 0, level == levels - 1
    args = [place, modes, *halos, own, got, series]
    if not first:
        args += list(carry)
    sums = [
        jax.ShapeDtypeStruct((members, width, frames), F32),
        jax.ShapeDtypeStruct((width, width), F32),
        jax.ShapeDtypeStruct((1, width), F32),
    ]
    outs = [jax.ShapeDtypeStruct((cells, width), BF16)]
    scratch, aliases = [], {}
    if last:
        outs += [jax.ShapeDtypeStruct((PARTS, PART_ROWS, 128), BF16)] * 2
        scratch = [pltpu.VMEM(s.shape, F32) for s in sums[:2]]
    else:
        outs += sums
        if not first:
            aliases = {9 + i: 1 + i for i in range(3)}
    return pl.pallas_call(
        functools.partial(step_kernel, level, first, last),
        in_specs=[SM] + [VM] * (len(args) - 1),
        out_specs=[VM] * len(outs),
        out_shape=outs,
        scratch_shapes=scratch,
        input_output_aliases=aliases,
        compiler_params=PARAMS,
        cost_estimate=pl.CostEstimate(
            flops=2 * cells * width * (width + members * frames),
            bytes_accessed=2 * cells * (4 * width + members * frames),
            transcendentals=0,
        ),
    )(*args)


def whole_squares(part):
    return part[SUM_ROWS : SUM_ROWS + 2, :] + part[SUM_ROWS + 2 : SUM_ROWS + 4, :]


def join_kernel(keep_ref, got_ref, out_ref):
    out_ref[:, 0:SUM_ROWS, :] = (
        keep_ref[:, 0:SUM_ROWS, :].astype(F32) + got_ref[:, 0:SUM_ROWS, :].astype(F32)
    ).astype(BF16)
    tail = keep_ref[0, SUM_ROWS:PART_ROWS, :].astype(F32) + got_ref[0, SUM_ROWS:PART_ROWS, :].astype(F32)
    packed = split_squares(tail[0:2, :] + tail[2:4, :], 8).astype(BF16)
    for j in range(PARTS):
        out_ref[j, SUM_ROWS:PART_ROWS, :] = packed


def gather_sum(in_ref):
    total = in_ref[0].astype(F32)
    for j in range(1, PARTS):
        total = total + in_ref[j].astype(F32)
    return total


def plane_kernel(in_ref, out_ref):
    total = gather_sum(in_ref)
    packed = split_squares(whole_squares(total), 8)
    mine = jnp.concatenate([total[0:SUM_ROWS, :], packed], axis=0).astype(BF16)
    for j in range(PARTS):
        out_ref[j] = mine


def reduce_kernel(total_cells, at_ref, in_ref, out_ref, shrink_ref, column_ref):
    core, part = at_ref[0], at_ref[2]
    total = gather_sum(in_ref)
    squares = whole_squares(total)
    shrink = jnp.maximum(0.0, 1.0 - TAU / jnp.sqrt(squares / total_cells + 1e-06))
    shrink_ref[...] = shrink
    for k in range(2):
        column_ref[k * 128 : (k + 1) * 128, :] = jnp.broadcast_to(shrink[k : k + 1, :], (128, 128)).T
    at = pl.multiple_of(lax.rem(part, 2) * 128, 128)
    proj = column_ref[pl.ds(at, 128), :] * total[0:PROJ_ROWS, :] * (1.0 / math.sqrt(total_cells))
    at = pl.multiple_of(part * GRAM_ROWS, GRAM_ROWS)
    lanes = jnp.where(core == 0, shrink[0:1, :], shrink[1:2, :])
    gram = column_ref[pl.ds(at, GRAM_ROWS), :] * total[PROJ_ROWS:SUM_ROWS, :] * lanes * (1.0 / total_cells)
    mine = jnp.concatenate([proj, gram], axis=0).astype(BF16)
    for j in range(PARTS):
        out_ref[j] = mine


def scale_kernel(shrink_ref, *refs):
    out_ref = refs[-1]
    for level, m_ref in enumerate(refs[:-1]):
        for k in range(2):
            lanes = slice(k * 128, (k + 1) * 128)
            out_ref[level, :, lanes] = (m_ref[:, lanes].astype(F32) * shrink_ref[k : k + 1, :]).astype(BF16)


def final_kernel(at_ref, own_ref, got_ref, proj_ref, gram_ref):
    core = at_ref[0]
    members = proj_ref.shape[0]
    for ref, half in ((own_ref, core), (got_ref, 1 - core)):
        for j in range(PARTS):
            tb, m, r = j // 4, (j // 2) % members, j % 2
            at = pl.multiple_of((half * 2 + tb) * 128, 128)
            proj_ref[m, r * 128 : (r + 1) * 128, pl.ds(at, 128)] = ref[j, 0:PROJ_ROWS, :].astype(F32)
            at = pl.multiple_of(half * 128, 128)
            gram_ref[j * GRAM_ROWS : (j + 1) * GRAM_ROWS, pl.ds(at, 128)] = (
                ref[j, PROJ_ROWS:SUM_ROWS, :].astype(F32)
            )


def both_ways(pairs):
    return [p for i, j in pairs for p in ((i, j), (j, i))]


def local(snapshots, coefficients, modes):
    members, levels, rows_x, rows_y, frames = snapshots.shape
    width = modes.shape[3]
    cells = rows_x * rows_y
    local_cells = levels * cells
    n_sx, n_z = lax.axis_size(SX), lax.axis_size("z")
    total_cells = local_cells * n_sx * n_z
    core = lax.axis_index("c").astype(jnp.int32)
    parity = lax.axis_index("z").astype(jnp.int32) % 2
    part = lax.axis_index(PLANE).astype(jnp.int32)
    place = jnp.stack([core, parity, part])
    flat_modes = modes.reshape(local_cells, width)
    series = snapshots.reshape(members, local_cells, frames)
    swap = [(0, 1), (1, 0)]

    own, got = [], []
    for level in range(levels):
        own.append(grad_level(flat_modes, coefficients, series, level, cells))
        got.append(lax.ppermute(own[level], "ens", swap))

    edge_modes, _ = lax.optimization_barrier((modes, own[1]))
    upper = (rows_x - 1) * (1 - core)
    edge_a = lax.dynamic_slice_in_dim(edge_modes, upper, 1, axis=1)
    edge_b = lax.dynamic_slice_in_dim(edge_modes, rows_x - 1 - upper, 1, axis=1)
    row_lo = edge_modes[:, :, 0].reshape(levels * rows_x, width)
    row_hi = edge_modes[:, :, rows_y - 1].reshape(levels * rows_x, width)
    xb = lax.ppermute(edge_b[:, 0], SX, both_ways([(i, i + 1) for i in range(1, n_sx - 1, 2)]))
    za = lax.ppermute(
        jnp.where(parity == 0, row_hi, row_lo), "z", both_ways([(i, i + 1) for i in range(0, n_z, 2)])
    )
    zb = lax.ppermute(
        jnp.where(parity == 0, row_lo, row_hi), "z", both_ways([(i, i + 1) for i in range(1, n_z - 1, 2)])
    )
    xa = lax.ppermute(edge_a[:, 0], "c", swap)
    halos = (xa[:, None], xb[:, None], za, zb)

    moved, carry = [], None
    for level in range(levels):
        m, *carry = step_level(
            level, levels, place, modes, halos, own[level], got[level], series, carry
        )
        moved.append(m)
    keep, send = carry

    part_shape = jax.ShapeDtypeStruct((PARTS, PART_ROWS, 128), BF16)
    other = lax.ppermute(send, "c", swap)
    joined = pl.pallas_call(
        join_kernel, in_specs=[VM, VM], out_specs=VM, out_shape=part_shape, compiler_params=PARAMS
    )(keep, other)
    parts = lax.all_to_all(joined, PLANE, 0, 0)
    planes = pl.pallas_call(
        plane_kernel, in_specs=[VM], out_specs=VM, out_shape=part_shape, compiler_params=PARAMS
    )(parts)
    planes = lax.all_to_all(planes, "z", 0, 0)
    spread, shrink = pl.pallas_call(
        functools.partial(reduce_kernel, total_cells),
        in_specs=[SM, VM],
        out_specs=[VM, VM],
        out_shape=[
            jax.ShapeDtypeStruct((PARTS, SUM_ROWS, 128), BF16),
            jax.ShapeDtypeStruct((2, 128), F32),
        ],
        scratch_shapes=[pltpu.VMEM((width, 128), F32)],
        compiler_params=PARAMS,
    )(place, planes)
    half = lax.all_to_all(spread, PLANE, 0, 0)
    new_modes = pl.pallas_call(
        scale_kernel,
        in_specs=[VM] * (1 + levels),
        out_specs=VM,
        out_shape=jax.ShapeDtypeStruct((levels, cells, width), BF16),
        compiler_params=PARAMS,
    )(shrink, *moved)
    half, new_modes = lax.optimization_barrier((half, new_modes))
    other_half = lax.ppermute(half, "c", swap)
    projected, gram = pl.pallas_call(
        final_kernel,
        in_specs=[SM, VM, VM],
        out_specs=[VM, VM],
        out_shape=[
            jax.ShapeDtypeStruct((members, width, frames), F32),
            jax.ShapeDtypeStruct((width, width), F32),
        ],
        compiler_params=PARAMS,
    )(place, half, other_half)
    return (new_modes.reshape(modes.shape), gram, projected)


def solution(mesh):
    ens, n_sx, n_sy = (mesh.shape[a] for a in ("ens", "sx", "sy"))
    fine = Mesh(mesh.devices.reshape(ens, 2, n_sx // 4, 2, n_sy), ("ens", "xh", "y", "c", "z"))
    in_specs = (P("ens", None, SX, "z", None), P("ens", None, None), P(None, SX, "z", None))
    out_specs = (P(None, SX, "z", None), P(), P("ens", None, None))
    return jax.shard_map(local, mesh=fine, in_specs=in_specs, out_specs=out_specs, check_vma=False)
```

```python
import functools
import math

import jax
import jax.numpy as jnp
from jax import lax
from jax.experimental import pallas as pl
from jax.experimental.pallas import tpu as pltpu
from jax.sharding import Mesh, PartitionSpec as P

ETA = 0.25
LAM = 0.5
TAU = 0.4

F32 = jnp.float32
BF16 = jnp.bfloat16
VMEM_LIMIT = 40 * 1024 * 1024
PARAMS = pltpu.CompilerParams(vmem_limit_bytes=VMEM_LIMIT)

SX = ("xh", "y", "c")
PLANE = ("xh", "y")
PARTS = 8
PROJ_ROWS = 128
GRAM_ROWS = 32
SUM_ROWS = PROJ_ROWS + GRAM_ROWS
PART_ROWS = SUM_ROWS + 8

VM = pl.BlockSpec(memory_space=pltpu.VMEM)
SM = pl.BlockSpec(memory_space=pltpu.SMEM)
HBM = pl.BlockSpec(memory_space=pltpu.HBM)


def in_hbm(array):
    return pltpu.with_memory_space_constraint(array, pltpu.HBM)


def gradient(m, coefficients, series):
    acc = None
    for e in range(len(coefficients)):
        c = coefficients[e]()
        fitted = jnp.dot(m, c, preferred_element_type=F32)
        misfit = (fitted - series[e]().astype(F32)).astype(BF16)
        term = lax.dot_general(misfit, c, (((1,), (1,)), ((), ())), preferred_element_type=F32)
        acc = term if acc is None else acc + term
    return acc.astype(BF16)


def grad_kernel(level, m_hbm, c_hbm, x_hbm, g_ref, m_ref, c_ref, x_ref, sems):
    members = c_ref.shape[0]
    cells = m_ref.shape[0]
    rows = pl.ds(level * cells, cells)
    copies = [pltpu.make_async_copy(m_hbm.at[rows], m_ref, sems.at[0])]
    for e in range(members):
        copies.append(pltpu.make_async_copy(c_hbm.at[e], c_ref.at[e], sems.at[1 + 2 * e]))
        copies.append(pltpu.make_async_copy(x_hbm.at[e, rows], x_ref.at[e], sems.at[2 + 2 * e]))
    for copy in copies:
        copy.start()
    copies[0].wait()

    def ready(copy, ref, e):
        def load():
            copy.wait()
            return ref[e]

        return load

    g_ref[...] = gradient(
        m_ref[...],
        [ready(copies[1 + 2 * e], c_ref, e) for e in range(members)],
        [ready(copies[2 + 2 * e], x_ref, e) for e in range(members)],
    )


def grad_level(flat_modes, coefficients, series, level, cells):
    members, _, frames = series.shape
    width = flat_modes.shape[1]
    return pl.pallas_call(
        functools.partial(grad_kernel, level),
        in_specs=[HBM, HBM, HBM],
        out_specs=VM,
        out_shape=jax.ShapeDtypeStruct((cells, width), BF16),
        scratch_shapes=[
            pltpu.VMEM((cells, width), BF16),
            pltpu.VMEM(coefficients.shape, BF16),
            pltpu.VMEM((members, cells, frames), BF16),
            pltpu.SemaphoreType.DMA((1 + 2 * members,)),
        ],
        compiler_params=PARAMS,
        cost_estimate=pl.CostEstimate(
            flops=4 * members * cells * frames * width,
            bytes_accessed=2 * cells * (2 * width + members * frames) + 2 * members * width * frames,
            transcendentals=0,
        ),
    )(in_hbm(flat_modes), in_hbm(coefficients), in_hbm(series))


def moved_of(level, at_ref, m_ref, xa_ref, xb_ref, za_ref, zb_ref, own_ref, got_ref):
    rows_x, rows_y, width = m_ref.shape
    f = m_ref[...].astype(F32)
    lower = at_ref[0] == 0
    even = at_ref[1] == 0
    xa, xb = xa_ref[level].astype(F32), xb_ref[level].astype(F32)
    rows = slice(level * rows_x, (level + 1) * rows_x)
    za, zb = za_ref[rows, :].astype(F32), zb_ref[rows, :].astype(F32)
    up = jnp.concatenate([jnp.where(lower, xb, xa), f[:-1]], axis=0)
    down = jnp.concatenate([f[1:], jnp.where(lower, xa, xb)], axis=0)
    at = lax.broadcasted_iota(jnp.int32, (rows_x, rows_y, width), 1)
    zlo = jnp.broadcast_to(jnp.where(even, zb, za)[:, None, :], f.shape)
    zhi = jnp.broadcast_to(jnp.where(even, za, zb)[:, None, :], f.shape)
    left = jnp.where(at == 0, zlo, pltpu.roll(f, 1, 1))
    right = jnp.where(at == rows_y - 1, zhi, pltpu.roll(f, rows_y - 1, 1))
    bent = 4.0 * f - (down + up + right + left)
    cells = rows_x * rows_y
    grad = own_ref[...].astype(F32) + got_ref[...].astype(F32)
    return (f.reshape(cells, width) - ETA * (grad + LAM * bent.reshape(cells, width))).astype(BF16)


def split_squares(squares, rows):
    high = squares.astype(BF16).astype(F32)
    return jnp.concatenate([high, squares - high, jnp.zeros((rows - 4, 128), F32)], axis=0)


def emit(out_ref, half, proj_ref, gram_ref, squares):
    members = proj_ref.shape[0]
    for j in range(PARTS):
        tb, m, r = j // 4, (j // 2) % members, j % 2
        at = pl.multiple_of((half * 2 + tb) * 128, 128)
        block = proj_ref[m, r * 128 : (r + 1) * 128, pl.ds(at, 128)]
        out_ref[j, 0:PROJ_ROWS, :] = block.astype(BF16)
        at = pl.multiple_of(half * 128, 128)
        block = gram_ref[j * GRAM_ROWS : (j + 1) * GRAM_ROWS, pl.ds(at, 128)]
        out_ref[j, PROJ_ROWS:SUM_ROWS, :] = block.astype(BF16)
        out_ref[j, SUM_ROWS:PART_ROWS, :] = squares


def step_kernel(level, first, last, *refs):
    (at_ref, m_hbm, *inputs), refs = refs[:8], refs[8:]
    x_hbm, refs = refs[0], refs[1:]
    *refs, m_ref, x_ref, sems = refs
    cells = x_ref.shape[1]
    copies = [pltpu.make_async_copy(m_hbm.at[level], m_ref, sems.at[0])]
    for e in range(x_ref.shape[0]):
        source = x_hbm.at[e, pl.ds(level * cells, cells)]
        copies.append(pltpu.make_async_copy(source, x_ref.at[e], sems.at[1 + e]))
    for copy in copies:
        copy.start()
    if not first:
        (proj_in, gram_in, squares_in), refs = refs[:3], refs[3:]
    if last:
        moved_ref, keep_ref, send_ref, proj_ref, gram_ref = refs
    else:
        moved_ref, proj_ref, gram_ref, squares_ref = refs
    copies[0].wait()
    moved = moved_of(level, at_ref, m_ref, *inputs)
    moved_ref[...] = moved
    wide = moved.astype(F32)
    squares = jnp.sum(wide * wide, axis=0, keepdims=True)
    if not first:
        squares = squares + squares_in[...]
    turned = moved.T
    gram = jnp.dot(turned, moved, preferred_element_type=F32)
    gram_ref[...] = gram if first else gram_in[...] + gram
    for e in range(x_ref.shape[0]):
        copies[1 + e].wait()
        proj = jnp.dot(turned, x_ref[e], preferred_element_type=F32)
        proj_ref[e] = proj if first else proj_in[e] + proj
    if last:
        core = at_ref[0]
        pair = jnp.concatenate([squares[:, 0:128], squares[:, 128:256]], axis=0)
        packed = split_squares(pair, 8).astype(BF16)
        emit(send_ref, 1 - core, proj_ref, gram_ref, packed)
        emit(keep_ref, core, proj_ref, gram_ref, packed)
    else:
        squares_ref[...] = squares


def step_level(level, levels, place, modes, halos, own, got, series, carry):
    members, _, frames = series.shape
    _, rows_x, rows_y, width = modes.shape
    cells = rows_x * rows_y
    first, last = level == 0, level == levels - 1
    args = [place, in_hbm(modes), *halos, own, got, in_hbm(series)]
    if not first:
        args += list(carry)
    sums = [
        jax.ShapeDtypeStruct((members, width, frames), F32),
        jax.ShapeDtypeStruct((width, width), F32),
        jax.ShapeDtypeStruct((1, width), F32),
    ]
    outs = [jax.ShapeDtypeStruct((cells, width), BF16)]
    scratch, aliases = [], {}
    if last:
        outs += [jax.ShapeDtypeStruct((PARTS, PART_ROWS, 128), BF16)] * 2
        scratch = [pltpu.VMEM(s.shape, F32) for s in sums[:2]]
    else:
        outs += sums
        if not first:
            aliases = {9 + i: 1 + i for i in range(3)}
    return pl.pallas_call(
        functools.partial(step_kernel, level, first, last),
        in_specs=[SM, HBM] + [VM] * 6 + [HBM] + [VM] * (len(args) - 9),
        out_specs=[VM] * len(outs),
        out_shape=outs,
        scratch_shapes=scratch
        + [
            pltpu.VMEM((rows_x, rows_y, width), BF16),
            pltpu.VMEM((members, cells, frames), BF16),
            pltpu.SemaphoreType.DMA((1 + members,)),
        ],
        input_output_aliases=aliases,
        compiler_params=PARAMS,
        cost_estimate=pl.CostEstimate(
            flops=2 * cells * width * (width + members * frames),
            bytes_accessed=2 * cells * (4 * width + members * frames),
            transcendentals=0,
        ),
    )(*args)


def whole_squares(part):
    return part[SUM_ROWS : SUM_ROWS + 2, :] + part[SUM_ROWS + 2 : SUM_ROWS + 4, :]


def join_kernel(keep_ref, got_ref, out_ref):
    out_ref[:, 0:SUM_ROWS, :] = (
        keep_ref[:, 0:SUM_ROWS, :].astype(F32) + got_ref[:, 0:SUM_ROWS, :].astype(F32)
    ).astype(BF16)
    tail = keep_ref[0, SUM_ROWS:PART_ROWS, :].astype(F32) + got_ref[0, SUM_ROWS:PART_ROWS, :].astype(F32)
    packed = split_squares(tail[0:2, :] + tail[2:4, :], 8).astype(BF16)
    for j in range(PARTS):
        out_ref[j, SUM_ROWS:PART_ROWS, :] = packed


def gather_sum(in_ref):
    total = in_ref[0].astype(F32)
    for j in range(1, PARTS):
        total = total + in_ref[j].astype(F32)
    return total


def plane_kernel(in_ref, out_ref):
    total = gather_sum(in_ref)
    packed = split_squares(whole_squares(total), 8)
    mine = jnp.concatenate([total[0:SUM_ROWS, :], packed], axis=0).astype(BF16)
    for j in range(PARTS):
        out_ref[j] = mine


def reduce_kernel(total_cells, at_ref, in_ref, out_ref, shrink_ref, column_ref):
    core, part = at_ref[0], at_ref[2]
    total = gather_sum(in_ref)
    squares = whole_squares(total)
    shrink = jnp.maximum(0.0, 1.0 - TAU / jnp.sqrt(squares / total_cells + 1e-06))
    shrink_ref[...] = shrink
    for k in range(2):
        column_ref[k * 128 : (k + 1) * 128, :] = jnp.broadcast_to(shrink[k : k + 1, :], (128, 128)).T
    at = pl.multiple_of(lax.rem(part, 2) * 128, 128)
    proj = column_ref[pl.ds(at, 128), :] * total[0:PROJ_ROWS, :] * (1.0 / math.sqrt(total_cells))
    at = pl.multiple_of(part * GRAM_ROWS, GRAM_ROWS)
    lanes = jnp.where(core == 0, shrink[0:1, :], shrink[1:2, :])
    gram = column_ref[pl.ds(at, GRAM_ROWS), :] * total[PROJ_ROWS:SUM_ROWS, :] * lanes * (1.0 / total_cells)
    mine = jnp.concatenate([proj, gram], axis=0).astype(BF16)
    for j in range(PARTS):
        out_ref[j] = mine


def scale_kernel(shrink_ref, *refs):
    out_ref = refs[-1]
    for level, m_ref in enumerate(refs[:-1]):
        for k in range(2):
            lanes = slice(k * 128, (k + 1) * 128)
            out_ref[level, :, lanes] = (m_ref[:, lanes].astype(F32) * shrink_ref[k : k + 1, :]).astype(BF16)


def final_kernel(at_ref, own_ref, got_ref, proj_ref, gram_ref):
    core = at_ref[0]
    members = proj_ref.shape[0]
    for ref, half in ((own_ref, core), (got_ref, 1 - core)):
        for j in range(PARTS):
            tb, m, r = j // 4, (j // 2) % members, j % 2
            at = pl.multiple_of((half * 2 + tb) * 128, 128)
            proj_ref[m, r * 128 : (r + 1) * 128, pl.ds(at, 128)] = ref[j, 0:PROJ_ROWS, :].astype(F32)
            at = pl.multiple_of(half * 128, 128)
            gram_ref[j * GRAM_ROWS : (j + 1) * GRAM_ROWS, pl.ds(at, 128)] = (
                ref[j, PROJ_ROWS:SUM_ROWS, :].astype(F32)
            )


def both_ways(pairs):
    return [p for i, j in pairs for p in ((i, j), (j, i))]


def local(snapshots, coefficients, modes):
    members, levels, rows_x, rows_y, frames = snapshots.shape
    width = modes.shape[3]
    cells = rows_x * rows_y
    local_cells = levels * cells
    n_sx, n_z = lax.axis_size(SX), lax.axis_size("z")
    total_cells = local_cells * n_sx * n_z
    core = lax.axis_index("c").astype(jnp.int32)
    parity = lax.axis_index("z").astype(jnp.int32) % 2
    part = lax.axis_index(PLANE).astype(jnp.int32)
    place = jnp.stack([core, parity, part])
    flat_modes = modes.reshape(local_cells, width)
    series = snapshots.reshape(members, local_cells, frames)
    swap = [(0, 1), (1, 0)]

    own, got = [], []

    def send_level(level, *after):
        c, *_ = lax.optimization_barrier((coefficients, *after))
        own.append(grad_level(flat_modes, c, series, level, cells))
        got.append(lax.ppermute(own[level], "ens", swap))

    send_level(0)
    edge_modes, _ = lax.optimization_barrier((modes, own[0]))
    upper = (rows_x - 1) * (1 - core)
    edge_a = lax.dynamic_slice_in_dim(edge_modes, upper, 1, axis=1)[:, 0]
    edge_b = lax.dynamic_slice_in_dim(edge_modes, rows_x - 1 - upper, 1, axis=1)[:, 0]
    xb = lax.ppermute(edge_b, SX, both_ways([(i, i + 1) for i in range(1, n_sx - 1, 2)]))
    send_level(1, own[0], edge_a, edge_b)
    edge_modes, _ = lax.optimization_barrier((modes, own[1]))
    row_lo = edge_modes[:, :, 0].reshape(levels * rows_x, width)
    row_hi = edge_modes[:, :, rows_y - 1].reshape(levels * rows_x, width)
    row_a, row_b = jnp.where(parity == 0, row_hi, row_lo), jnp.where(parity == 0, row_lo, row_hi)
    za = lax.ppermute(row_a, "z", both_ways([(i, i + 1) for i in range(0, n_z, 2)]))
    zb = lax.ppermute(row_b, "z", both_ways([(i, i + 1) for i in range(1, n_z - 1, 2)]))
    xa = lax.ppermute(edge_a, "c", swap)
    send_level(2, own[1], row_a, row_b)
    for level in range(3, levels):
        send_level(level, own[level - 1])
    halos = (xa[:, None], xb[:, None], za, zb)

    moved, carry = [], None
    for level in range(levels):
        m, *carry = step_level(
            level, levels, place, modes, halos, own[level], got[level], series, carry
        )
        moved.append(m)
    keep, send = carry

    part_shape = jax.ShapeDtypeStruct((PARTS, PART_ROWS, 128), BF16)
    other = lax.ppermute(send, "c", swap)
    joined = pl.pallas_call(
        join_kernel, in_specs=[VM, VM], out_specs=VM, out_shape=part_shape, compiler_params=PARAMS
    )(keep, other)
    parts = lax.all_to_all(joined, PLANE, 0, 0)
    planes = pl.pallas_call(
        plane_kernel, in_specs=[VM], out_specs=VM, out_shape=part_shape, compiler_params=PARAMS
    )(parts)
    planes = lax.all_to_all(planes, "z", 0, 0)
    spread, shrink = pl.pallas_call(
        functools.partial(reduce_kernel, total_cells),
        in_specs=[SM, VM],
        out_specs=[VM, VM],
        out_shape=[
            jax.ShapeDtypeStruct((PARTS, SUM_ROWS, 128), BF16),
            jax.ShapeDtypeStruct((2, 128), F32),
        ],
        scratch_shapes=[pltpu.VMEM((width, 128), F32)],
        compiler_params=PARAMS,
    )(place, planes)
    half = lax.all_to_all(spread, PLANE, 0, 0)
    new_modes = pl.pallas_call(
        scale_kernel,
        in_specs=[VM] * (1 + levels),
        out_specs=VM,
        out_shape=jax.ShapeDtypeStruct((levels, cells, width), BF16),
        compiler_params=PARAMS,
    )(shrink, *moved)
    half, new_modes = lax.optimization_barrier((half, new_modes))
    other_half = lax.ppermute(half, "c", swap)
    projected, gram = pl.pallas_call(
        final_kernel,
        in_specs=[SM, VM, VM],
        out_specs=[VM, VM],
        out_shape=[
            jax.ShapeDtypeStruct((members, width, frames), F32),
            jax.ShapeDtypeStruct((width, width), F32),
        ],
        compiler_params=PARAMS,
    )(place, half, other_half)
    return (new_modes.reshape(modes.shape), gram, projected)


def solution(mesh):
    ens, n_sx, n_sy = (mesh.shape[a] for a in ("ens", "sx", "sy"))
    fine = Mesh(mesh.devices.reshape(ens, 2, n_sx // 4, 2, n_sy), ("ens", "xh", "y", "c", "z"))
    in_specs = (P("ens", None, SX, "z", None), P("ens", None, None), P(None, SX, "z", None))
    out_specs = (P(None, SX, "z", None), P(), P("ens", None, None))
    return jax.shard_map(local, mesh=fine, in_specs=in_specs, out_specs=out_specs, check_vma=False)
```

```python
import functools
import math

import jax
import jax.numpy as jnp
from jax import lax
from jax.experimental import pallas as pl
from jax.experimental.pallas import tpu as pltpu
from jax.sharding import Mesh, PartitionSpec as P

ETA = 0.25
LAM = 0.5
TAU = 0.4

F32 = jnp.float32
BF16 = jnp.bfloat16
VMEM_LIMIT = 40 * 1024 * 1024
PARAMS = pltpu.CompilerParams(vmem_limit_bytes=VMEM_LIMIT)

SX = ("xh", "y", "c")
PLANE = ("xh", "y")
PARTS = 8
PROJ_ROWS = 128
GRAM_ROWS = 32
SUM_ROWS = PROJ_ROWS + GRAM_ROWS
PART_ROWS = SUM_ROWS + 8

VM = pl.BlockSpec(memory_space=pltpu.VMEM)
SM = pl.BlockSpec(memory_space=pltpu.SMEM)
HBM = pl.BlockSpec(memory_space=pltpu.HBM)


def core_of(place):
    return place & 1


def parity_of(place):
    return (place >> 1) & 1


def part_of(place):
    return place >> 2


def gradient(m, coefficients, series):
    acc = None
    for e in range(len(coefficients)):
        c = coefficients[e]()
        fitted = jnp.dot(m, c, preferred_element_type=F32)
        misfit = (fitted - series[e]().astype(F32)).astype(BF16)
        term = lax.dot_general(misfit, c, (((1,), (1,)), ((), ())), preferred_element_type=F32)
        acc = term if acc is None else acc + term
    return acc.astype(BF16)


def first_grad_kernel(count, at_ref, m_hbm, c_hbm, x_hbm, *refs):
    g_ref, m_ref, c_ref, x_ref, xa_ref, xb_ref, za_ref, zb_ref, tmp_ref, sems = refs
    members, levels, cells, _ = x_hbm.shape
    _, rows_x, rows_y, width = m_ref.shape
    head, rest = pl.ds(0, count), pl.ds(count, levels - count)
    copies = [(m_hbm, m_ref)]
    for e in range(members):
        copies.append((c_hbm.at[e], c_ref.at[e]))
        copies.append((x_hbm.at[e, head], x_ref.at[e, head]))
    for e in range(members):
        copies.append((x_hbm.at[e, rest], x_ref.at[e, rest]))
    copies = [pltpu.make_async_copy(s, d, sems.at[i]) for i, (s, d) in enumerate(copies)]
    for copy in copies:
        copy.start()
    copies[0].wait()

    def part(copy, ref, *at):
        def load():
            copy.wait()
            return ref[at].reshape(-1, ref.shape[-1])

        return load

    g_ref[...] = gradient(
        m_ref[0:count].reshape(count * cells, width),
        [part(copies[1 + 2 * e], c_ref, e) for e in range(members)],
        [part(copies[2 + 2 * e], x_ref, e, slice(0, count)) for e in range(members)],
    )
    core, even = core_of(at_ref[0]), parity_of(at_ref[0]) == 0
    xa_ref[...] = m_ref[:, (rows_x - 1) * (1 - core)]
    xb_ref[...] = m_ref[:, (rows_x - 1) * core]
    tmp_ref[0] = m_ref[:, :, 0:8, :].reshape(levels * rows_x, 8, width).astype(F32)
    tmp_ref[1] = m_ref[:, :, rows_y - 8 : rows_y, :].reshape(levels * rows_x, 8, width).astype(F32)
    lo, hi = tmp_ref[0, :, 0, :], tmp_ref[1, :, 7, :]
    za_ref[...] = jnp.where(even, hi, lo).astype(BF16)
    zb_ref[...] = jnp.where(even, lo, hi).astype(BF16)
    for copy in copies[1 + 2 * members :]:
        copy.wait()


def grad_kernel(level, m_ref, c_ref, x_ref, g_ref):
    members = c_ref.shape[0]

    def part(ref, *at):
        return lambda: ref[at]

    g_ref[...] = gradient(
        m_ref[level].reshape(g_ref.shape),
        [part(c_ref, e) for e in range(members)],
        [part(x_ref, e, level) for e in range(members)],
    )


def grad_cost(members, cells, frames, width):
    return pl.CostEstimate(
        flops=4 * members * cells * frames * width,
        bytes_accessed=2 * cells * (2 * width + members * frames) + 2 * members * width * frames,
        transcendentals=0,
    )


def first_grad(place, modes, coefficients, series, count):
    members, levels, cells, frames = series.shape
    _, rows_x, rows_y, width = modes.shape
    arrays = [modes, coefficients, series]
    outs = [jax.ShapeDtypeStruct((count * cells, width), BF16)]
    outs += [pltpu.VMEM(a.shape, a.dtype) for a in arrays]
    outs += [jax.ShapeDtypeStruct((levels, rows_y, width), BF16)] * 2
    outs += [jax.ShapeDtypeStruct((levels * rows_x, width), BF16)] * 2
    return pl.pallas_call(
        functools.partial(first_grad_kernel, count),
        in_specs=[SM] + [HBM] * 3,
        out_specs=[VM] * len(outs),
        out_shape=outs,
        scratch_shapes=[
            pltpu.VMEM((2, levels * rows_x, 8, width), F32),
            pltpu.SemaphoreType.DMA((1 + 3 * members,)),
        ],
        compiler_params=PARAMS,
        cost_estimate=grad_cost(members, count * cells, frames, width),
    )(place, *[pltpu.with_memory_space_constraint(a, pltpu.HBM) for a in arrays])


def grad_level(modes, coefficients, series, level):
    members, _, cells, frames = series.shape
    width = modes.shape[3]
    return pl.pallas_call(
        functools.partial(grad_kernel, level),
        in_specs=[VM] * 3,
        out_specs=VM,
        out_shape=jax.ShapeDtypeStruct((cells, width), BF16),
        compiler_params=PARAMS,
        cost_estimate=grad_cost(members, cells, frames, width),
    )(modes, coefficients, series)


def base_kernel(at_ref, m_ref, xa_ref, xb_ref, za_ref, zb_ref, base_ref):
    levels, rows_x, rows_y, width = m_ref.shape
    lower, even = core_of(at_ref[0]) == 0, parity_of(at_ref[0]) == 0
    shape = (rows_x, rows_y, width)
    at = lax.broadcasted_iota(jnp.int32, shape, 1)
    for level in range(levels):
        f = m_ref[level].astype(F32)
        xa, xb = xa_ref[level : level + 1].astype(F32), xb_ref[level : level + 1].astype(F32)
        rows = slice(level * rows_x, (level + 1) * rows_x)
        za, zb = za_ref[rows, :].astype(F32), zb_ref[rows, :].astype(F32)
        up = jnp.concatenate([jnp.where(lower, xb, xa), f[:-1]], axis=0)
        down = jnp.concatenate([f[1:], jnp.where(lower, xa, xb)], axis=0)
        zlo = jnp.broadcast_to(jnp.where(even, zb, za)[:, None, :], shape)
        zhi = jnp.broadcast_to(jnp.where(even, za, zb)[:, None, :], shape)
        left = jnp.where(at == 0, zlo, pltpu.roll(f, 1, 1))
        right = jnp.where(at == rows_y - 1, zhi, pltpu.roll(f, rows_y - 1, 1))
        bent = 4.0 * f - (down + up + right + left)
        base_ref[level] = (f - (ETA * LAM) * bent).reshape(rows_x * rows_y, width)


def split_squares(squares, rows):
    high = squares.astype(BF16).astype(F32)
    return jnp.concatenate([high, squares - high, jnp.zeros((rows - 4, 128), F32)], axis=0)


def emit(out_ref, half, proj_ref, gram_ref, squares):
    members = proj_ref.shape[0]
    for j in range(PARTS):
        tb, m, r = j // 4, (j // 2) % members, j % 2
        at = pl.multiple_of((half * 2 + tb) * 128, 128)
        block = proj_ref[m, r * 128 : (r + 1) * 128, pl.ds(at, 128)]
        out_ref[j, 0:PROJ_ROWS, :] = block.astype(BF16)
        at = pl.multiple_of(half * 128, 128)
        block = gram_ref[j * GRAM_ROWS : (j + 1) * GRAM_ROWS, pl.ds(at, 128)]
        out_ref[j, PROJ_ROWS:SUM_ROWS, :] = block.astype(BF16)
        out_ref[j, SUM_ROWS:PART_ROWS, :] = squares


def step_kernel(level, count, first, last, *refs):
    (at_ref, base_ref, own_ref, got_ref, x_ref), refs = refs[:5], refs[5:]
    if not first:
        (proj_in, gram_in, squares_in), refs = refs[:3], refs[3:]
    if last:
        moved_ref, keep_ref, send_ref, proj_ref, gram_ref = refs
    else:
        moved_ref, proj_ref, gram_ref, squares_ref = refs
    grad = own_ref[...].astype(F32) + got_ref[...].astype(F32)
    levels = slice(level, level + count)
    moved = (base_ref[levels].reshape(grad.shape) - ETA * grad).astype(BF16)
    moved_ref[...] = moved
    wide = moved.astype(F32)
    squares = jnp.sum(wide * wide, axis=0, keepdims=True)
    if not first:
        squares = squares + squares_in[...]
    turned = moved.T
    gram = jnp.dot(turned, moved, preferred_element_type=F32)
    gram_ref[...] = gram if first else gram_in[...] + gram
    for e in range(x_ref.shape[0]):
        x = x_ref[e, levels].reshape(grad.shape[0], -1)
        proj = jnp.dot(turned, x, preferred_element_type=F32)
        proj_ref[e] = proj if first else proj_in[e] + proj
    if last:
        core = core_of(at_ref[0])
        pair = jnp.concatenate([squares[:, 0:128], squares[:, 128:256]], axis=0)
        packed = split_squares(pair, 8).astype(BF16)
        emit(send_ref, 1 - core, proj_ref, gram_ref, packed)
        emit(keep_ref, core, proj_ref, gram_ref, packed)
    else:
        squares_ref[...] = squares


def step_levels(level, count, place, base, own, got, series, carry):
    members, levels, cells, frames = series.shape
    rows, width = own.shape
    first, last = carry is None, level + count == levels
    args = [place, base, own, got, series]
    if not first:
        args += list(carry)
    sums = [
        jax.ShapeDtypeStruct((members, width, frames), F32),
        jax.ShapeDtypeStruct((width, width), F32),
        jax.ShapeDtypeStruct((1, width), F32),
    ]
    outs = [jax.ShapeDtypeStruct((rows, width), BF16)]
    scratch, aliases = [], {}
    if last:
        outs += [jax.ShapeDtypeStruct((PARTS, PART_ROWS, 128), BF16)] * 2
        scratch = [pltpu.VMEM(s.shape, F32) for s in sums[:2]]
    else:
        outs += sums
        if not first:
            aliases = {5 + i: 1 + i for i in range(3)}
    return pl.pallas_call(
        functools.partial(step_kernel, level, count, first, last),
        in_specs=[SM] + [VM] * (len(args) - 1),
        out_specs=[VM] * len(outs),
        out_shape=outs,
        scratch_shapes=scratch,
        input_output_aliases=aliases,
        compiler_params=PARAMS,
        cost_estimate=pl.CostEstimate(
            flops=2 * rows * width * (width + members * frames),
            bytes_accessed=2 * rows * (4 * width + members * frames),
            transcendentals=0,
        ),
    )(*args)


def whole_squares(part):
    return part[SUM_ROWS : SUM_ROWS + 2, :] + part[SUM_ROWS + 2 : SUM_ROWS + 4, :]


def join_kernel(keep_ref, got_ref, out_ref):
    out_ref[:, 0:SUM_ROWS, :] = (
        keep_ref[:, 0:SUM_ROWS, :].astype(F32) + got_ref[:, 0:SUM_ROWS, :].astype(F32)
    ).astype(BF16)
    tail = keep_ref[0, SUM_ROWS:PART_ROWS, :].astype(F32) + got_ref[0, SUM_ROWS:PART_ROWS, :].astype(F32)
    packed = split_squares(tail[0:2, :] + tail[2:4, :], 8).astype(BF16)
    for j in range(PARTS):
        out_ref[j, SUM_ROWS:PART_ROWS, :] = packed


def gather_sum(in_ref):
    total = in_ref[0].astype(F32)
    for j in range(1, PARTS):
        total = total + in_ref[j].astype(F32)
    return total


def plane_kernel(in_ref, out_ref):
    total = gather_sum(in_ref)
    packed = split_squares(whole_squares(total), 8)
    mine = jnp.concatenate([total[0:SUM_ROWS, :], packed], axis=0).astype(BF16)
    for j in range(PARTS):
        out_ref[j] = mine


def reduce_kernel(total_cells, at_ref, in_ref, out_ref, shrink_ref, column_ref):
    core, part = core_of(at_ref[0]), part_of(at_ref[0])
    total = gather_sum(in_ref)
    squares = whole_squares(total)
    shrink = jnp.maximum(0.0, 1.0 - TAU / jnp.sqrt(squares / total_cells + 1e-06))
    shrink_ref[...] = shrink
    for k in range(2):
        column_ref[k * 128 : (k + 1) * 128, :] = jnp.broadcast_to(shrink[k : k + 1, :], (128, 128)).T
    at = pl.multiple_of(lax.rem(part, 2) * 128, 128)
    proj = column_ref[pl.ds(at, 128), :] * total[0:PROJ_ROWS, :] * (1.0 / math.sqrt(total_cells))
    at = pl.multiple_of(part * GRAM_ROWS, GRAM_ROWS)
    lanes = jnp.where(core == 0, shrink[0:1, :], shrink[1:2, :])
    gram = column_ref[pl.ds(at, GRAM_ROWS), :] * total[PROJ_ROWS:SUM_ROWS, :] * lanes * (1.0 / total_cells)
    mine = jnp.concatenate([proj, gram], axis=0).astype(BF16)
    for j in range(PARTS):
        out_ref[j] = mine


def scale_kernel(shrink_ref, *refs):
    out_ref = refs[-1]
    at = 0
    for m_ref in refs[:-1]:
        rows = slice(at, at + m_ref.shape[0])
        at = rows.stop
        for k in range(2):
            lanes = slice(k * 128, (k + 1) * 128)
            out_ref[rows, lanes] = (m_ref[:, lanes].astype(F32) * shrink_ref[k : k + 1, :]).astype(BF16)


def final_kernel(at_ref, own_ref, got_ref, proj_ref, gram_ref):
    core = core_of(at_ref[0])
    members = proj_ref.shape[0]
    for ref, half in ((own_ref, core), (got_ref, 1 - core)):
        for j in range(PARTS):
            tb, m, r = j // 4, (j // 2) % members, j % 2
            at = pl.multiple_of((half * 2 + tb) * 128, 128)
            proj_ref[m, r * 128 : (r + 1) * 128, pl.ds(at, 128)] = ref[j, 0:PROJ_ROWS, :].astype(F32)
            at = pl.multiple_of(half * 128, 128)
            gram_ref[j * GRAM_ROWS : (j + 1) * GRAM_ROWS, pl.ds(at, 128)] = (
                ref[j, PROJ_ROWS:SUM_ROWS, :].astype(F32)
            )


def both_ways(pairs):
    return [p for i, j in pairs for p in ((i, j), (j, i))]


def local(snapshots, coefficients, modes):
    members, levels, rows_x, rows_y, frames = snapshots.shape
    width = modes.shape[3]
    cells = rows_x * rows_y
    local_cells = levels * cells
    n_sx, n_z = lax.axis_size(SX), lax.axis_size("z")
    total_cells = local_cells * n_sx * n_z
    core = lax.axis_index("c").astype(jnp.int32)
    parity = lax.axis_index("z").astype(jnp.int32) & 1
    part = lax.axis_index(PLANE).astype(jnp.int32)
    place = (core + 2 * parity + 4 * part).reshape(1)
    series = snapshots.reshape(members, levels, cells, frames)
    swap = [(0, 1), (1, 0)]

    chunks = [(0, 2), (2, 1), (3, 1)]
    g, modes, coefficients, series, edge_a, edge_b, row_a, row_b = first_grad(
        place, modes, coefficients, series, chunks[0][1]
    )
    own, got = [g], [lax.ppermute(g, "ens", swap)]
    xb = lax.ppermute(edge_b, SX, both_ways([(i, i + 1) for i in range(1, n_sx - 1, 2)]))
    za = lax.ppermute(row_a, "z", both_ways([(i, i + 1) for i in range(0, n_z, 2)]))
    zb = lax.ppermute(row_b, "z", both_ways([(i, i + 1) for i in range(1, n_z - 1, 2)]))
    xa = lax.ppermute(edge_a, "c", swap)

    def send_level(level, *after):
        c, *_ = lax.optimization_barrier((coefficients, *after))
        g = grad_level(modes, c, series, level)
        own.append(g)
        got.append(lax.ppermute(g, "ens", swap))

    send_level(2, xa, xb, za, zb)
    base = pl.pallas_call(
        base_kernel,
        in_specs=[SM] + [VM] * 5,
        out_specs=VM,
        out_shape=jax.ShapeDtypeStruct((levels, cells, width), F32),
        compiler_params=PARAMS,
        cost_estimate=pl.CostEstimate(flops=12 * local_cells * width, bytes_accessed=6 * local_cells * width, transcendentals=0),
    )(place, modes, xa, xb, za, zb)
    send_level(3, own[1], base)

    moved, carry = [], None
    for i, (level, count) in enumerate(chunks):
        m, *carry = step_levels(level, count, place, base, own[i], got[i], series, carry)
        moved.append(m)
    keep, send = carry

    part_shape = jax.ShapeDtypeStruct((PARTS, PART_ROWS, 128), BF16)
    other = lax.ppermute(send, "c", swap)
    joined = pl.pallas_call(
        join_kernel, in_specs=[VM, VM], out_specs=VM, out_shape=part_shape, compiler_params=PARAMS
    )(keep, other)
    parts = lax.all_to_all(joined, PLANE, 0, 0)
    planes = pl.pallas_call(
        plane_kernel, in_specs=[VM], out_specs=VM, out_shape=part_shape, compiler_params=PARAMS
    )(parts)
    planes = lax.all_to_all(planes, "z", 0, 0)
    spread, shrink = pl.pallas_call(
        functools.partial(reduce_kernel, total_cells),
        in_specs=[SM, VM],
        out_specs=[VM, VM],
        out_shape=[
            jax.ShapeDtypeStruct((PARTS, SUM_ROWS, 128), BF16),
            jax.ShapeDtypeStruct((2, 128), F32),
        ],
        scratch_shapes=[pltpu.VMEM((width, 128), F32)],
        compiler_params=PARAMS,
    )(place, planes)
    half = lax.all_to_all(spread, PLANE, 0, 0)
    new_modes = pl.pallas_call(
        scale_kernel,
        in_specs=[VM] * (1 + len(moved)),
        out_specs=VM,
        out_shape=jax.ShapeDtypeStruct((local_cells, width), BF16),
        compiler_params=PARAMS,
    )(shrink, *moved)
    half, new_modes = lax.optimization_barrier((half, new_modes))
    other_half = lax.ppermute(half, "c", swap)
    projected, gram = pl.pallas_call(
        final_kernel,
        in_specs=[SM, VM, VM],
        out_specs=[VM, VM],
        out_shape=[
            jax.ShapeDtypeStruct((members, width, frames), F32),
            jax.ShapeDtypeStruct((width, width), F32),
        ],
        compiler_params=PARAMS,
    )(place, half, other_half)
    return (new_modes.reshape(levels, rows_x, rows_y, width), gram, projected)


def solution(mesh):
    ens, n_sx, n_sy = (mesh.shape[a] for a in ("ens", "sx", "sy"))
    fine = Mesh(mesh.devices.reshape(ens, 2, n_sx // 4, 2, n_sy), ("ens", "xh", "y", "c", "z"))
    in_specs = (P("ens", None, SX, "z", None), P("ens", None, None), P(None, SX, "z", None))
    out_specs = (P(None, SX, "z", None), P(), P("ens", None, None))
    return jax.shard_map(local, mesh=fine, in_specs=in_specs, out_specs=out_specs, check_vma=False)
```

```python
import functools
import math

import jax
import jax.numpy as jnp
from jax import lax
from jax.experimental import pallas as pl
from jax.experimental.pallas import tpu as pltpu
from jax.sharding import Mesh, PartitionSpec as P

ETA = 0.25
LAM = 0.5
TAU = 0.4

F32 = jnp.float32
BF16 = jnp.bfloat16
VMEM_LIMIT = 40 * 1024 * 1024
PARAMS = pltpu.CompilerParams(vmem_limit_bytes=VMEM_LIMIT)

SX = ("xh", "y", "c")
PLANE = ("xh", "y")
PARTS = 8
PROJ_ROWS = 128
GRAM_ROWS = 32
SUM_ROWS = PROJ_ROWS + GRAM_ROWS
PART_ROWS = SUM_ROWS + 8

VM = pl.BlockSpec(memory_space=pltpu.VMEM)
SM = pl.BlockSpec(memory_space=pltpu.SMEM)
HBM = pl.BlockSpec(memory_space=pltpu.HBM)


def core_of(place):
    return place & 1


def parity_of(place):
    return (place >> 1) & 1


def part_of(place):
    return place >> 2


def gradient(m, coefficients, series):
    acc = None
    for e in range(len(coefficients)):
        c = coefficients[e]()
        fitted = jnp.dot(m, c, preferred_element_type=F32)
        misfit = (fitted - series[e]().astype(F32)).astype(BF16)
        term = lax.dot_general(misfit, c, (((1,), (1,)), ((), ())), preferred_element_type=F32)
        acc = term if acc is None else acc + term
    return acc.astype(BF16)


def edge_kernel(at_ref, m_hbm, out_ref, sem):
    last = m_hbm.shape[1] - 1
    copy = pltpu.make_async_copy(m_hbm.at[:, last * core_of(at_ref[0])], out_ref, sem)
    copy.start()
    copy.wait()


def first_grad_kernel(count, at_ref, m_hbm, c_hbm, x_hbm, *refs):
    g_ref, m_ref, c_ref, x_ref, xa_ref, za_ref, zb_ref, tmp_ref, sems = refs
    members, levels, cells, _ = x_hbm.shape
    _, rows_x, rows_y, width = m_ref.shape
    head, rest = pl.ds(0, count), pl.ds(count, levels - count)
    copies = [(m_hbm, m_ref)]
    for e in range(members):
        copies.append((c_hbm.at[e], c_ref.at[e]))
        copies.append((x_hbm.at[e, head], x_ref.at[e, head]))
    for e in range(members):
        copies.append((x_hbm.at[e, rest], x_ref.at[e, rest]))
    copies = [pltpu.make_async_copy(s, d, sems.at[i]) for i, (s, d) in enumerate(copies)]
    for copy in copies:
        copy.start()
    copies[0].wait()

    def part(copy, ref, *at):
        def load():
            copy.wait()
            return ref[at].reshape(-1, ref.shape[-1])

        return load

    g_ref[...] = gradient(
        m_ref[0:count].reshape(count * cells, width),
        [part(copies[1 + 2 * e], c_ref, e) for e in range(members)],
        [part(copies[2 + 2 * e], x_ref, e, slice(0, count)) for e in range(members)],
    )
    core, even = core_of(at_ref[0]), parity_of(at_ref[0]) == 0
    xa_ref[...] = m_ref[:, (rows_x - 1) * (1 - core)]
    tmp_ref[0] = m_ref[:, :, 0:8, :].reshape(levels * rows_x, 8, width).astype(F32)
    tmp_ref[1] = m_ref[:, :, rows_y - 8 : rows_y, :].reshape(levels * rows_x, 8, width).astype(F32)
    lo, hi = tmp_ref[0, :, 0, :], tmp_ref[1, :, 7, :]
    za_ref[...] = jnp.where(even, hi, lo).astype(BF16)
    zb_ref[...] = jnp.where(even, lo, hi).astype(BF16)
    for copy in copies[1 + 2 * members :]:
        copy.wait()


def grad_kernel(level, m_ref, c_ref, x_ref, g_ref):
    members = c_ref.shape[0]

    def part(ref, *at):
        return lambda: ref[at]

    g_ref[...] = gradient(
        m_ref[level].reshape(g_ref.shape),
        [part(c_ref, e) for e in range(members)],
        [part(x_ref, e, level) for e in range(members)],
    )


def grad_cost(members, cells, frames, width):
    return pl.CostEstimate(
        flops=4 * members * cells * frames * width,
        bytes_accessed=2 * cells * (2 * width + members * frames) + 2 * members * width * frames,
        transcendentals=0,
    )


def first_grad(place, modes, coefficients, series, count):
    members, levels, cells, frames = series.shape
    _, rows_x, rows_y, width = modes.shape
    arrays = [modes, coefficients, series]
    outs = [jax.ShapeDtypeStruct((count * cells, width), BF16)]
    outs += [pltpu.VMEM(a.shape, a.dtype) for a in arrays]
    outs += [jax.ShapeDtypeStruct((levels, rows_y, width), BF16)]
    outs += [jax.ShapeDtypeStruct((levels * rows_x, width), BF16)] * 2
    return pl.pallas_call(
        functools.partial(first_grad_kernel, count),
        in_specs=[SM] + [HBM] * 3,
        out_specs=[VM] * len(outs),
        out_shape=outs,
        scratch_shapes=[
            pltpu.VMEM((2, levels * rows_x, 8, width), F32),
            pltpu.SemaphoreType.DMA((1 + 3 * members,)),
        ],
        compiler_params=PARAMS,
        cost_estimate=grad_cost(members, count * cells, frames, width),
    )(place, *[pltpu.with_memory_space_constraint(a, pltpu.HBM) for a in arrays])


def grad_level(modes, coefficients, series, level):
    members, _, cells, frames = series.shape
    width = modes.shape[3]
    return pl.pallas_call(
        functools.partial(grad_kernel, level),
        in_specs=[VM] * 3,
        out_specs=VM,
        out_shape=jax.ShapeDtypeStruct((cells, width), BF16),
        compiler_params=PARAMS,
        cost_estimate=grad_cost(members, cells, frames, width),
    )(modes, coefficients, series)


def base_kernel(at_ref, m_ref, xa_ref, xb_ref, za_ref, zb_ref, base_ref):
    levels, rows_x, rows_y, width = m_ref.shape
    lower, even = core_of(at_ref[0]) == 0, parity_of(at_ref[0]) == 0
    shape = (rows_x, rows_y, width)
    at = lax.broadcasted_iota(jnp.int32, shape, 1)
    for level in range(levels):
        f = m_ref[level].astype(F32)
        xa, xb = xa_ref[level : level + 1].astype(F32), xb_ref[level : level + 1].astype(F32)
        rows = slice(level * rows_x, (level + 1) * rows_x)
        za, zb = za_ref[rows, :].astype(F32), zb_ref[rows, :].astype(F32)
        up = jnp.concatenate([jnp.where(lower, xb, xa), f[:-1]], axis=0)
        down = jnp.concatenate([f[1:], jnp.where(lower, xa, xb)], axis=0)
        zlo = jnp.broadcast_to(jnp.where(even, zb, za)[:, None, :], shape)
        zhi = jnp.broadcast_to(jnp.where(even, za, zb)[:, None, :], shape)
        left = jnp.where(at == 0, zlo, pltpu.roll(f, 1, 1))
        right = jnp.where(at == rows_y - 1, zhi, pltpu.roll(f, rows_y - 1, 1))
        bent = 4.0 * f - (down + up + right + left)
        base_ref[level] = (f - (ETA * LAM) * bent).reshape(rows_x * rows_y, width)


def split_squares(squares, rows):
    high = squares.astype(BF16).astype(F32)
    return jnp.concatenate([high, squares - high, jnp.zeros((rows - 4, 128), F32)], axis=0)


def emit(out_ref, half, proj_ref, gram_ref, squares):
    members = proj_ref.shape[0]
    for j in range(PARTS):
        tb, m, r = j // 4, (j // 2) % members, j % 2
        at = pl.multiple_of((half * 2 + tb) * 128, 128)
        block = proj_ref[m, r * 128 : (r + 1) * 128, pl.ds(at, 128)]
        out_ref[j, 0:PROJ_ROWS, :] = block.astype(BF16)
        at = pl.multiple_of(half * 128, 128)
        block = gram_ref[j * GRAM_ROWS : (j + 1) * GRAM_ROWS, pl.ds(at, 128)]
        out_ref[j, PROJ_ROWS:SUM_ROWS, :] = block.astype(BF16)
        out_ref[j, SUM_ROWS:PART_ROWS, :] = squares


def step_kernel(level, count, first, last, *refs):
    (at_ref, base_ref, own_ref, got_ref, x_ref), refs = refs[:5], refs[5:]
    if not first:
        (proj_in, gram_in, squares_in), refs = refs[:3], refs[3:]
    if last:
        moved_ref, keep_ref, send_ref, proj_ref, gram_ref = refs
    else:
        moved_ref, proj_ref, gram_ref, squares_ref = refs
    grad = own_ref[...].astype(F32) + got_ref[...].astype(F32)
    levels = slice(level, level + count)
    moved = (base_ref[levels].reshape(grad.shape) - ETA * grad).astype(BF16)
    moved_ref[...] = moved
    wide = moved.astype(F32)
    squares = jnp.sum(wide * wide, axis=0, keepdims=True)
    if not first:
        squares = squares + squares_in[...]
    turned = moved.T
    gram = jnp.dot(turned, moved, preferred_element_type=F32)
    gram_ref[...] = gram if first else gram_in[...] + gram
    for e in range(x_ref.shape[0]):
        x = x_ref[e, levels].reshape(grad.shape[0], -1)
        proj = jnp.dot(turned, x, preferred_element_type=F32)
        proj_ref[e] = proj if first else proj_in[e] + proj
    if last:
        core = core_of(at_ref[0])
        pair = jnp.concatenate([squares[:, 0:128], squares[:, 128:256]], axis=0)
        packed = split_squares(pair, 8).astype(BF16)
        emit(send_ref, 1 - core, proj_ref, gram_ref, packed)
        emit(keep_ref, core, proj_ref, gram_ref, packed)
    else:
        squares_ref[...] = squares


def step_levels(level, count, place, base, own, got, series, carry):
    members, levels, cells, frames = series.shape
    rows, width = own.shape
    first, last = carry is None, level + count == levels
    args = [place, base, own, got, series]
    if not first:
        args += list(carry)
    sums = [
        jax.ShapeDtypeStruct((members, width, frames), F32),
        jax.ShapeDtypeStruct((width, width), F32),
        jax.ShapeDtypeStruct((1, width), F32),
    ]
    outs = [jax.ShapeDtypeStruct((rows, width), BF16)]
    scratch, aliases = [], {}
    if last:
        outs += [jax.ShapeDtypeStruct((PARTS, PART_ROWS, 128), BF16)] * 2
        scratch = [pltpu.VMEM(s.shape, F32) for s in sums[:2]]
    else:
        outs += sums
        if not first:
            aliases = {5 + i: 1 + i for i in range(3)}
    return pl.pallas_call(
        functools.partial(step_kernel, level, count, first, last),
        in_specs=[SM] + [VM] * (len(args) - 1),
        out_specs=[VM] * len(outs),
        out_shape=outs,
        scratch_shapes=scratch,
        input_output_aliases=aliases,
        compiler_params=PARAMS,
        cost_estimate=pl.CostEstimate(
            flops=2 * rows * width * (width + members * frames),
            bytes_accessed=2 * rows * (4 * width + members * frames),
            transcendentals=0,
        ),
    )(*args)


def whole_squares(part):
    return part[SUM_ROWS : SUM_ROWS + 2, :] + part[SUM_ROWS + 2 : SUM_ROWS + 4, :]


def packed_squares(total):
    return split_squares(whole_squares(total), 8).astype(BF16)


def join_kernel(keep_ref, got_ref, out_ref):
    out_ref[:, 0:SUM_ROWS, :] = (
        keep_ref[:, 0:SUM_ROWS, :].astype(F32) + got_ref[:, 0:SUM_ROWS, :].astype(F32)
    ).astype(BF16)
    tail = keep_ref[0].astype(F32) + got_ref[0].astype(F32)
    packed = packed_squares(tail)
    for j in range(PARTS):
        out_ref[j, SUM_ROWS:PART_ROWS, :] = packed


def plane_kernel(in_ref, out_ref):
    total = in_ref[0].astype(F32)
    for j in range(1, PARTS):
        total = total + in_ref[j].astype(F32)
    out_ref[0:SUM_ROWS, :] = total[0:SUM_ROWS, :].astype(BF16)
    out_ref[SUM_ROWS:PART_ROWS, :] = packed_squares(total)


def add_kernel(own_ref, got_ref, out_ref):
    total = own_ref[...].astype(F32) + got_ref[...].astype(F32)
    out_ref[0:SUM_ROWS, :] = total[0:SUM_ROWS, :].astype(BF16)
    out_ref[SUM_ROWS:PART_ROWS, :] = packed_squares(total)


def reduce_kernel(total_cells, at_ref, own_ref, got_ref, out_ref, shrink_ref, column_ref):
    core, part = core_of(at_ref[0]), part_of(at_ref[0])
    total = own_ref[...].astype(F32) + got_ref[...].astype(F32)
    squares = whole_squares(total)
    shrink = jnp.maximum(0.0, 1.0 - TAU / jnp.sqrt(squares / total_cells + 1e-06))
    shrink_ref[...] = shrink
    for k in range(2):
        column_ref[k * 128 : (k + 1) * 128, :] = jnp.broadcast_to(shrink[k : k + 1, :], (128, 128)).T
    at = pl.multiple_of(lax.rem(part, 2) * 128, 128)
    proj = column_ref[pl.ds(at, 128), :] * total[0:PROJ_ROWS, :] * (1.0 / math.sqrt(total_cells))
    at = pl.multiple_of(part * GRAM_ROWS, GRAM_ROWS)
    lanes = jnp.where(core == 0, shrink[0:1, :], shrink[1:2, :])
    gram = column_ref[pl.ds(at, GRAM_ROWS), :] * total[PROJ_ROWS:SUM_ROWS, :] * lanes * (1.0 / total_cells)
    mine = jnp.concatenate([proj, gram], axis=0).astype(BF16)
    for j in range(PARTS):
        out_ref[j] = mine


def scale_kernel(shrink_ref, *refs):
    out_ref = refs[-1]
    at = 0
    for m_ref in refs[:-1]:
        rows = slice(at, at + m_ref.shape[0])
        at = rows.stop
        for k in range(2):
            lanes = slice(k * 128, (k + 1) * 128)
            out_ref[rows, lanes] = (m_ref[:, lanes].astype(F32) * shrink_ref[k : k + 1, :]).astype(BF16)


def final_kernel(at_ref, own_ref, got_ref, proj_ref, gram_ref):
    core = core_of(at_ref[0])
    members = proj_ref.shape[0]
    for ref, half in ((own_ref, core), (got_ref, 1 - core)):
        for j in range(PARTS):
            tb, m, r = j // 4, (j // 2) % members, j % 2
            at = pl.multiple_of((half * 2 + tb) * 128, 128)
            proj_ref[m, r * 128 : (r + 1) * 128, pl.ds(at, 128)] = ref[j, 0:PROJ_ROWS, :].astype(F32)
            at = pl.multiple_of(half * 128, 128)
            gram_ref[j * GRAM_ROWS : (j + 1) * GRAM_ROWS, pl.ds(at, 128)] = (
                ref[j, PROJ_ROWS:SUM_ROWS, :].astype(F32)
            )


def both_ways(pairs):
    return [p for i, j in pairs for p in ((i, j), (j, i))]


def local(snapshots, coefficients, modes):
    members, levels, rows_x, rows_y, frames = snapshots.shape
    width = modes.shape[3]
    cells = rows_x * rows_y
    local_cells = levels * cells
    n_sx, n_z = lax.axis_size(SX), lax.axis_size("z")
    total_cells = local_cells * n_sx * n_z
    core = lax.axis_index("c").astype(jnp.int32)
    parity = lax.axis_index("z").astype(jnp.int32) & 1
    part = lax.axis_index(PLANE).astype(jnp.int32)
    place = (core + 2 * parity + 4 * part).reshape(1)
    series = snapshots.reshape(members, levels, cells, frames)
    swap = [(0, 1), (1, 0)]

    chunks = [(0, 2), (2, 1), (3, 1)]
    edge_b = pl.pallas_call(
        edge_kernel,
        in_specs=[SM, HBM],
        out_specs=VM,
        out_shape=jax.ShapeDtypeStruct((levels, rows_y, width), BF16),
        scratch_shapes=[pltpu.SemaphoreType.DMA],
        compiler_params=PARAMS,
    )(place, pltpu.with_memory_space_constraint(modes, pltpu.HBM))
    xb = lax.ppermute(edge_b, SX, both_ways([(i, i + 1) for i in range(1, n_sx - 1, 2)]))
    coefficients, _ = lax.optimization_barrier((coefficients, edge_b))
    g, modes, coefficients, series, edge_a, row_a, row_b = first_grad(
        place, modes, coefficients, series, chunks[0][1]
    )
    g, xb = lax.optimization_barrier((g, xb))
    own, got = [g], [lax.ppermute(g, "ens", swap)]
    za = lax.ppermute(row_a, "z", both_ways([(i, i + 1) for i in range(0, n_z, 2)]))
    zb = lax.ppermute(row_b, "z", both_ways([(i, i + 1) for i in range(1, n_z - 1, 2)]))
    xa = lax.ppermute(edge_a, "c", swap)

    def send_level(level, *after):
        c, *_ = lax.optimization_barrier((coefficients, *after))
        g = grad_level(modes, c, series, level)
        own.append(g)
        got.append(lax.ppermute(g, "ens", swap))

    send_level(2, xa, za, zb)
    base = pl.pallas_call(
        base_kernel,
        in_specs=[SM] + [VM] * 5,
        out_specs=VM,
        out_shape=jax.ShapeDtypeStruct((levels, cells, width), F32),
        compiler_params=PARAMS,
        cost_estimate=pl.CostEstimate(flops=12 * local_cells * width, bytes_accessed=6 * local_cells * width, transcendentals=0),
    )(place, modes, xa, xb, za, zb)
    send_level(3, own[1])

    moved, carry = [], None
    for i, (level, count) in enumerate(chunks):
        m, *carry = step_levels(level, count, place, base, own[i], got[i], series, carry)
        moved.append(m)
    keep, send = carry

    part_shape = jax.ShapeDtypeStruct((PARTS, PART_ROWS, 128), BF16)
    other = lax.ppermute(send, "c", swap)
    joined = pl.pallas_call(
        join_kernel, in_specs=[VM, VM], out_specs=VM, out_shape=part_shape, compiler_params=PARAMS
    )(keep, other)
    parts = lax.all_to_all(joined, PLANE, 0, 0)
    line_shape = jax.ShapeDtypeStruct((PART_ROWS, 128), BF16)
    line = pl.pallas_call(
        plane_kernel, in_specs=[VM], out_specs=VM, out_shape=line_shape, compiler_params=PARAMS
    )(parts)
    span = 2
    while True:
        pairs = [(i, i ^ (span - 1)) for i in range(n_z)]
        near = lax.ppermute(line, "z", pairs)
        if span == n_z:
            break
        line = pl.pallas_call(
            add_kernel, in_specs=[VM, VM], out_specs=VM, out_shape=line_shape, compiler_params=PARAMS
        )(line, near)
        span *= 2
    spread, shrink = pl.pallas_call(
        functools.partial(reduce_kernel, total_cells),
        in_specs=[SM, VM, VM],
        out_specs=[VM, VM],
        out_shape=[
            jax.ShapeDtypeStruct((PARTS, SUM_ROWS, 128), BF16),
            jax.ShapeDtypeStruct((2, 128), F32),
        ],
        scratch_shapes=[pltpu.VMEM((width, 128), F32)],
        compiler_params=PARAMS,
    )(place, line, near)
    half = lax.all_to_all(spread, PLANE, 0, 0)
    new_modes = pl.pallas_call(
        scale_kernel,
        in_specs=[VM] * (1 + len(moved)),
        out_specs=VM,
        out_shape=jax.ShapeDtypeStruct((local_cells, width), BF16),
        compiler_params=PARAMS,
    )(shrink, *moved)
    half, new_modes = lax.optimization_barrier((half, new_modes))
    other_half = lax.ppermute(half, "c", swap)
    projected, gram = pl.pallas_call(
        final_kernel,
        in_specs=[SM, VM, VM],
        out_specs=[VM, VM],
        out_shape=[
            jax.ShapeDtypeStruct((members, width, frames), F32),
            jax.ShapeDtypeStruct((width, width), F32),
        ],
        compiler_params=PARAMS,
    )(place, half, other_half)
    return (new_modes.reshape(levels, rows_x, rows_y, width), gram, projected)


def solution(mesh):
    ens, n_sx, n_sy = (mesh.shape[a] for a in ("ens", "sx", "sy"))
    fine = Mesh(mesh.devices.reshape(ens, 2, n_sx // 4, 2, n_sy), ("ens", "xh", "y", "c", "z"))
    in_specs = (P("ens", None, SX, "z", None), P("ens", None, None), P(None, SX, "z", None))
    out_specs = (P(None, SX, "z", None), P(), P("ens", None, None))
    return jax.shard_map(local, mesh=fine, in_specs=in_specs, out_specs=out_specs, check_vma=False)
```

```python
import functools
import math

import jax
import jax.numpy as jnp
from jax import lax
from jax.experimental import pallas as pl
from jax.experimental.pallas import tpu as pltpu
from jax.sharding import Mesh, PartitionSpec as P

ETA = 0.25
LAM = 0.5
TAU = 0.4

F32 = jnp.float32
BF16 = jnp.bfloat16
VMEM_LIMIT = 40 * 1024 * 1024
PARAMS = pltpu.CompilerParams(vmem_limit_bytes=VMEM_LIMIT)

SX = ("xh", "y", "c")
PLANE = ("xh", "y")
PARTS = 8
PROJ_ROWS = 128
GRAM_ROWS = 32
SUM_ROWS = PROJ_ROWS + GRAM_ROWS
PART_ROWS = SUM_ROWS + 8

VM = pl.BlockSpec(memory_space=pltpu.VMEM)
SM = pl.BlockSpec(memory_space=pltpu.SMEM)
HBM = pl.BlockSpec(memory_space=pltpu.HBM)


def core_of(place):
    return place & 1


def parity_of(place):
    return (place >> 1) & 1


def part_of(place):
    return place >> 2


def gradient(m, coefficients, series):
    acc = None
    for e in range(len(coefficients)):
        c = coefficients[e]()
        fitted = jnp.dot(m, c, preferred_element_type=F32)
        misfit = (fitted - series[e]().astype(F32)).astype(BF16)
        term = lax.dot_general(misfit, c, (((1,), (1,)), ((), ())), preferred_element_type=F32)
        acc = term if acc is None else acc + term
    return acc.astype(BF16)


def start_all(copies, sems):
    copies = [pltpu.make_async_copy(s, d, sems.at[i]) for i, (s, d) in enumerate(copies)]
    for copy in copies:
        copy.start()
    return copies


def after(copy, ref, *at):
    def load():
        copy.wait()
        return ref[at].reshape(-1, ref.shape[-1])

    return load


def first_grad_kernel(at_ref, m_hbm, c_hbm, x_hbm, g_ref, c_ref, x_ref, xb_ref, m_ref, sems):
    members = c_hbm.shape[0]
    last = m_hbm.shape[1] - 1
    copies = [(m_hbm.at[0], m_ref)]
    for e in range(members):
        copies.append((c_hbm.at[e], c_ref.at[e]))
        copies.append((x_hbm.at[e, 0], x_ref.at[e]))
    copies.append((m_hbm.at[:, last * core_of(at_ref[0])], xb_ref))
    copies = start_all(copies, sems)
    copies[0].wait()
    g_ref[...] = gradient(
        m_ref[...].reshape(g_ref.shape),
        [after(copies[1 + 2 * e], c_ref, e) for e in range(members)],
        [after(copies[2 + 2 * e], x_ref, e) for e in range(members)],
    )
    copies[-1].wait()


def second_grad_kernel(count, at_ref, m_hbm, c_ref, x_hbm, *refs):
    g_ref, m_ref, x_ref, xa_ref, za_ref, zb_ref, tmp_ref, sems = refs
    members, levels, cells, _ = x_hbm.shape
    _, rows_x, rows_y, width = m_ref.shape
    copies = [(m_hbm, m_ref)]
    for level in range(1, levels):
        for e in range(members):
            copies.append((x_hbm.at[e, level], x_ref.at[e, level - 1]))
    copies = start_all(copies, sems)
    copies[0].wait()
    core, even = core_of(at_ref[0]), parity_of(at_ref[0]) == 0
    xa_ref[...] = m_ref[:, (rows_x - 1) * (1 - core)]
    tmp_ref[0] = m_ref[:, :, 0:8, :].reshape(levels * rows_x, 8, width).astype(F32)
    tmp_ref[1] = m_ref[:, :, rows_y - 8 : rows_y, :].reshape(levels * rows_x, 8, width).astype(F32)
    lo, hi = tmp_ref[0, :, 0, :], tmp_ref[1, :, 7, :]
    za_ref[...] = jnp.where(even, hi, lo).astype(BF16)
    zb_ref[...] = jnp.where(even, lo, hi).astype(BF16)
    for i in range(count):
        g_ref[i * cells : (i + 1) * cells, :] = gradient(
            m_ref[1 + i].reshape(cells, width),
            [functools.partial(c_ref.__getitem__, e) for e in range(members)],
            [after(copies[1 + i * members + e], x_ref, e, i) for e in range(members)],
        )
    for copy in copies[1 + count * members :]:
        copy.wait()


def grad_kernel(level, m_ref, c_ref, x_ref, g_ref):
    members = c_ref.shape[0]
    g_ref[...] = gradient(
        m_ref[level].reshape(g_ref.shape),
        [functools.partial(c_ref.__getitem__, e) for e in range(members)],
        [functools.partial(x_ref.__getitem__, (e, level - 1)) for e in range(members)],
    )


def grad_cost(members, cells, frames, width):
    return pl.CostEstimate(
        flops=4 * members * cells * frames * width,
        bytes_accessed=2 * cells * (2 * width + members * frames) + 2 * members * width * frames,
        transcendentals=0,
    )


def in_hbm(array):
    return pltpu.with_memory_space_constraint(array, pltpu.HBM)


def first_grad(place, modes, coefficients, series):
    members, _, cells, frames = series.shape
    levels, rows_x, rows_y, width = modes.shape
    outs = [
        jax.ShapeDtypeStruct((cells, width), BF16),
        pltpu.VMEM(coefficients.shape, BF16),
        pltpu.VMEM((members, cells, frames), BF16),
        jax.ShapeDtypeStruct((levels, rows_y, width), BF16),
    ]
    return pl.pallas_call(
        first_grad_kernel,
        in_specs=[SM] + [HBM] * 3,
        out_specs=[VM] * len(outs),
        out_shape=outs,
        scratch_shapes=[
            pltpu.VMEM((rows_x, rows_y, width), BF16),
            pltpu.SemaphoreType.DMA((2 + 2 * members,)),
        ],
        compiler_params=PARAMS,
        cost_estimate=grad_cost(members, cells, frames, width),
    )(place, in_hbm(modes), in_hbm(coefficients), in_hbm(series))


def second_grad(place, modes, coefficients, series, count):
    members, levels, cells, frames = series.shape
    _, rows_x, rows_y, width = modes.shape
    outs = [
        jax.ShapeDtypeStruct((count * cells, width), BF16),
        pltpu.VMEM(modes.shape, BF16),
        pltpu.VMEM((members, levels - 1, cells, frames), BF16),
        jax.ShapeDtypeStruct((levels, rows_y, width), BF16),
        jax.ShapeDtypeStruct((levels * rows_x, width), BF16),
        jax.ShapeDtypeStruct((levels * rows_x, width), BF16),
    ]
    return pl.pallas_call(
        functools.partial(second_grad_kernel, count),
        in_specs=[SM, HBM, VM, HBM],
        out_specs=[VM] * len(outs),
        out_shape=outs,
        scratch_shapes=[
            pltpu.VMEM((2, levels * rows_x, 8, width), F32),
            pltpu.SemaphoreType.DMA((1 + members * (levels - 1),)),
        ],
        compiler_params=PARAMS,
        cost_estimate=grad_cost(members, count * cells, frames, width),
    )(place, in_hbm(modes), coefficients, in_hbm(series))


def grad_level(modes, coefficients, series, level):
    members, _, cells, frames = series.shape
    width = modes.shape[3]
    return pl.pallas_call(
        functools.partial(grad_kernel, level),
        in_specs=[VM] * 3,
        out_specs=VM,
        out_shape=jax.ShapeDtypeStruct((cells, width), BF16),
        compiler_params=PARAMS,
        cost_estimate=grad_cost(members, cells, frames, width),
    )(modes, coefficients, series)


def base_kernel(at_ref, m_ref, xa_ref, xb_ref, za_ref, zb_ref, base_ref):
    levels, rows_x, rows_y, width = m_ref.shape
    lower, even = core_of(at_ref[0]) == 0, parity_of(at_ref[0]) == 0
    shape = (rows_x, rows_y, width)
    at = lax.broadcasted_iota(jnp.int32, shape, 1)
    for level in range(levels):
        f = m_ref[level].astype(F32)
        xa, xb = xa_ref[level : level + 1].astype(F32), xb_ref[level : level + 1].astype(F32)
        rows = slice(level * rows_x, (level + 1) * rows_x)
        za, zb = za_ref[rows, :].astype(F32), zb_ref[rows, :].astype(F32)
        up = jnp.concatenate([jnp.where(lower, xb, xa), f[:-1]], axis=0)
        down = jnp.concatenate([f[1:], jnp.where(lower, xa, xb)], axis=0)
        zlo = jnp.broadcast_to(jnp.where(even, zb, za)[:, None, :], shape)
        zhi = jnp.broadcast_to(jnp.where(even, za, zb)[:, None, :], shape)
        left = jnp.where(at == 0, zlo, pltpu.roll(f, 1, 1))
        right = jnp.where(at == rows_y - 1, zhi, pltpu.roll(f, rows_y - 1, 1))
        bent = 4.0 * f - (down + up + right + left)
        base_ref[level] = (f - (ETA * LAM) * bent).reshape(rows_x * rows_y, width)


def split_squares(squares, rows):
    high = squares.astype(BF16).astype(F32)
    return jnp.concatenate([high, squares - high, jnp.zeros((rows - 4, 128), F32)], axis=0)


def emit(out_ref, half, proj_ref, gram_ref, squares):
    members = proj_ref.shape[0]
    for j in range(PARTS):
        tb, m, r = j // 4, (j // 2) % members, j % 2
        at = pl.multiple_of((half * 2 + tb) * 128, 128)
        block = proj_ref[m, r * 128 : (r + 1) * 128, pl.ds(at, 128)]
        out_ref[j, 0:PROJ_ROWS, :] = block.astype(BF16)
        at = pl.multiple_of(half * 128, 128)
        block = gram_ref[j * GRAM_ROWS : (j + 1) * GRAM_ROWS, pl.ds(at, 128)]
        out_ref[j, PROJ_ROWS:SUM_ROWS, :] = block.astype(BF16)
        out_ref[j, SUM_ROWS:PART_ROWS, :] = squares


def step_kernel(level, count, first, last, *refs):
    (at_ref, base_ref, own_ref, got_ref, x_ref), refs = refs[:5], refs[5:]
    if not first:
        (proj_in, gram_in, squares_in), refs = refs[:3], refs[3:]
    if last:
        moved_ref, keep_ref, send_ref, proj_ref, gram_ref = refs
    else:
        moved_ref, proj_ref, gram_ref, squares_ref = refs
    grad = own_ref[...].astype(F32) + got_ref[...].astype(F32)
    levels = slice(level, level + count)
    moved = (base_ref[levels].reshape(grad.shape) - ETA * grad).astype(BF16)
    moved_ref[...] = moved
    wide = moved.astype(F32)
    squares = jnp.sum(wide * wide, axis=0, keepdims=True)
    if not first:
        squares = squares + squares_in[...]
    turned = moved.T
    gram = jnp.dot(turned, moved, preferred_element_type=F32)
    gram_ref[...] = gram if first else gram_in[...] + gram
    for e in range(x_ref.shape[0]):
        x = x_ref[e] if level == 0 else x_ref[e, level - 1 : level - 1 + count]
        x = x.reshape(grad.shape[0], -1)
        proj = jnp.dot(turned, x, preferred_element_type=F32)
        proj_ref[e] = proj if first else proj_in[e] + proj
    if last:
        core = core_of(at_ref[0])
        pair = jnp.concatenate([squares[:, 0:128], squares[:, 128:256]], axis=0)
        packed = split_squares(pair, 8).astype(BF16)
        emit(send_ref, 1 - core, proj_ref, gram_ref, packed)
        emit(keep_ref, core, proj_ref, gram_ref, packed)
    else:
        squares_ref[...] = squares


def step_levels(level, count, place, base, own, got, series, carry):
    members, frames = series.shape[0], series.shape[-1]
    rows, width = own.shape
    first, last = carry is None, level + count == base.shape[0]
    args = [place, base, own, got, series]
    if not first:
        args += list(carry)
    sums = [
        jax.ShapeDtypeStruct((members, width, frames), F32),
        jax.ShapeDtypeStruct((width, width), F32),
        jax.ShapeDtypeStruct((1, width), F32),
    ]
    outs = [jax.ShapeDtypeStruct((rows, width), BF16)]
    scratch, aliases = [], {}
    if last:
        outs += [jax.ShapeDtypeStruct((PARTS, PART_ROWS, 128), BF16)] * 2
        scratch = [pltpu.VMEM(s.shape, F32) for s in sums[:2]]
    else:
        outs += sums
        if not first:
            aliases = {5 + i: 1 + i for i in range(3)}
    return pl.pallas_call(
        functools.partial(step_kernel, level, count, first, last),
        in_specs=[SM] + [VM] * (len(args) - 1),
        out_specs=[VM] * len(outs),
        out_shape=outs,
        scratch_shapes=scratch,
        input_output_aliases=aliases,
        compiler_params=PARAMS,
        cost_estimate=pl.CostEstimate(
            flops=2 * rows * width * (width + members * frames),
            bytes_accessed=2 * rows * (4 * width + members * frames),
            transcendentals=0,
        ),
    )(*args)


def whole_squares(part):
    return part[SUM_ROWS : SUM_ROWS + 2, :] + part[SUM_ROWS + 2 : SUM_ROWS + 4, :]


def packed_squares(total):
    return split_squares(whole_squares(total), 8).astype(BF16)


def join_kernel(keep_ref, got_ref, out_ref):
    out_ref[:, 0:SUM_ROWS, :] = (
        keep_ref[:, 0:SUM_ROWS, :].astype(F32) + got_ref[:, 0:SUM_ROWS, :].astype(F32)
    ).astype(BF16)
    tail = keep_ref[0].astype(F32) + got_ref[0].astype(F32)
    packed = packed_squares(tail)
    for j in range(PARTS):
        out_ref[j, SUM_ROWS:PART_ROWS, :] = packed


def plane_kernel(in_ref, out_ref):
    total = in_ref[0].astype(F32)
    for j in range(1, PARTS):
        total = total + in_ref[j].astype(F32)
    out_ref[0:SUM_ROWS, :] = total[0:SUM_ROWS, :].astype(BF16)
    out_ref[SUM_ROWS:PART_ROWS, :] = packed_squares(total)


def add_kernel(own_ref, got_ref, out_ref):
    total = own_ref[...].astype(F32) + got_ref[...].astype(F32)
    out_ref[0:SUM_ROWS, :] = total[0:SUM_ROWS, :].astype(BF16)
    out_ref[SUM_ROWS:PART_ROWS, :] = packed_squares(total)


def reduce_kernel(total_cells, at_ref, *refs):
    *in_refs, out_ref, shrink_ref, column_ref = refs
    core, part = core_of(at_ref[0]), part_of(at_ref[0])
    a, b, c, d = (ref[...].astype(F32) for ref in in_refs)
    total = (a + b) + (c + d)
    squares = whole_squares(total)
    shrink = jnp.maximum(0.0, 1.0 - TAU / jnp.sqrt(squares / total_cells + 1e-06))
    shrink_ref[...] = shrink
    for k in range(2):
        column_ref[k * 128 : (k + 1) * 128, :] = jnp.broadcast_to(shrink[k : k + 1, :], (128, 128)).T
    at = pl.multiple_of(lax.rem(part, 2) * 128, 128)
    proj = column_ref[pl.ds(at, 128), :] * total[0:PROJ_ROWS, :] * (1.0 / math.sqrt(total_cells))
    at = pl.multiple_of(part * GRAM_ROWS, GRAM_ROWS)
    lanes = jnp.where(core == 0, shrink[0:1, :], shrink[1:2, :])
    gram = column_ref[pl.ds(at, GRAM_ROWS), :] * total[PROJ_ROWS:SUM_ROWS, :] * lanes * (1.0 / total_cells)
    mine = jnp.concatenate([proj, gram], axis=0).astype(BF16)
    for j in range(PARTS):
        out_ref[j] = mine


def scale_kernel(shrink_ref, *refs):
    out_ref = refs[-1]
    at = 0
    for m_ref in refs[:-1]:
        rows = slice(at, at + m_ref.shape[0])
        at = rows.stop
        for k in range(2):
            lanes = slice(k * 128, (k + 1) * 128)
            out_ref[rows, lanes] = (m_ref[:, lanes].astype(F32) * shrink_ref[k : k + 1, :]).astype(BF16)


def final_kernel(at_ref, own_ref, got_ref, proj_ref, gram_ref):
    core = core_of(at_ref[0])
    members = proj_ref.shape[0]
    for ref, half in ((own_ref, core), (got_ref, 1 - core)):
        for j in range(PARTS):
            tb, m, r = j // 4, (j // 2) % members, j % 2
            at = pl.multiple_of((half * 2 + tb) * 128, 128)
            proj_ref[m, r * 128 : (r + 1) * 128, pl.ds(at, 128)] = ref[j, 0:PROJ_ROWS, :].astype(F32)
            at = pl.multiple_of(half * 128, 128)
            gram_ref[j * GRAM_ROWS : (j + 1) * GRAM_ROWS, pl.ds(at, 128)] = (
                ref[j, PROJ_ROWS:SUM_ROWS, :].astype(F32)
            )


def both_ways(pairs):
    return [p for i, j in pairs for p in ((i, j), (j, i))]


def local(snapshots, coefficients, modes):
    members, levels, rows_x, rows_y, frames = snapshots.shape
    width = modes.shape[3]
    cells = rows_x * rows_y
    local_cells = levels * cells
    n_sx, n_z = lax.axis_size(SX), lax.axis_size("z")
    total_cells = local_cells * n_sx * n_z
    core = lax.axis_index("c").astype(jnp.int32)
    parity = lax.axis_index("z").astype(jnp.int32) & 1
    part = lax.axis_index(PLANE).astype(jnp.int32)
    place = (core + 2 * parity + 4 * part).reshape(1)
    series = snapshots.reshape(members, levels, cells, frames)
    swap = [(0, 1), (1, 0)]

    chunks = [(0, 1), (1, 2), (3, 1)]
    g, coefficients, head, edge_b = first_grad(place, modes, coefficients, series)
    own, got = [g], [lax.ppermute(g, "ens", swap)]
    xb = lax.ppermute(edge_b, SX, both_ways([(i, i + 1) for i in range(1, n_sx - 1, 2)]))
    g, modes, series, edge_a, row_a, row_b = second_grad(place, modes, coefficients, series, chunks[1][1])
    g, xb = lax.optimization_barrier((g, xb))
    own.append(g)
    got.append(lax.ppermute(g, "ens", swap))
    got[0], edge_a, row_a, row_b = lax.optimization_barrier((got[0], edge_a, row_a, row_b))
    xa = lax.ppermute(edge_a, "c", swap)
    za = lax.ppermute(row_a, "z", both_ways([(i, i + 1) for i in range(0, n_z, 2)]))
    zb = lax.ppermute(row_b, "z", both_ways([(i, i + 1) for i in range(1, n_z - 1, 2)]))
    coefficients, *_ = lax.optimization_barrier((coefficients, xa, za, zb))
    own.append(grad_level(modes, coefficients, series, chunks[2][0]))
    got.append(lax.ppermute(own[2], "ens", swap))
    base = pl.pallas_call(
        base_kernel,
        in_specs=[SM] + [VM] * 5,
        out_specs=VM,
        out_shape=jax.ShapeDtypeStruct((levels, cells, width), F32),
        compiler_params=PARAMS,
        cost_estimate=pl.CostEstimate(flops=12 * local_cells * width, bytes_accessed=6 * local_cells * width, transcendentals=0),
    )(place, modes, xa, xb, za, zb)

    moved, carry = [], None
    for i, (level, count) in enumerate(chunks):
        x = head if level == 0 else series
        m, *carry = step_levels(level, count, place, base, own[i], got[i], x, carry)
        moved.append(m)
    keep, send = carry

    part_shape = jax.ShapeDtypeStruct((PARTS, PART_ROWS, 128), BF16)
    other = lax.ppermute(send, "c", swap)
    joined = pl.pallas_call(
        join_kernel, in_specs=[VM, VM], out_specs=VM, out_shape=part_shape, compiler_params=PARAMS
    )(keep, other)
    parts = lax.all_to_all(joined, PLANE, 0, 0)
    line_shape = jax.ShapeDtypeStruct((PART_ROWS, 128), BF16)
    line = pl.pallas_call(
        plane_kernel, in_specs=[VM], out_specs=VM, out_shape=line_shape, compiler_params=PARAMS
    )(parts)
    near = lax.ppermute(line, "z", [(i, i ^ 1) for i in range(n_z)])
    line = pl.pallas_call(
        add_kernel, in_specs=[VM, VM], out_specs=VM, out_shape=line_shape, compiler_params=PARAMS
    )(line, near)
    others = [lax.ppermute(line, "z", [(i, i ^ k) for i in range(n_z)]) for k in (3, 5, 7)]
    spread, shrink = pl.pallas_call(
        functools.partial(reduce_kernel, total_cells),
        in_specs=[SM] + [VM] * 4,
        out_specs=[VM, VM],
        out_shape=[
            jax.ShapeDtypeStruct((PARTS, SUM_ROWS, 128), BF16),
            jax.ShapeDtypeStruct((2, 128), F32),
        ],
        scratch_shapes=[pltpu.VMEM((width, 128), F32)],
        compiler_params=PARAMS,
    )(place, line, *others)
    half = lax.all_to_all(spread, PLANE, 0, 0)
    new_modes = pl.pallas_call(
        scale_kernel,
        in_specs=[VM] * (1 + len(moved)),
        out_specs=VM,
        out_shape=jax.ShapeDtypeStruct((local_cells, width), BF16),
        compiler_params=PARAMS,
    )(shrink, *moved)
    half, new_modes = lax.optimization_barrier((half, new_modes))
    other_half = lax.ppermute(half, "c", swap)
    projected, gram = pl.pallas_call(
        final_kernel,
        in_specs=[SM, VM, VM],
        out_specs=[VM, VM],
        out_shape=[
            jax.ShapeDtypeStruct((members, width, frames), F32),
            jax.ShapeDtypeStruct((width, width), F32),
        ],
        compiler_params=PARAMS,
    )(place, half, other_half)
    return (new_modes.reshape(levels, rows_x, rows_y, width), gram, projected)


def solution(mesh):
    ens, n_sx, n_sy = (mesh.shape[a] for a in ("ens", "sx", "sy"))
    fine = Mesh(mesh.devices.reshape(ens, 2, n_sx // 4, 2, n_sy), ("ens", "xh", "y", "c", "z"))
    in_specs = (P("ens", None, SX, "z", None), P("ens", None, None), P(None, SX, "z", None))
    out_specs = (P(None, SX, "z", None), P(), P("ens", None, None))
    return jax.shard_map(local, mesh=fine, in_specs=in_specs, out_specs=out_specs, check_vma=False)
```

```python
import functools
import math

import jax
import jax.numpy as jnp
from jax import lax
from jax.experimental import pallas as pl
from jax.experimental.pallas import tpu as pltpu
from jax.sharding import Mesh, PartitionSpec as P

ETA = 0.25
LAM = 0.5
TAU = 0.4

F32 = jnp.float32
BF16 = jnp.bfloat16
VMEM_LIMIT = 40 * 1024 * 1024
PARAMS = pltpu.CompilerParams(vmem_limit_bytes=VMEM_LIMIT)

SX = ("xh", "y", "c")
SY = ("zh", "zl")
GROUP = ("xh", "y", "zl")
PARTS = 16
PROJ_ROWS = 64
GRAM_ROWS = 16
SUM_ROWS = PROJ_ROWS + GRAM_ROWS
PART_ROWS = SUM_ROWS + 8

VM = pl.BlockSpec(memory_space=pltpu.VMEM)
SM = pl.BlockSpec(memory_space=pltpu.SMEM)
HBM = pl.BlockSpec(memory_space=pltpu.HBM)


def core_of(place):
    return place & 1


def parity_of(place):
    return (place >> 1) & 1


def part_of(place):
    return place >> 2


def gradient(m, coefficients, series):
    acc = None
    for e in range(len(coefficients)):
        c = coefficients[e]()
        fitted = jnp.dot(m, c, preferred_element_type=F32)
        misfit = (fitted - series[e]().astype(F32)).astype(BF16)
        term = lax.dot_general(misfit, c, (((1,), (1,)), ((), ())), preferred_element_type=F32)
        acc = term if acc is None else acc + term
    return acc.astype(BF16)


def start_all(copies, sems):
    copies = [pltpu.make_async_copy(s, d, sems.at[i]) for i, (s, d) in enumerate(copies)]
    for copy in copies:
        copy.start()
    return copies


def after(copy, ref, *at):
    def load():
        copy.wait()
        return ref[at].reshape(-1, ref.shape[-1])

    return load


def first_grad_kernel(at_ref, m_hbm, c_hbm, x_hbm, g_ref, c_ref, x_ref, xb_ref, m_ref, sems):
    members = c_hbm.shape[0]
    last = m_hbm.shape[1] - 1
    copies = [(m_hbm.at[0], m_ref)]
    for e in range(members):
        copies.append((c_hbm.at[e], c_ref.at[e]))
        copies.append((x_hbm.at[e, 0], x_ref.at[e]))
    copies.append((m_hbm.at[:, last * core_of(at_ref[0])], xb_ref))
    copies = start_all(copies, sems)
    copies[0].wait()
    g_ref[...] = gradient(
        m_ref[...].reshape(g_ref.shape),
        [after(copies[1 + 2 * e], c_ref, e) for e in range(members)],
        [after(copies[2 + 2 * e], x_ref, e) for e in range(members)],
    )
    copies[-1].wait()


def second_grad_kernel(at_ref, m_hbm, c_ref, x_hbm, *refs):
    *g_refs, m_ref, x_ref, xa_ref, za_ref, zb_ref, tmp_ref, sems = refs
    members, levels, cells, _ = x_hbm.shape
    _, rows_x, rows_y, width = m_ref.shape
    copies = [(m_hbm, m_ref)]
    for level in range(1, levels):
        for e in range(members):
            copies.append((x_hbm.at[e, level], x_ref.at[e, level - 1]))
    copies = start_all(copies, sems)
    copies[0].wait()
    core, even = core_of(at_ref[0]), parity_of(at_ref[0]) == 0
    xa_ref[...] = m_ref[:, (rows_x - 1) * (1 - core)]
    tmp_ref[0] = m_ref[:, :, 0:8, :].reshape(levels * rows_x, 8, width).astype(F32)
    tmp_ref[1] = m_ref[:, :, rows_y - 8 : rows_y, :].reshape(levels * rows_x, 8, width).astype(F32)
    lo, hi = tmp_ref[0, :, 0, :], tmp_ref[1, :, 7, :]
    za_ref[...] = jnp.where(even, hi, lo).astype(BF16)
    zb_ref[...] = jnp.where(even, lo, hi).astype(BF16)
    at = 0
    for g_ref in g_refs:
        for first in range(0, g_ref.shape[0], cells):
            g_ref[first : first + cells, :] = gradient(
                m_ref[1 + at].reshape(cells, width),
                [functools.partial(c_ref.__getitem__, e) for e in range(members)],
                [after(copies[1 + at * members + e], x_ref, e, at) for e in range(members)],
            )
            at += 1


def grad_cost(members, cells, frames, width):
    return pl.CostEstimate(
        flops=4 * members * cells * frames * width,
        bytes_accessed=2 * cells * (2 * width + members * frames) + 2 * members * width * frames,
        transcendentals=0,
    )


def in_hbm(array):
    return pltpu.with_memory_space_constraint(array, pltpu.HBM)


def first_grad(place, modes, coefficients, series):
    members, _, cells, frames = series.shape
    levels, rows_x, rows_y, width = modes.shape
    outs = [
        jax.ShapeDtypeStruct((cells, width), BF16),
        pltpu.VMEM(coefficients.shape, BF16),
        pltpu.VMEM((members, cells, frames), BF16),
        jax.ShapeDtypeStruct((levels, rows_y, width), BF16),
    ]
    return pl.pallas_call(
        first_grad_kernel,
        in_specs=[SM] + [HBM] * 3,
        out_specs=[VM] * len(outs),
        out_shape=outs,
        scratch_shapes=[
            pltpu.VMEM((rows_x, rows_y, width), BF16),
            pltpu.SemaphoreType.DMA((2 + 2 * members,)),
        ],
        compiler_params=PARAMS,
        cost_estimate=grad_cost(members, cells, frames, width),
    )(place, in_hbm(modes), in_hbm(coefficients), in_hbm(series))


def second_grad(place, modes, coefficients, series, counts):
    members, levels, cells, frames = series.shape
    _, rows_x, rows_y, width = modes.shape
    outs = [jax.ShapeDtypeStruct((count * cells, width), BF16) for count in counts]
    outs += [
        pltpu.VMEM(modes.shape, BF16),
        pltpu.VMEM((members, levels - 1, cells, frames), BF16),
        jax.ShapeDtypeStruct((levels, rows_y, width), BF16),
        jax.ShapeDtypeStruct((levels * rows_x, width), BF16),
        jax.ShapeDtypeStruct((levels * rows_x, width), BF16),
    ]
    return pl.pallas_call(
        second_grad_kernel,
        in_specs=[SM, HBM, VM, HBM],
        out_specs=[VM] * len(outs),
        out_shape=outs,
        scratch_shapes=[
            pltpu.VMEM((2, levels * rows_x, 8, width), F32),
            pltpu.SemaphoreType.DMA((1 + members * (levels - 1),)),
        ],
        compiler_params=PARAMS,
        cost_estimate=grad_cost(members, sum(counts) * cells, frames, width),
    )(place, in_hbm(modes), coefficients, in_hbm(series))


def base_kernel(at_ref, m_ref, xa_ref, xb_ref, za_ref, zb_ref, base_ref):
    levels, rows_x, rows_y, width = m_ref.shape
    lower, even = core_of(at_ref[0]) == 0, parity_of(at_ref[0]) == 0
    shape = (rows_x, rows_y, width)
    at = lax.broadcasted_iota(jnp.int32, shape, 1)
    for level in range(levels):
        f = m_ref[level].astype(F32)
        xa, xb = xa_ref[level : level + 1].astype(F32), xb_ref[level : level + 1].astype(F32)
        rows = slice(level * rows_x, (level + 1) * rows_x)
        za, zb = za_ref[rows, :].astype(F32), zb_ref[rows, :].astype(F32)
        up = jnp.concatenate([jnp.where(lower, xb, xa), f[:-1]], axis=0)
        down = jnp.concatenate([f[1:], jnp.where(lower, xa, xb)], axis=0)
        zlo = jnp.broadcast_to(jnp.where(even, zb, za)[:, None, :], shape)
        zhi = jnp.broadcast_to(jnp.where(even, za, zb)[:, None, :], shape)
        left = jnp.where(at == 0, zlo, pltpu.roll(f, 1, 1))
        right = jnp.where(at == rows_y - 1, zhi, pltpu.roll(f, rows_y - 1, 1))
        bent = 4.0 * f - (down + up + right + left)
        base_ref[level] = (f - (ETA * LAM) * bent).reshape(rows_x * rows_y, width)


def split_squares(squares, rows):
    high = squares.astype(BF16).astype(F32)
    return jnp.concatenate([high, squares - high, jnp.zeros((rows - 4, 128), F32)], axis=0)


def emit(out_ref, half, proj_ref, gram_ref, squares):
    members = proj_ref.shape[0]
    for j in range(PARTS):
        tb, m, r = j // 8, (j // 4) % members, j % 4
        at = pl.multiple_of((half * 2 + tb) * 128, 128)
        block = proj_ref[m, r * PROJ_ROWS : (r + 1) * PROJ_ROWS, pl.ds(at, 128)]
        out_ref[j, 0:PROJ_ROWS, :] = block.astype(BF16)
        at = pl.multiple_of(half * 128, 128)
        block = gram_ref[j * GRAM_ROWS : (j + 1) * GRAM_ROWS, pl.ds(at, 128)]
        out_ref[j, PROJ_ROWS:SUM_ROWS, :] = block.astype(BF16)
        out_ref[j, SUM_ROWS:PART_ROWS, :] = squares


def step_kernel(level, count, first, last, *refs):
    (at_ref, base_ref, own_ref, got_ref, x_ref), refs = refs[:5], refs[5:]
    if not first:
        (proj_in, gram_in, squares_in), refs = refs[:3], refs[3:]
    if last:
        moved_ref, keep_ref, send_ref, proj_ref, gram_ref = refs
    else:
        moved_ref, proj_ref, gram_ref, squares_ref = refs
    grad = own_ref[...].astype(F32) + got_ref[...].astype(F32)
    levels = slice(level, level + count)
    moved = (base_ref[levels].reshape(grad.shape) - ETA * grad).astype(BF16)
    moved_ref[...] = moved
    wide = moved.astype(F32)
    squares = jnp.sum(wide * wide, axis=0, keepdims=True)
    if not first:
        squares = squares + squares_in[...]
    turned = moved.T
    gram = jnp.dot(turned, moved, preferred_element_type=F32)
    gram_ref[...] = gram if first else gram_in[...] + gram
    for e in range(x_ref.shape[0]):
        x = x_ref[e] if level == 0 else x_ref[e, level - 1 : level - 1 + count]
        x = x.reshape(grad.shape[0], -1)
        proj = jnp.dot(turned, x, preferred_element_type=F32)
        proj_ref[e] = proj if first else proj_in[e] + proj
    if last:
        core = core_of(at_ref[0])
        pair = jnp.concatenate([squares[:, 0:128], squares[:, 128:256]], axis=0)
        packed = split_squares(pair, 8).astype(BF16)
        emit(send_ref, 1 - core, proj_ref, gram_ref, packed)
        emit(keep_ref, core, proj_ref, gram_ref, packed)
    else:
        squares_ref[...] = squares


def step_levels(level, count, place, base, own, got, series, carry):
    members, frames = series.shape[0], series.shape[-1]
    rows, width = own.shape
    first, last = carry is None, level + count == base.shape[0]
    args = [place, base, own, got, series]
    if not first:
        args += list(carry)
    sums = [
        jax.ShapeDtypeStruct((members, width, frames), F32),
        jax.ShapeDtypeStruct((width, width), F32),
        jax.ShapeDtypeStruct((1, width), F32),
    ]
    outs = [jax.ShapeDtypeStruct((rows, width), BF16)]
    scratch, aliases = [], {}
    if last:
        outs += [jax.ShapeDtypeStruct((PARTS, PART_ROWS, 128), BF16)] * 2
        scratch = [pltpu.VMEM(s.shape, F32) for s in sums[:2]]
    else:
        outs += sums
        if not first:
            aliases = {5 + i: 1 + i for i in range(3)}
    return pl.pallas_call(
        functools.partial(step_kernel, level, count, first, last),
        in_specs=[SM] + [VM] * (len(args) - 1),
        out_specs=[VM] * len(outs),
        out_shape=outs,
        scratch_shapes=scratch,
        input_output_aliases=aliases,
        compiler_params=PARAMS,
        cost_estimate=pl.CostEstimate(
            flops=2 * rows * width * (width + members * frames),
            bytes_accessed=2 * rows * (4 * width + members * frames),
            transcendentals=0,
        ),
    )(*args)


def whole_squares(part):
    return part[SUM_ROWS : SUM_ROWS + 2, :] + part[SUM_ROWS + 2 : SUM_ROWS + 4, :]


def packed_squares(total):
    return split_squares(whole_squares(total), 8).astype(BF16)


def join_kernel(keep_ref, got_ref, out_ref):
    out_ref[:, 0:SUM_ROWS, :] = (
        keep_ref[:, 0:SUM_ROWS, :].astype(F32) + got_ref[:, 0:SUM_ROWS, :].astype(F32)
    ).astype(BF16)
    tail = keep_ref[0].astype(F32) + got_ref[0].astype(F32)
    packed = packed_squares(tail)
    for j in range(PARTS):
        out_ref[j, SUM_ROWS:PART_ROWS, :] = packed


def group_kernel(in_ref, out_ref):
    total = in_ref[0].astype(F32)
    for j in range(1, PARTS):
        total = total + in_ref[j].astype(F32)
    out_ref[0:SUM_ROWS, :] = total[0:SUM_ROWS, :].astype(BF16)
    out_ref[SUM_ROWS:PART_ROWS, :] = packed_squares(total)


def reduce_kernel(total_cells, at_ref, *refs):
    *in_refs, out_ref, shrink_ref, column_ref = refs
    core, part = core_of(at_ref[0]), part_of(at_ref[0])
    a, b, c, d = (ref[...].astype(F32) for ref in in_refs)
    total = (a + b) + (c + d)
    squares = whole_squares(total)
    shrink = jnp.maximum(0.0, 1.0 - TAU / jnp.sqrt(squares / total_cells + 1e-06))
    shrink_ref[...] = shrink
    for k in range(2):
        column_ref[k * 128 : (k + 1) * 128, :] = jnp.broadcast_to(shrink[k : k + 1, :], (128, 128)).T
    at = pl.multiple_of((part & 3) * PROJ_ROWS, PROJ_ROWS)
    proj = column_ref[pl.ds(at, PROJ_ROWS), :] * total[0:PROJ_ROWS, :] * (1.0 / math.sqrt(total_cells))
    at = pl.multiple_of(part * GRAM_ROWS, GRAM_ROWS)
    lanes = jnp.where(core == 0, shrink[0:1, :], shrink[1:2, :])
    gram = column_ref[pl.ds(at, GRAM_ROWS), :] * total[PROJ_ROWS:SUM_ROWS, :] * lanes * (1.0 / total_cells)
    mine = jnp.concatenate([proj, gram], axis=0).astype(BF16)
    for j in range(PARTS):
        out_ref[j] = mine


def scale_kernel(shrink_ref, *refs):
    out_ref = refs[-1]
    at = 0
    for m_ref in refs[:-1]:
        rows = slice(at, at + m_ref.shape[0])
        at = rows.stop
        for k in range(2):
            lanes = slice(k * 128, (k + 1) * 128)
            out_ref[rows, lanes] = (m_ref[:, lanes].astype(F32) * shrink_ref[k : k + 1, :]).astype(BF16)


def final_kernel(at_ref, own_ref, got_ref, proj_ref, gram_ref):
    core = core_of(at_ref[0])
    members = proj_ref.shape[0]
    for ref, half in ((own_ref, core), (got_ref, 1 - core)):
        for j in range(PARTS):
            tb, m, r = j // 8, (j // 4) % members, j % 4
            at = pl.multiple_of((half * 2 + tb) * 128, 128)
            rows = slice(r * PROJ_ROWS, (r + 1) * PROJ_ROWS)
            proj_ref[m, rows, pl.ds(at, 128)] = ref[j, 0:PROJ_ROWS, :].astype(F32)
            at = pl.multiple_of(half * 128, 128)
            gram_ref[j * GRAM_ROWS : (j + 1) * GRAM_ROWS, pl.ds(at, 128)] = (
                ref[j, PROJ_ROWS:SUM_ROWS, :].astype(F32)
            )


def both_ways(pairs):
    return [p for i, j in pairs for p in ((i, j), (j, i))]


def local(snapshots, coefficients, modes):
    members, levels, rows_x, rows_y, frames = snapshots.shape
    width = modes.shape[3]
    cells = rows_x * rows_y
    local_cells = levels * cells
    n_sx, n_z = lax.axis_size(SX), lax.axis_size(SY)
    total_cells = local_cells * n_sx * n_z
    core = lax.axis_index("c").astype(jnp.int32)
    parity = lax.axis_index("zl").astype(jnp.int32)
    part = lax.axis_index(GROUP).astype(jnp.int32)
    place = (core + 2 * parity + 4 * part).reshape(1)
    series = snapshots.reshape(members, levels, cells, frames)
    swap = [(0, 1), (1, 0)]

    chunks = [(0, 1), (1, 2), (3, 1)]
    g, coefficients, head, edge_b = first_grad(place, modes, coefficients, series)
    own, got = [g], [lax.ppermute(g, "ens", swap)]
    xb = lax.ppermute(edge_b, SX, both_ways([(i, i + 1) for i in range(1, n_sx - 1, 2)]))
    counts = [count for _, count in chunks[1:]]
    mid, tail, modes, series, edge_a, row_a, row_b = second_grad(
        place, modes, coefficients, series, counts
    )
    mid, xb = lax.optimization_barrier((mid, xb))
    got.append(lax.ppermute(mid, "ens", swap))
    got[0], edge_a, row_a, row_b = lax.optimization_barrier((got[0], edge_a, row_a, row_b))
    own += [mid, tail]
    xa = lax.ppermute(edge_a, "c", swap)
    za = lax.ppermute(row_a, SY, both_ways([(i, i + 1) for i in range(0, n_z, 2)]))
    zb = lax.ppermute(row_b, SY, both_ways([(i, i + 1) for i in range(1, n_z - 1, 2)]))
    tail, xa, za, zb = lax.optimization_barrier((tail, xa, za, zb))
    got.append(lax.ppermute(tail, "ens", swap))
    base = pl.pallas_call(
        base_kernel,
        in_specs=[SM] + [VM] * 5,
        out_specs=VM,
        out_shape=jax.ShapeDtypeStruct((levels, cells, width), F32),
        compiler_params=PARAMS,
        cost_estimate=pl.CostEstimate(flops=12 * local_cells * width, bytes_accessed=6 * local_cells * width, transcendentals=0),
    )(place, modes, xa, xb, za, zb)

    moved, carry = [], None
    for i, (level, count) in enumerate(chunks):
        x = head if level == 0 else series
        m, *carry = step_levels(level, count, place, base, own[i], got[i], x, carry)
        moved.append(m)
    keep, send = carry

    part_shape = jax.ShapeDtypeStruct((PARTS, PART_ROWS, 128), BF16)
    other = lax.ppermute(send, "c", swap)
    joined = pl.pallas_call(
        join_kernel, in_specs=[VM, VM], out_specs=VM, out_shape=part_shape, compiler_params=PARAMS
    )(keep, other)
    parts = lax.all_to_all(joined, GROUP, 0, 0)
    line_shape = jax.ShapeDtypeStruct((PART_ROWS, 128), BF16)
    line = pl.pallas_call(
        group_kernel, in_specs=[VM], out_specs=VM, out_shape=line_shape, compiler_params=PARAMS
    )(parts)
    pairs = lax.axis_size("zh")
    others = [lax.ppermute(line, "zh", [(i, i ^ k) for i in range(pairs)]) for k in (1, 2, 3)]
    spread, shrink = pl.pallas_call(
        functools.partial(reduce_kernel, total_cells),
        in_specs=[SM] + [VM] * 4,
        out_specs=[VM, VM],
        out_shape=[
            jax.ShapeDtypeStruct((PARTS, SUM_ROWS, 128), BF16),
            jax.ShapeDtypeStruct((2, 128), F32),
        ],
        scratch_shapes=[pltpu.VMEM((width, 128), F32)],
        compiler_params=PARAMS,
    )(place, line, *others)
    half = lax.all_to_all(spread, GROUP, 0, 0)
    new_modes = pl.pallas_call(
        scale_kernel,
        in_specs=[VM] * (1 + len(moved)),
        out_specs=VM,
        out_shape=jax.ShapeDtypeStruct((local_cells, width), BF16),
        compiler_params=PARAMS,
    )(shrink, *moved)
    half, new_modes = lax.optimization_barrier((half, new_modes))
    other_half = lax.ppermute(half, "c", swap)
    projected, gram = pl.pallas_call(
        final_kernel,
        in_specs=[SM, VM, VM],
        out_specs=[VM, VM],
        out_shape=[
            jax.ShapeDtypeStruct((members, width, frames), F32),
            jax.ShapeDtypeStruct((width, width), F32),
        ],
        compiler_params=PARAMS,
    )(place, half, other_half)
    return (new_modes.reshape(levels, rows_x, rows_y, width), gram, projected)


def solution(mesh):
    ens, n_sx, n_sy = (mesh.shape[a] for a in ("ens", "sx", "sy"))
    fine = Mesh(mesh.devices.reshape(ens, 2, n_sx // 4, 2, n_sy // 2, 2), ("ens", *SX, *SY))
    in_specs = (P("ens", None, SX, SY, None), P("ens", None, None), P(None, SX, SY, None))
    out_specs = (P(None, SX, SY, None), P(), P("ens", None, None))
    return jax.shard_map(local, mesh=fine, in_specs=in_specs, out_specs=out_specs, check_vma=False)
```

```python
import functools
import math

import jax
import jax.numpy as jnp
from jax import lax
from jax.experimental import pallas as pl
from jax.experimental.pallas import tpu as pltpu
from jax.sharding import Mesh, PartitionSpec as P

ETA = 0.25
LAM = 0.5
TAU = 0.4

F32 = jnp.float32
BF16 = jnp.bfloat16
VMEM_LIMIT = 40 * 1024 * 1024
PARAMS = pltpu.CompilerParams(vmem_limit_bytes=VMEM_LIMIT)

SX = ("xh", "y", "c")
SY = ("zh", "zl")
GROUP = ("xh", "y", "zl")
PARTS = 16
PROJ_ROWS = 64
GRAM_ROWS = 16
SUM_ROWS = PROJ_ROWS + GRAM_ROWS
PART_ROWS = SUM_ROWS + 8

VM = pl.BlockSpec(memory_space=pltpu.VMEM)
SM = pl.BlockSpec(memory_space=pltpu.SMEM)
HBM = pl.BlockSpec(memory_space=pltpu.HBM)


def core_of(place):
    return place & 1


def parity_of(place):
    return (place >> 1) & 1


def part_of(place):
    return place >> 2


def gradient(m, coefficients, series):
    acc = None
    for e in range(len(coefficients)):
        c = coefficients[e]()
        fitted = jnp.dot(m, c, preferred_element_type=F32)
        misfit = (fitted - series[e]().astype(F32)).astype(BF16)
        term = lax.dot_general(misfit, c, (((1,), (1,)), ((), ())), preferred_element_type=F32)
        acc = term if acc is None else acc + term
    return acc.astype(BF16)


def start_all(copies, sems):
    copies = [pltpu.make_async_copy(s, d, sems.at[i]) for i, (s, d) in enumerate(copies)]
    for copy in copies:
        copy.start()
    return copies


def after(copy, ref, *at):
    def load():
        copy.wait()
        return ref[at].reshape(-1, ref.shape[-1])

    return load


def first_grad_kernel(at_ref, m_hbm, c_hbm, x_hbm, g_ref, c_ref, x_ref, xb_ref, m_ref, sems):
    members = c_hbm.shape[0]
    last = m_hbm.shape[1] - 1
    copies = [(m_hbm.at[0], m_ref)]
    for e in range(members):
        copies.append((c_hbm.at[e], c_ref.at[e]))
        copies.append((x_hbm.at[e, 0], x_ref.at[e]))
    copies.append((m_hbm.at[:, last * core_of(at_ref[0])], xb_ref))
    copies = start_all(copies, sems)
    copies[0].wait()
    g_ref[...] = gradient(
        m_ref[...].reshape(g_ref.shape),
        [after(copies[1 + 2 * e], c_ref, e) for e in range(members)],
        [after(copies[2 + 2 * e], x_ref, e) for e in range(members)],
    )
    copies[-1].wait()


def second_grad_kernel(level, m_hbm, c_ref, x_hbm, g_ref, x_ref, m_ref, sems):
    members = c_ref.shape[0]
    copies = [(m_hbm.at[level], m_ref)]
    for e in range(members):
        copies.append((x_hbm.at[e, level], x_ref.at[e]))
    copies = start_all(copies, sems)
    copies[0].wait()
    g_ref[...] = gradient(
        m_ref[...].reshape(g_ref.shape),
        [functools.partial(c_ref.__getitem__, e) for e in range(members)],
        [after(copies[1 + e], x_ref, e) for e in range(members)],
    )


def rest_grad_kernel(begin, at_ref, m_hbm, c_ref, x_hbm, *refs):
    *g_refs, m_ref, x_ref, xa_ref, za_ref, zb_ref, tmp_ref, sems = refs
    members, levels, cells, _ = x_hbm.shape
    _, rows_x, rows_y, width = m_ref.shape
    copies = [(m_hbm, m_ref)]
    for level in range(begin, levels):
        for e in range(members):
            copies.append((x_hbm.at[e, level], x_ref.at[e, level - begin]))
    copies = start_all(copies, sems)
    copies[0].wait()
    core, even = core_of(at_ref[0]), parity_of(at_ref[0]) == 0
    xa_ref[...] = m_ref[:, (rows_x - 1) * (1 - core)]
    tmp_ref[0] = m_ref[:, :, 0:8, :].reshape(levels * rows_x, 8, width).astype(F32)
    tmp_ref[1] = m_ref[:, :, rows_y - 8 : rows_y, :].reshape(levels * rows_x, 8, width).astype(F32)
    lo, hi = tmp_ref[0, :, 0, :], tmp_ref[1, :, 7, :]
    za_ref[...] = jnp.where(even, hi, lo).astype(BF16)
    zb_ref[...] = jnp.where(even, lo, hi).astype(BF16)
    for i, g_ref in enumerate(g_refs):
        g_ref[...] = gradient(
            m_ref[begin + i].reshape(g_ref.shape),
            [functools.partial(c_ref.__getitem__, e) for e in range(members)],
            [after(copies[1 + i * members + e], x_ref, e, i) for e in range(members)],
        )


def grad_cost(members, cells, frames, width):
    return pl.CostEstimate(
        flops=4 * members * cells * frames * width,
        bytes_accessed=2 * cells * (2 * width + members * frames) + 2 * members * width * frames,
        transcendentals=0,
    )


def in_hbm(array):
    return pltpu.with_memory_space_constraint(array, pltpu.HBM)


def first_grad(place, modes, coefficients, series):
    members, _, cells, frames = series.shape
    levels, rows_x, rows_y, width = modes.shape
    outs = [
        jax.ShapeDtypeStruct((cells, width), BF16),
        pltpu.VMEM(coefficients.shape, BF16),
        pltpu.VMEM((members, cells, frames), BF16),
        jax.ShapeDtypeStruct((levels, rows_y, width), BF16),
    ]
    return pl.pallas_call(
        first_grad_kernel,
        in_specs=[SM] + [HBM] * 3,
        out_specs=[VM] * len(outs),
        out_shape=outs,
        scratch_shapes=[
            pltpu.VMEM((rows_x, rows_y, width), BF16),
            pltpu.SemaphoreType.DMA((2 + 2 * members,)),
        ],
        compiler_params=PARAMS,
        cost_estimate=grad_cost(members, cells, frames, width),
    )(place, in_hbm(modes), in_hbm(coefficients), in_hbm(series))


def second_grad(modes, coefficients, series, level):
    members, _, cells, frames = series.shape
    _, rows_x, rows_y, width = modes.shape
    outs = [jax.ShapeDtypeStruct((cells, width), BF16), pltpu.VMEM((members, cells, frames), BF16)]
    return pl.pallas_call(
        functools.partial(second_grad_kernel, level),
        in_specs=[HBM, VM, HBM],
        out_specs=[VM] * len(outs),
        out_shape=outs,
        scratch_shapes=[
            pltpu.VMEM((rows_x, rows_y, width), BF16),
            pltpu.SemaphoreType.DMA((1 + members,)),
        ],
        compiler_params=PARAMS,
        cost_estimate=grad_cost(members, cells, frames, width),
    )(in_hbm(modes), coefficients, in_hbm(series))


def rest_grad(place, modes, coefficients, series, begin):
    members, levels, cells, frames = series.shape
    _, rows_x, rows_y, width = modes.shape
    count = levels - begin
    outs = [jax.ShapeDtypeStruct((cells, width), BF16)] * count
    outs += [
        pltpu.VMEM(modes.shape, BF16),
        pltpu.VMEM((members, count, cells, frames), BF16),
        jax.ShapeDtypeStruct((levels, rows_y, width), BF16),
        jax.ShapeDtypeStruct((levels * rows_x, width), BF16),
        jax.ShapeDtypeStruct((levels * rows_x, width), BF16),
    ]
    return pl.pallas_call(
        functools.partial(rest_grad_kernel, begin),
        in_specs=[SM, HBM, VM, HBM],
        out_specs=[VM] * len(outs),
        out_shape=outs,
        scratch_shapes=[
            pltpu.VMEM((2, levels * rows_x, 8, width), F32),
            pltpu.SemaphoreType.DMA((1 + members * count,)),
        ],
        compiler_params=PARAMS,
        cost_estimate=grad_cost(members, count * cells, frames, width),
    )(place, in_hbm(modes), coefficients, in_hbm(series))


def base_kernel(at_ref, m_ref, xa_ref, xb_ref, za_ref, zb_ref, base_ref):
    levels, rows_x, rows_y, width = m_ref.shape
    lower, even = core_of(at_ref[0]) == 0, parity_of(at_ref[0]) == 0
    shape = (rows_x, rows_y, width)
    at = lax.broadcasted_iota(jnp.int32, shape, 1)
    for level in range(levels):
        f = m_ref[level].astype(F32)
        xa, xb = xa_ref[level : level + 1].astype(F32), xb_ref[level : level + 1].astype(F32)
        rows = slice(level * rows_x, (level + 1) * rows_x)
        za, zb = za_ref[rows, :].astype(F32), zb_ref[rows, :].astype(F32)
        up = jnp.concatenate([jnp.where(lower, xb, xa), f[:-1]], axis=0)
        down = jnp.concatenate([f[1:], jnp.where(lower, xa, xb)], axis=0)
        zlo = jnp.broadcast_to(jnp.where(even, zb, za)[:, None, :], shape)
        zhi = jnp.broadcast_to(jnp.where(even, za, zb)[:, None, :], shape)
        left = jnp.where(at == 0, zlo, pltpu.roll(f, 1, 1))
        right = jnp.where(at == rows_y - 1, zhi, pltpu.roll(f, rows_y - 1, 1))
        bent = 4.0 * f - (down + up + right + left)
        base_ref[level] = (f - (ETA * LAM) * bent).reshape(rows_x * rows_y, width)


def split_squares(squares, rows):
    high = squares.astype(BF16).astype(F32)
    return jnp.concatenate([high, squares - high, jnp.zeros((rows - 4, 128), F32)], axis=0)


def emit(out_ref, half, proj_ref, gram_ref, squares):
    members = proj_ref.shape[0]
    for j in range(PARTS):
        tb, m, r = j // 8, (j // 4) % members, j % 4
        at = pl.multiple_of((half * 2 + tb) * 128, 128)
        block = proj_ref[m, r * PROJ_ROWS : (r + 1) * PROJ_ROWS, pl.ds(at, 128)]
        out_ref[j, 0:PROJ_ROWS, :] = block.astype(BF16)
        at = pl.multiple_of(half * 128, 128)
        block = gram_ref[j * GRAM_ROWS : (j + 1) * GRAM_ROWS, pl.ds(at, 128)]
        out_ref[j, PROJ_ROWS:SUM_ROWS, :] = block.astype(BF16)
        out_ref[j, SUM_ROWS:PART_ROWS, :] = squares


def step_kernel(level, x_at, first, last, *refs):
    (at_ref, base_ref, own_ref, got_ref, x_ref), refs = refs[:5], refs[5:]
    if not first:
        (proj_in, gram_in, squares_in), refs = refs[:3], refs[3:]
    if last:
        moved_ref, keep_ref, send_ref, proj_ref, gram_ref = refs
    else:
        moved_ref, proj_ref, gram_ref, squares_ref = refs
    grad = own_ref[...].astype(F32) + got_ref[...].astype(F32)
    moved = (base_ref[level] - ETA * grad).astype(BF16)
    moved_ref[...] = moved
    wide = moved.astype(F32)
    squares = jnp.sum(wide * wide, axis=0, keepdims=True)
    if not first:
        squares = squares + squares_in[...]
    turned = moved.T
    gram = jnp.dot(turned, moved, preferred_element_type=F32)
    gram_ref[...] = gram if first else gram_in[...] + gram
    for e in range(x_ref.shape[0]):
        x = x_ref[e] if x_at is None else x_ref[e, x_at]
        proj = jnp.dot(turned, x, preferred_element_type=F32)
        proj_ref[e] = proj if first else proj_in[e] + proj
    if last:
        core = core_of(at_ref[0])
        pair = jnp.concatenate([squares[:, 0:128], squares[:, 128:256]], axis=0)
        packed = split_squares(pair, 8).astype(BF16)
        emit(send_ref, 1 - core, proj_ref, gram_ref, packed)
        emit(keep_ref, core, proj_ref, gram_ref, packed)
    else:
        squares_ref[...] = squares


def step_level(level, x_at, place, base, own, got, series, carry):
    members, frames = series.shape[0], series.shape[-1]
    rows, width = own.shape
    first, last = carry is None, level == base.shape[0] - 1
    args = [place, base, own, got, series]
    if not first:
        args += list(carry)
    sums = [
        jax.ShapeDtypeStruct((members, width, frames), F32),
        jax.ShapeDtypeStruct((width, width), F32),
        jax.ShapeDtypeStruct((1, width), F32),
    ]
    outs = [jax.ShapeDtypeStruct((rows, width), BF16)]
    scratch, aliases = [], {}
    if last:
        outs += [jax.ShapeDtypeStruct((PARTS, PART_ROWS, 128), BF16)] * 2
        scratch = [pltpu.VMEM(s.shape, F32) for s in sums[:2]]
    else:
        outs += sums
        if not first:
            aliases = {5 + i: 1 + i for i in range(3)}
    return pl.pallas_call(
        functools.partial(step_kernel, level, x_at, first, last),
        in_specs=[SM] + [VM] * (len(args) - 1),
        out_specs=[VM] * len(outs),
        out_shape=outs,
        scratch_shapes=scratch,
        input_output_aliases=aliases,
        compiler_params=PARAMS,
        cost_estimate=pl.CostEstimate(
            flops=2 * rows * width * (width + members * frames),
            bytes_accessed=2 * rows * (4 * width + members * frames),
            transcendentals=0,
        ),
    )(*args)


def whole_squares(part):
    return part[SUM_ROWS : SUM_ROWS + 2, :] + part[SUM_ROWS + 2 : SUM_ROWS + 4, :]


def packed_squares(total):
    return split_squares(whole_squares(total), 8).astype(BF16)


def join_kernel(keep_ref, got_ref, out_ref):
    out_ref[:, 0:SUM_ROWS, :] = (
        keep_ref[:, 0:SUM_ROWS, :].astype(F32) + got_ref[:, 0:SUM_ROWS, :].astype(F32)
    ).astype(BF16)
    tail = keep_ref[0].astype(F32) + got_ref[0].astype(F32)
    packed = packed_squares(tail)
    for j in range(PARTS):
        out_ref[j, SUM_ROWS:PART_ROWS, :] = packed


def group_kernel(in_ref, out_ref):
    total = in_ref[0].astype(F32)
    for j in range(1, PARTS):
        total = total + in_ref[j].astype(F32)
    out_ref[0:SUM_ROWS, :] = total[0:SUM_ROWS, :].astype(BF16)
    out_ref[SUM_ROWS:PART_ROWS, :] = packed_squares(total)


def add_kernel(own_ref, got_ref, out_ref):
    total = own_ref[...].astype(F32) + got_ref[...].astype(F32)
    out_ref[0:SUM_ROWS, :] = total[0:SUM_ROWS, :].astype(BF16)
    out_ref[SUM_ROWS:PART_ROWS, :] = packed_squares(total)


def reduce_kernel(total_cells, at_ref, own_ref, got_ref, out_ref, shrink_ref, column_ref):
    core, part = core_of(at_ref[0]), part_of(at_ref[0])
    total = own_ref[...].astype(F32) + got_ref[...].astype(F32)
    squares = whole_squares(total)
    shrink = jnp.maximum(0.0, 1.0 - TAU / jnp.sqrt(squares / total_cells + 1e-06))
    shrink_ref[...] = shrink
    for k in range(2):
        column_ref[k * 128 : (k + 1) * 128, :] = jnp.broadcast_to(shrink[k : k + 1, :], (128, 128)).T
    at = pl.multiple_of((part & 3) * PROJ_ROWS, PROJ_ROWS)
    proj = column_ref[pl.ds(at, PROJ_ROWS), :] * total[0:PROJ_ROWS, :] * (1.0 / math.sqrt(total_cells))
    at = pl.multiple_of(part * GRAM_ROWS, GRAM_ROWS)
    lanes = jnp.where(core == 0, shrink[0:1, :], shrink[1:2, :])
    gram = column_ref[pl.ds(at, GRAM_ROWS), :] * total[PROJ_ROWS:SUM_ROWS, :] * lanes * (1.0 / total_cells)
    mine = jnp.concatenate([proj, gram], axis=0).astype(BF16)
    for j in range(PARTS):
        out_ref[j] = mine


def scale_kernel(shrink_ref, *refs):
    out_ref = refs[-1]
    at = 0
    for m_ref in refs[:-1]:
        rows = slice(at, at + m_ref.shape[0])
        at = rows.stop
        for k in range(2):
            lanes = slice(k * 128, (k + 1) * 128)
            out_ref[rows, lanes] = (m_ref[:, lanes].astype(F32) * shrink_ref[k : k + 1, :]).astype(BF16)


def final_kernel(at_ref, own_ref, got_ref, proj_ref, gram_ref):
    core = core_of(at_ref[0])
    members = proj_ref.shape[0]
    for ref, half in ((own_ref, core), (got_ref, 1 - core)):
        for j in range(PARTS):
            tb, m, r = j // 8, (j // 4) % members, j % 4
            at = pl.multiple_of((half * 2 + tb) * 128, 128)
            rows = slice(r * PROJ_ROWS, (r + 1) * PROJ_ROWS)
            proj_ref[m, rows, pl.ds(at, 128)] = ref[j, 0:PROJ_ROWS, :].astype(F32)
            at = pl.multiple_of(half * 128, 128)
            gram_ref[j * GRAM_ROWS : (j + 1) * GRAM_ROWS, pl.ds(at, 128)] = (
                ref[j, PROJ_ROWS:SUM_ROWS, :].astype(F32)
            )


def both_ways(pairs):
    return [p for i, j in pairs for p in ((i, j), (j, i))]


def local(snapshots, coefficients, modes):
    members, levels, rows_x, rows_y, frames = snapshots.shape
    width = modes.shape[3]
    cells = rows_x * rows_y
    local_cells = levels * cells
    n_sx, n_z = lax.axis_size(SX), lax.axis_size(SY)
    total_cells = local_cells * n_sx * n_z
    core = lax.axis_index("c").astype(jnp.int32)
    parity = lax.axis_index("zl").astype(jnp.int32)
    part = lax.axis_index(GROUP).astype(jnp.int32)
    place = (core + 2 * parity + 4 * part).reshape(1)
    series = snapshots.reshape(members, levels, cells, frames)
    swap = [(0, 1), (1, 0)]

    g0, coefficients, x0, edge_b = first_grad(place, modes, coefficients, series)
    got0 = lax.ppermute(g0, "ens", swap)
    xb = lax.ppermute(edge_b, SX, both_ways([(i, i + 1) for i in range(1, n_sx - 1, 2)]))
    g1, x1 = second_grad(modes, coefficients, series, 1)
    g1, xb = lax.optimization_barrier((g1, xb))
    got1 = lax.ppermute(g1, "ens", swap)
    coefficients, _ = lax.optimization_barrier((coefficients, g1))
    g2, g3, modes, series, edge_a, row_a, row_b = rest_grad(place, modes, coefficients, series, 2)
    got2 = lax.ppermute(g2, "ens", swap)
    got0, g3 = lax.optimization_barrier((got0, g3))
    got3 = lax.ppermute(g3, "ens", swap)
    got1, edge_a, row_a, row_b = lax.optimization_barrier((got1, edge_a, row_a, row_b))
    xa = lax.ppermute(edge_a, "c", swap)
    za = lax.ppermute(row_a, SY, both_ways([(i, i + 1) for i in range(0, n_z, 2)]))
    zb = lax.ppermute(row_b, SY, both_ways([(i, i + 1) for i in range(1, n_z - 1, 2)]))
    base = pl.pallas_call(
        base_kernel,
        in_specs=[SM] + [VM] * 5,
        out_specs=VM,
        out_shape=jax.ShapeDtypeStruct((levels, cells, width), F32),
        compiler_params=PARAMS,
        cost_estimate=pl.CostEstimate(flops=12 * local_cells * width, bytes_accessed=6 * local_cells * width, transcendentals=0),
    )(place, modes, xa, xb, za, zb)

    moved, carry = [], None
    work = [(None, g0, got0, x0), (None, g1, got1, x1), (0, g2, got2, series), (1, g3, got3, series)]
    for level, (x_at, own, got, x) in enumerate(work):
        m, *carry = step_level(level, x_at, place, base, own, got, x, carry)
        moved.append(m)
    keep, send = carry

    part_shape = jax.ShapeDtypeStruct((PARTS, PART_ROWS, 128), BF16)
    other = lax.ppermute(send, "c", swap)
    joined = pl.pallas_call(
        join_kernel, in_specs=[VM, VM], out_specs=VM, out_shape=part_shape, compiler_params=PARAMS
    )(keep, other)
    parts = lax.all_to_all(joined, GROUP, 0, 0)
    line_shape = jax.ShapeDtypeStruct((PART_ROWS, 128), BF16)
    line = pl.pallas_call(
        group_kernel, in_specs=[VM], out_specs=VM, out_shape=line_shape, compiler_params=PARAMS
    )(parts)
    pairs = lax.axis_size("zh")
    near = lax.ppermute(line, "zh", [(i, i ^ 1) for i in range(pairs)])
    line = pl.pallas_call(
        add_kernel, in_specs=[VM, VM], out_specs=VM, out_shape=line_shape, compiler_params=PARAMS
    )(line, near)
    near = lax.ppermute(line, "zh", [(i, i ^ 3) for i in range(pairs)])
    spread, shrink = pl.pallas_call(
        functools.partial(reduce_kernel, total_cells),
        in_specs=[SM, VM, VM],
        out_specs=[VM, VM],
        out_shape=[
            jax.ShapeDtypeStruct((PARTS, SUM_ROWS, 128), BF16),
            jax.ShapeDtypeStruct((2, 128), F32),
        ],
        scratch_shapes=[pltpu.VMEM((width, 128), F32)],
        compiler_params=PARAMS,
    )(place, line, near)
    half = lax.all_to_all(spread, GROUP, 0, 0)
    new_modes = pl.pallas_call(
        scale_kernel,
        in_specs=[VM] * (1 + len(moved)),
        out_specs=VM,
        out_shape=jax.ShapeDtypeStruct((local_cells, width), BF16),
        compiler_params=PARAMS,
    )(shrink, *moved)
    half, new_modes = lax.optimization_barrier((half, new_modes))
    other_half = lax.ppermute(half, "c", swap)
    projected, gram = pl.pallas_call(
        final_kernel,
        in_specs=[SM, VM, VM],
        out_specs=[VM, VM],
        out_shape=[
            jax.ShapeDtypeStruct((members, width, frames), F32),
            jax.ShapeDtypeStruct((width, width), F32),
        ],
        compiler_params=PARAMS,
    )(place, half, other_half)
    return (new_modes.reshape(levels, rows_x, rows_y, width), gram, projected)


def solution(mesh):
    ens, n_sx, n_sy = (mesh.shape[a] for a in ("ens", "sx", "sy"))
    fine = Mesh(mesh.devices.reshape(ens, 2, n_sx // 4, 2, n_sy // 2, 2), ("ens", *SX, *SY))
    in_specs = (P("ens", None, SX, SY, None), P("ens", None, None), P(None, SX, SY, None))
    out_specs = (P(None, SX, SY, None), P(), P("ens", None, None))
    return jax.shard_map(local, mesh=fine, in_specs=in_specs, out_specs=out_specs, check_vma=False)
```

```python
import functools
import math

import jax
import jax.numpy as jnp
from jax import lax
from jax.experimental import pallas as pl
from jax.experimental.pallas import tpu as pltpu
from jax.sharding import Mesh, PartitionSpec as P

ETA = 0.25
LAM = 0.5
TAU = 0.4

F32 = jnp.float32
BF16 = jnp.bfloat16
VMEM_LIMIT = 40 * 1024 * 1024
PARAMS = pltpu.CompilerParams(vmem_limit_bytes=VMEM_LIMIT)

SX = ("xh", "y", "c")
SY = ("zh", "zl")
GROUP = ("xh", "y", "zl")
PARTS = 16
PROJ_ROWS = 64
GRAM_ROWS = 16
SUM_ROWS = PROJ_ROWS + GRAM_ROWS
PART_ROWS = SUM_ROWS + 8

VM = pl.BlockSpec(memory_space=pltpu.VMEM)
SM = pl.BlockSpec(memory_space=pltpu.SMEM)
HBM = pl.BlockSpec(memory_space=pltpu.HBM)


def core_of(place):
    return place & 1


def parity_of(place):
    return (place >> 1) & 1


def part_of(place):
    return place >> 2


def gradient(m, coefficients, series):
    acc = None
    for e in range(len(coefficients)):
        c = coefficients[e]()
        fitted = jnp.dot(m, c, preferred_element_type=F32)
        misfit = (fitted - series[e]().astype(F32)).astype(BF16)
        term = lax.dot_general(misfit, c, (((1,), (1,)), ((), ())), preferred_element_type=F32)
        acc = term if acc is None else acc + term
    return acc.astype(BF16)


def start_all(copies, sems):
    copies = [pltpu.make_async_copy(s, d, sems.at[i]) for i, (s, d) in enumerate(copies)]
    for copy in copies:
        copy.start()
    return copies


def after(copy, ref, *at):
    def load():
        copy.wait()
        return ref[at].reshape(-1, ref.shape[-1])

    return load


def first_grad_kernel(at_ref, m_hbm, c_hbm, x_hbm, g_ref, c_ref, x_ref, xb_ref, m_ref, sems):
    members = c_hbm.shape[0]
    last = m_hbm.shape[1] - 1
    copies = [(m_hbm.at[0], m_ref)]
    for e in range(members):
        copies.append((c_hbm.at[e], c_ref.at[e]))
        copies.append((x_hbm.at[e, 0], x_ref.at[e]))
    copies.append((m_hbm.at[:, last * core_of(at_ref[0])], xb_ref))
    copies = start_all(copies, sems)
    copies[0].wait()
    g_ref[...] = gradient(
        m_ref[...].reshape(g_ref.shape),
        [after(copies[1 + 2 * e], c_ref, e) for e in range(members)],
        [after(copies[2 + 2 * e], x_ref, e) for e in range(members)],
    )
    copies[-1].wait()


def second_grad_kernel(level, m_hbm, c_ref, x_hbm, g_ref, x_ref, m_ref, sems):
    members = c_ref.shape[0]
    copies = [(m_hbm.at[level], m_ref)]
    for e in range(members):
        copies.append((x_hbm.at[e, level], x_ref.at[e]))
    copies = start_all(copies, sems)
    copies[0].wait()
    g_ref[...] = gradient(
        m_ref[...].reshape(g_ref.shape),
        [functools.partial(c_ref.__getitem__, e) for e in range(members)],
        [after(copies[1 + e], x_ref, e) for e in range(members)],
    )


def rest_grad_kernel(begin, at_ref, m_hbm, c_ref, x_hbm, *refs):
    *g_refs, m_ref, x_ref, xa_ref, za_ref, zb_ref, tmp_ref, sems = refs
    members, levels, cells, _ = x_hbm.shape
    _, rows_x, rows_y, width = m_ref.shape
    copies = [(m_hbm, m_ref)]
    for level in range(begin, levels):
        for e in range(members):
            copies.append((x_hbm.at[e, level], x_ref.at[e, level - begin]))
    copies = start_all(copies, sems)
    copies[0].wait()
    core, even = core_of(at_ref[0]), parity_of(at_ref[0]) == 0
    xa_ref[...] = m_ref[:, (rows_x - 1) * (1 - core)]
    tmp_ref[0] = m_ref[:, :, 0:8, :].reshape(levels * rows_x, 8, width).astype(F32)
    tmp_ref[1] = m_ref[:, :, rows_y - 8 : rows_y, :].reshape(levels * rows_x, 8, width).astype(F32)
    lo, hi = tmp_ref[0, :, 0, :], tmp_ref[1, :, 7, :]
    za_ref[...] = jnp.where(even, hi, lo).astype(BF16)
    zb_ref[...] = jnp.where(even, lo, hi).astype(BF16)
    for i, g_ref in enumerate(g_refs):
        g_ref[...] = gradient(
            m_ref[begin + i].reshape(g_ref.shape),
            [functools.partial(c_ref.__getitem__, e) for e in range(members)],
            [after(copies[1 + i * members + e], x_ref, e, i) for e in range(members)],
        )


def grad_cost(members, cells, frames, width):
    return pl.CostEstimate(
        flops=4 * members * cells * frames * width,
        bytes_accessed=2 * cells * (2 * width + members * frames) + 2 * members * width * frames,
        transcendentals=0,
    )


def in_hbm(array):
    return pltpu.with_memory_space_constraint(array, pltpu.HBM)


def first_grad(place, modes, coefficients, series):
    members, _, cells, frames = series.shape
    levels, rows_x, rows_y, width = modes.shape
    outs = [
        jax.ShapeDtypeStruct((cells, width), BF16),
        pltpu.VMEM(coefficients.shape, BF16),
        pltpu.VMEM((members, cells, frames), BF16),
        jax.ShapeDtypeStruct((levels, rows_y, width), BF16),
    ]
    return pl.pallas_call(
        first_grad_kernel,
        in_specs=[SM] + [HBM] * 3,
        out_specs=[VM] * len(outs),
        out_shape=outs,
        scratch_shapes=[
            pltpu.VMEM((rows_x, rows_y, width), BF16),
            pltpu.SemaphoreType.DMA((2 + 2 * members,)),
        ],
        compiler_params=PARAMS,
        cost_estimate=grad_cost(members, cells, frames, width),
    )(place, in_hbm(modes), in_hbm(coefficients), in_hbm(series))


def second_grad(modes, coefficients, series, level):
    members, _, cells, frames = series.shape
    _, rows_x, rows_y, width = modes.shape
    outs = [jax.ShapeDtypeStruct((cells, width), BF16), pltpu.VMEM((members, cells, frames), BF16)]
    return pl.pallas_call(
        functools.partial(second_grad_kernel, level),
        in_specs=[HBM, VM, HBM],
        out_specs=[VM] * len(outs),
        out_shape=outs,
        scratch_shapes=[
            pltpu.VMEM((rows_x, rows_y, width), BF16),
            pltpu.SemaphoreType.DMA((1 + members,)),
        ],
        compiler_params=PARAMS,
        cost_estimate=grad_cost(members, cells, frames, width),
    )(in_hbm(modes), coefficients, in_hbm(series))


def rest_grad(place, modes, coefficients, series, begin):
    members, levels, cells, frames = series.shape
    _, rows_x, rows_y, width = modes.shape
    count = levels - begin
    outs = [jax.ShapeDtypeStruct((cells, width), BF16)] * count
    outs += [
        pltpu.VMEM(modes.shape, BF16),
        pltpu.VMEM((members, count, cells, frames), BF16),
        jax.ShapeDtypeStruct((levels, rows_y, width), BF16),
        jax.ShapeDtypeStruct((levels * rows_x, width), BF16),
        jax.ShapeDtypeStruct((levels * rows_x, width), BF16),
    ]
    return pl.pallas_call(
        functools.partial(rest_grad_kernel, begin),
        in_specs=[SM, HBM, VM, HBM],
        out_specs=[VM] * len(outs),
        out_shape=outs,
        scratch_shapes=[
            pltpu.VMEM((2, levels * rows_x, 8, width), F32),
            pltpu.SemaphoreType.DMA((1 + members * count,)),
        ],
        compiler_params=PARAMS,
        cost_estimate=grad_cost(members, count * cells, frames, width),
    )(place, in_hbm(modes), coefficients, in_hbm(series))


def base_kernel(at_ref, m_ref, xa_ref, xb_ref, za_ref, zb_ref, base_ref):
    levels, rows_x, rows_y, width = m_ref.shape
    lower, even = core_of(at_ref[0]) == 0, parity_of(at_ref[0]) == 0
    shape = (rows_x, rows_y, width)
    at = lax.broadcasted_iota(jnp.int32, shape, 1)
    for level in range(levels):
        f = m_ref[level].astype(F32)
        xa, xb = xa_ref[level : level + 1].astype(F32), xb_ref[level : level + 1].astype(F32)
        rows = slice(level * rows_x, (level + 1) * rows_x)
        za, zb = za_ref[rows, :].astype(F32), zb_ref[rows, :].astype(F32)
        up = jnp.concatenate([jnp.where(lower, xb, xa), f[:-1]], axis=0)
        down = jnp.concatenate([f[1:], jnp.where(lower, xa, xb)], axis=0)
        zlo = jnp.broadcast_to(jnp.where(even, zb, za)[:, None, :], shape)
        zhi = jnp.broadcast_to(jnp.where(even, za, zb)[:, None, :], shape)
        left = jnp.where(at == 0, zlo, pltpu.roll(f, 1, 1))
        right = jnp.where(at == rows_y - 1, zhi, pltpu.roll(f, rows_y - 1, 1))
        bent = 4.0 * f - (down + up + right + left)
        base_ref[level] = (f - (ETA * LAM) * bent).reshape(rows_x * rows_y, width)


def split_squares(squares, rows):
    high = squares.astype(BF16).astype(F32)
    return jnp.concatenate([high, squares - high, jnp.zeros((rows - 4, 128), F32)], axis=0)


def emit(out_ref, half, proj_ref, gram_ref, squares):
    members = proj_ref.shape[0]
    for j in range(PARTS):
        tb, m, r = j // 8, (j // 4) % members, j % 4
        at = pl.multiple_of((half * 2 + tb) * 128, 128)
        block = proj_ref[m, r * PROJ_ROWS : (r + 1) * PROJ_ROWS, pl.ds(at, 128)]
        out_ref[j, 0:PROJ_ROWS, :] = block.astype(BF16)
        at = pl.multiple_of(half * 128, 128)
        block = gram_ref[j * GRAM_ROWS : (j + 1) * GRAM_ROWS, pl.ds(at, 128)]
        out_ref[j, PROJ_ROWS:SUM_ROWS, :] = block.astype(BF16)
        out_ref[j, SUM_ROWS:PART_ROWS, :] = squares


def step_kernel(level, x_at, first, last, *refs):
    (at_ref, base_ref, own_ref, got_ref, x_ref), refs = refs[:5], refs[5:]
    if not first:
        (proj_in, gram_in, squares_in), refs = refs[:3], refs[3:]
    if last:
        moved_ref, keep_ref, send_ref, proj_ref, gram_ref = refs
    else:
        moved_ref, proj_ref, gram_ref, squares_ref = refs
    grad = own_ref[...].astype(F32) + got_ref[...].astype(F32)
    moved = (base_ref[level] - ETA * grad).astype(BF16)
    moved_ref[...] = moved
    wide = moved.astype(F32)
    squares = jnp.sum(wide * wide, axis=0, keepdims=True)
    if not first:
        squares = squares + squares_in[...]
    turned = moved.T
    gram = jnp.dot(turned, moved, preferred_element_type=F32)
    gram_ref[...] = gram if first else gram_in[...] + gram
    for e in range(x_ref.shape[0]):
        x = x_ref[e] if x_at is None else x_ref[e, x_at]
        proj = jnp.dot(turned, x, preferred_element_type=F32)
        proj_ref[e] = proj if first else proj_in[e] + proj
    if last:
        core = core_of(at_ref[0])
        pair = jnp.concatenate([squares[:, 0:128], squares[:, 128:256]], axis=0)
        packed = split_squares(pair, 8).astype(BF16)
        emit(send_ref, 1 - core, proj_ref, gram_ref, packed)
        emit(keep_ref, core, proj_ref, gram_ref, packed)
    else:
        squares_ref[...] = squares


def step_level(level, x_at, place, base, own, got, series, carry):
    members, frames = series.shape[0], series.shape[-1]
    rows, width = own.shape
    first, last = carry is None, level == base.shape[0] - 1
    args = [place, base, own, got, series]
    if not first:
        args += list(carry)
    sums = [
        jax.ShapeDtypeStruct((members, width, frames), F32),
        jax.ShapeDtypeStruct((width, width), F32),
        jax.ShapeDtypeStruct((1, width), F32),
    ]
    outs = [jax.ShapeDtypeStruct((rows, width), BF16)]
    scratch, aliases = [], {}
    if last:
        outs += [jax.ShapeDtypeStruct((PARTS, PART_ROWS, 128), BF16)] * 2
        scratch = [pltpu.VMEM(s.shape, F32) for s in sums[:2]]
    else:
        outs += sums
        if not first:
            aliases = {5 + i: 1 + i for i in range(3)}
    return pl.pallas_call(
        functools.partial(step_kernel, level, x_at, first, last),
        in_specs=[SM] + [VM] * (len(args) - 1),
        out_specs=[VM] * len(outs),
        out_shape=outs,
        scratch_shapes=scratch,
        input_output_aliases=aliases,
        compiler_params=PARAMS,
        cost_estimate=pl.CostEstimate(
            flops=2 * rows * width * (width + members * frames),
            bytes_accessed=2 * rows * (4 * width + members * frames),
            transcendentals=0,
        ),
    )(*args)


def whole_squares(part):
    return part[SUM_ROWS : SUM_ROWS + 2, :] + part[SUM_ROWS + 2 : SUM_ROWS + 4, :]


def packed_squares(total):
    return split_squares(whole_squares(total), 8).astype(BF16)


def join_kernel(keep_ref, got_ref, out_ref):
    out_ref[:, 0:SUM_ROWS, :] = (
        keep_ref[:, 0:SUM_ROWS, :].astype(F32) + got_ref[:, 0:SUM_ROWS, :].astype(F32)
    ).astype(BF16)
    tail = keep_ref[0].astype(F32) + got_ref[0].astype(F32)
    packed = packed_squares(tail)
    for j in range(PARTS):
        out_ref[j, SUM_ROWS:PART_ROWS, :] = packed


def group_kernel(in_ref, out_ref):
    total = in_ref[0].astype(F32)
    for j in range(1, PARTS):
        total = total + in_ref[j].astype(F32)
    out_ref[0:SUM_ROWS, :] = total[0:SUM_ROWS, :].astype(BF16)
    out_ref[SUM_ROWS:PART_ROWS, :] = packed_squares(total)


def add_kernel(own_ref, got_ref, out_ref):
    total = own_ref[...].astype(F32) + got_ref[...].astype(F32)
    out_ref[0:SUM_ROWS, :] = total[0:SUM_ROWS, :].astype(BF16)
    out_ref[SUM_ROWS:PART_ROWS, :] = packed_squares(total)


def reduce_kernel(total_cells, at_ref, own_ref, got_ref, out_ref, shrink_ref, column_ref):
    core, part = core_of(at_ref[0]), part_of(at_ref[0])
    total = own_ref[...].astype(F32) + got_ref[...].astype(F32)
    squares = whole_squares(total)
    shrink = jnp.maximum(0.0, 1.0 - TAU / jnp.sqrt(squares / total_cells + 1e-06))
    shrink_ref[...] = shrink
    for k in range(2):
        column_ref[k * 128 : (k + 1) * 128, :] = jnp.broadcast_to(shrink[k : k + 1, :], (128, 128)).T
    at = pl.multiple_of((part & 3) * PROJ_ROWS, PROJ_ROWS)
    proj = column_ref[pl.ds(at, PROJ_ROWS), :] * total[0:PROJ_ROWS, :] * (1.0 / math.sqrt(total_cells))
    at = pl.multiple_of(part * GRAM_ROWS, GRAM_ROWS)
    lanes = jnp.where(core == 0, shrink[0:1, :], shrink[1:2, :])
    gram = column_ref[pl.ds(at, GRAM_ROWS), :] * total[PROJ_ROWS:SUM_ROWS, :] * lanes * (1.0 / total_cells)
    mine = jnp.concatenate([proj, gram], axis=0).astype(BF16)
    for j in range(PARTS):
        out_ref[j] = mine


def scale_kernel(shrink_ref, *refs):
    out_ref = refs[-1]
    at = 0
    for m_ref in refs[:-1]:
        rows = slice(at, at + m_ref.shape[0])
        at = rows.stop
        for k in range(2):
            lanes = slice(k * 128, (k + 1) * 128)
            out_ref[rows, lanes] = (m_ref[:, lanes].astype(F32) * shrink_ref[k : k + 1, :]).astype(BF16)


def final_kernel(at_ref, own_ref, got_ref, proj_ref, gram_ref):
    core = core_of(at_ref[0])
    members = proj_ref.shape[0]
    for ref, half in ((own_ref, core), (got_ref, 1 - core)):
        for j in range(PARTS):
            tb, m, r = j // 8, (j // 4) % members, j % 4
            at = pl.multiple_of((half * 2 + tb) * 128, 128)
            rows = slice(r * PROJ_ROWS, (r + 1) * PROJ_ROWS)
            proj_ref[m, rows, pl.ds(at, 128)] = ref[j, 0:PROJ_ROWS, :].astype(F32)
            at = pl.multiple_of(half * 128, 128)
            gram_ref[j * GRAM_ROWS : (j + 1) * GRAM_ROWS, pl.ds(at, 128)] = (
                ref[j, PROJ_ROWS:SUM_ROWS, :].astype(F32)
            )


def both_ways(pairs):
    return [p for i, j in pairs for p in ((i, j), (j, i))]


def local(snapshots, coefficients, modes):
    members, levels, rows_x, rows_y, frames = snapshots.shape
    width = modes.shape[3]
    cells = rows_x * rows_y
    local_cells = levels * cells
    n_sx, n_z = lax.axis_size(SX), lax.axis_size(SY)
    total_cells = local_cells * n_sx * n_z
    core = lax.axis_index("c").astype(jnp.int32)
    parity = lax.axis_index("zl").astype(jnp.int32)
    part = lax.axis_index(GROUP).astype(jnp.int32)
    place = (core + 2 * parity + 4 * part).reshape(1)
    series = snapshots.reshape(members, levels, cells, frames)
    swap = [(0, 1), (1, 0)]

    g0, coefficients, x0, edge_b = first_grad(place, modes, coefficients, series)
    got0 = lax.ppermute(g0, "ens", swap)
    xb = lax.ppermute(edge_b, SX, both_ways([(i, i + 1) for i in range(1, n_sx - 1, 2)]))
    g1, x1 = second_grad(modes, coefficients, series, 1)
    g1, xb = lax.optimization_barrier((g1, xb))
    got1 = lax.ppermute(g1, "ens", swap)
    coefficients, got0, _ = lax.optimization_barrier((coefficients, got0, g1))
    g2, g3, modes, series, edge_a, row_a, row_b = rest_grad(place, modes, coefficients, series, 2)
    got2 = lax.ppermute(g2, "ens", swap)
    got3 = lax.ppermute(g3, "ens", swap)
    got0, row_a, row_b = lax.optimization_barrier((got0, row_a, row_b))
    za = lax.ppermute(row_a, SY, both_ways([(i, i + 1) for i in range(0, n_z, 2)]))
    zb = lax.ppermute(row_b, SY, both_ways([(i, i + 1) for i in range(1, n_z - 1, 2)]))
    got1, edge_a, za, zb = lax.optimization_barrier((got1, edge_a, za, zb))
    xa = lax.ppermute(edge_a, "c", swap)
    base = pl.pallas_call(
        base_kernel,
        in_specs=[SM] + [VM] * 5,
        out_specs=VM,
        out_shape=jax.ShapeDtypeStruct((levels, cells, width), F32),
        compiler_params=PARAMS,
        cost_estimate=pl.CostEstimate(flops=12 * local_cells * width, bytes_accessed=6 * local_cells * width, transcendentals=0),
    )(place, modes, xa, xb, za, zb)

    moved, carry = [], None
    work = [(None, g0, got0, x0), (None, g1, got1, x1), (0, g2, got2, series), (1, g3, got3, series)]
    for level, (x_at, own, got, x) in enumerate(work):
        m, *carry = step_level(level, x_at, place, base, own, got, x, carry)
        moved.append(m)
    keep, send = carry

    part_shape = jax.ShapeDtypeStruct((PARTS, PART_ROWS, 128), BF16)
    other = lax.ppermute(send, "c", swap)
    joined = pl.pallas_call(
        join_kernel, in_specs=[VM, VM], out_specs=VM, out_shape=part_shape, compiler_params=PARAMS
    )(keep, other)
    parts = lax.all_to_all(joined, GROUP, 0, 0)
    line_shape = jax.ShapeDtypeStruct((PART_ROWS, 128), BF16)
    line = pl.pallas_call(
        group_kernel, in_specs=[VM], out_specs=VM, out_shape=line_shape, compiler_params=PARAMS
    )(parts)
    pairs = lax.axis_size("zh")
    near = lax.ppermute(line, "zh", [(i, i ^ 1) for i in range(pairs)])
    line = pl.pallas_call(
        add_kernel, in_specs=[VM, VM], out_specs=VM, out_shape=line_shape, compiler_params=PARAMS
    )(line, near)
    near = lax.ppermute(line, "zh", [(i, i ^ 3) for i in range(pairs)])
    spread, shrink = pl.pallas_call(
        functools.partial(reduce_kernel, total_cells),
        in_specs=[SM, VM, VM],
        out_specs=[VM, VM],
        out_shape=[
            jax.ShapeDtypeStruct((PARTS, SUM_ROWS, 128), BF16),
            jax.ShapeDtypeStruct((2, 128), F32),
        ],
        scratch_shapes=[pltpu.VMEM((width, 128), F32)],
        compiler_params=PARAMS,
    )(place, line, near)
    half = lax.all_to_all(spread, GROUP, 0, 0)
    new_modes = pl.pallas_call(
        scale_kernel,
        in_specs=[VM] * (1 + len(moved)),
        out_specs=VM,
        out_shape=jax.ShapeDtypeStruct((local_cells, width), BF16),
        compiler_params=PARAMS,
    )(shrink, *moved)
    half, new_modes = lax.optimization_barrier((half, new_modes))
    other_half = lax.ppermute(half, "c", swap)
    projected, gram = pl.pallas_call(
        final_kernel,
        in_specs=[SM, VM, VM],
        out_specs=[VM, VM],
        out_shape=[
            jax.ShapeDtypeStruct((members, width, frames), F32),
            jax.ShapeDtypeStruct((width, width), F32),
        ],
        compiler_params=PARAMS,
    )(place, half, other_half)
    return (new_modes.reshape(levels, rows_x, rows_y, width), gram, projected)


def solution(mesh):
    ens, n_sx, n_sy = (mesh.shape[a] for a in ("ens", "sx", "sy"))
    fine = Mesh(mesh.devices.reshape(ens, 2, n_sx // 4, 2, n_sy // 2, 2), ("ens", *SX, *SY))
    in_specs = (P("ens", None, SX, SY, None), P("ens", None, None), P(None, SX, SY, None))
    out_specs = (P(None, SX, SY, None), P(), P("ens", None, None))
    return jax.shard_map(local, mesh=fine, in_specs=in_specs, out_specs=out_specs, check_vma=False)
```

```python
import functools
import math

import jax
import jax.numpy as jnp
from jax import lax
from jax.experimental import pallas as pl
from jax.experimental.pallas import tpu as pltpu
from jax.sharding import Mesh, PartitionSpec as P

ETA = 0.25
LAM = 0.5
TAU = 0.4

F32 = jnp.float32
BF16 = jnp.bfloat16
VMEM_LIMIT = 40 * 1024 * 1024
PARAMS = pltpu.CompilerParams(vmem_limit_bytes=VMEM_LIMIT)

SX = ("xh", "y", "c")
SY = ("zh", "zl")
GROUP = ("xh", "y", "zl")
PARTS = 16
PROJ_ROWS = 64
GRAM_ROWS = 16
SUM_ROWS = PROJ_ROWS + GRAM_ROWS
PART_ROWS = SUM_ROWS + 8

VM = pl.BlockSpec(memory_space=pltpu.VMEM)
SM = pl.BlockSpec(memory_space=pltpu.SMEM)
HBM = pl.BlockSpec(memory_space=pltpu.HBM)


def core_of(place):
    return place & 1


def parity_of(place):
    return (place >> 1) & 1


def part_of(place):
    return (place >> 2) & 15


def at_end(place, which):
    return ((place >> (6 + which)) & 1) == 1


def gradient(m, coefficients, series):
    acc = None
    for e in range(len(coefficients)):
        c = coefficients[e]()
        fitted = jnp.dot(m, c, preferred_element_type=F32)
        misfit = (fitted - series[e]().astype(F32)).astype(BF16)
        term = lax.dot_general(misfit, c, (((1,), (1,)), ((), ())), preferred_element_type=F32)
        acc = term if acc is None else acc + term
    return acc.astype(BF16)


def start_all(copies, sems):
    copies = [pltpu.make_async_copy(s, d, sems.at[i]) for i, (s, d) in enumerate(copies)]
    for copy in copies:
        copy.start()
    return copies


def after(copy, ref, *at):
    def load():
        copy.wait()
        return ref[at].reshape(-1, ref.shape[-1])

    return load


def first_grad_kernel(at_ref, m_hbm, c_hbm, x_hbm, g_ref, c_ref, x_ref, xb_ref, m_ref, sems):
    members = c_hbm.shape[0]
    last = m_hbm.shape[1] - 1
    copies = [(m_hbm.at[0], m_ref)]
    for e in range(members):
        copies.append((c_hbm.at[e], c_ref.at[e]))
        copies.append((x_hbm.at[e, 0], x_ref.at[e]))
    copies.append((m_hbm.at[:, last * core_of(at_ref[0])], xb_ref))
    copies = start_all(copies, sems)
    copies[0].wait()
    g_ref[...] = gradient(
        m_ref[...].reshape(g_ref.shape),
        [after(copies[1 + 2 * e], c_ref, e) for e in range(members)],
        [after(copies[2 + 2 * e], x_ref, e) for e in range(members)],
    )
    copies[-1].wait()


def second_grad_kernel(level, m_hbm, c_ref, x_hbm, g_ref, x_ref, m_ref, sems):
    members = c_ref.shape[0]
    copies = [(m_hbm.at[level], m_ref)]
    for e in range(members):
        copies.append((x_hbm.at[e, level], x_ref.at[e]))
    copies = start_all(copies, sems)
    copies[0].wait()
    g_ref[...] = gradient(
        m_ref[...].reshape(g_ref.shape),
        [functools.partial(c_ref.__getitem__, e) for e in range(members)],
        [after(copies[1 + e], x_ref, e) for e in range(members)],
    )


def rest_grad_kernel(begin, at_ref, m_hbm, c_ref, x_hbm, *refs):
    *g_refs, m_ref, x_ref, xa_ref, za_ref, zb_ref, tmp_ref, sems = refs
    members, levels, cells, _ = x_hbm.shape
    _, rows_x, rows_y, width = m_ref.shape
    copies = [(m_hbm, m_ref)]
    for level in range(begin, levels):
        for e in range(members):
            copies.append((x_hbm.at[e, level], x_ref.at[e, level - begin]))
    copies = start_all(copies, sems)
    copies[0].wait()
    core, even = core_of(at_ref[0]), parity_of(at_ref[0]) == 0
    xa_ref[...] = m_ref[:, (rows_x - 1) * (1 - core)]
    tmp_ref[0] = m_ref[:, :, 0:8, :].reshape(levels * rows_x, 8, width).astype(F32)
    tmp_ref[1] = m_ref[:, :, rows_y - 8 : rows_y, :].reshape(levels * rows_x, 8, width).astype(F32)
    lo, hi = tmp_ref[0, :, 0, :], tmp_ref[1, :, 7, :]
    za_ref[...] = jnp.where(even, hi, lo).astype(BF16)
    zb_ref[...] = jnp.where(even, lo, hi).astype(BF16)
    for i, g_ref in enumerate(g_refs):
        g_ref[...] = gradient(
            m_ref[begin + i].reshape(g_ref.shape),
            [functools.partial(c_ref.__getitem__, e) for e in range(members)],
            [after(copies[1 + i * members + e], x_ref, e, i) for e in range(members)],
        )


def grad_cost(members, cells, frames, width):
    return pl.CostEstimate(
        flops=4 * members * cells * frames * width,
        bytes_accessed=2 * cells * (2 * width + members * frames) + 2 * members * width * frames,
        transcendentals=0,
    )


def in_hbm(array):
    return pltpu.with_memory_space_constraint(array, pltpu.HBM)


def first_grad(place, modes, coefficients, series):
    members, _, cells, frames = series.shape
    levels, rows_x, rows_y, width = modes.shape
    outs = [
        jax.ShapeDtypeStruct((cells, width), BF16),
        pltpu.VMEM(coefficients.shape, BF16),
        pltpu.VMEM((members, cells, frames), BF16),
        jax.ShapeDtypeStruct((levels, rows_y, width), BF16),
    ]
    return pl.pallas_call(
        first_grad_kernel,
        in_specs=[SM] + [HBM] * 3,
        out_specs=[VM] * len(outs),
        out_shape=outs,
        scratch_shapes=[
            pltpu.VMEM((rows_x, rows_y, width), BF16),
            pltpu.SemaphoreType.DMA((2 + 2 * members,)),
        ],
        compiler_params=PARAMS,
        cost_estimate=grad_cost(members, cells, frames, width),
    )(place, in_hbm(modes), in_hbm(coefficients), in_hbm(series))


def second_grad(modes, coefficients, series, level):
    members, _, cells, frames = series.shape
    _, rows_x, rows_y, width = modes.shape
    outs = [jax.ShapeDtypeStruct((cells, width), BF16), pltpu.VMEM((members, cells, frames), BF16)]
    return pl.pallas_call(
        functools.partial(second_grad_kernel, level),
        in_specs=[HBM, VM, HBM],
        out_specs=[VM] * len(outs),
        out_shape=outs,
        scratch_shapes=[
            pltpu.VMEM((rows_x, rows_y, width), BF16),
            pltpu.SemaphoreType.DMA((1 + members,)),
        ],
        compiler_params=PARAMS,
        cost_estimate=grad_cost(members, cells, frames, width),
    )(in_hbm(modes), coefficients, in_hbm(series))


def rest_grad(place, modes, coefficients, series, begin):
    members, levels, cells, frames = series.shape
    _, rows_x, rows_y, width = modes.shape
    count = levels - begin
    outs = [jax.ShapeDtypeStruct((cells, width), BF16)] * count
    outs += [
        pltpu.VMEM(modes.shape, BF16),
        pltpu.VMEM((members, count, cells, frames), BF16),
        jax.ShapeDtypeStruct((levels, rows_y, width), BF16),
        jax.ShapeDtypeStruct((levels * rows_x, width), BF16),
        jax.ShapeDtypeStruct((levels * rows_x, width), BF16),
    ]
    return pl.pallas_call(
        functools.partial(rest_grad_kernel, begin),
        in_specs=[SM, HBM, VM, HBM],
        out_specs=[VM] * len(outs),
        out_shape=outs,
        scratch_shapes=[
            pltpu.VMEM((2, levels * rows_x, 8, width), F32),
            pltpu.SemaphoreType.DMA((1 + members * count,)),
        ],
        compiler_params=PARAMS,
        cost_estimate=grad_cost(members, count * cells, frames, width),
    )(place, in_hbm(modes), coefficients, in_hbm(series))


def base_of(level, place, m_ref, xa_ref, xb_ref, za_ref, zb_ref):
    _, rows_x, rows_y, width = m_ref.shape
    lower, even = core_of(place) == 0, parity_of(place) == 0
    shape = (rows_x, rows_y, width)
    f = m_ref[level].astype(F32)
    xa, xb = xa_ref[level : level + 1].astype(F32), xb_ref[level : level + 1].astype(F32)
    rows = slice(level * rows_x, (level + 1) * rows_x)
    za, zb = za_ref[rows, :].astype(F32), zb_ref[rows, :].astype(F32)
    xlo = jnp.where(at_end(place, 0), 0.0, jnp.where(lower, xb, xa))
    xhi = jnp.where(at_end(place, 1), 0.0, jnp.where(lower, xa, xb))
    zlo = jnp.where(at_end(place, 2), 0.0, jnp.where(even, zb, za))
    zhi = jnp.where(at_end(place, 3), 0.0, jnp.where(even, za, zb))
    up = jnp.concatenate([xlo, f[:-1]], axis=0)
    down = jnp.concatenate([f[1:], xhi], axis=0)
    at = lax.broadcasted_iota(jnp.int32, shape, 1)
    left = jnp.where(at == 0, jnp.broadcast_to(zlo[:, None, :], shape), pltpu.roll(f, 1, 1))
    right = jnp.where(
        at == rows_y - 1, jnp.broadcast_to(zhi[:, None, :], shape), pltpu.roll(f, rows_y - 1, 1)
    )
    bent = 4.0 * f - (down + up + right + left)
    return (f - (ETA * LAM) * bent).reshape(rows_x * rows_y, width)


def split_squares(squares, rows):
    high = squares.astype(BF16).astype(F32)
    return jnp.concatenate([high, squares - high, jnp.zeros((rows - 4, 128), F32)], axis=0)


def emit(out_ref, half, proj_ref, gram_ref, squares):
    members = proj_ref.shape[0]
    for j in range(PARTS):
        tb, m, r = j // 8, (j // 4) % members, j % 4
        at = pl.multiple_of((half * 2 + tb) * 128, 128)
        block = proj_ref[m, r * PROJ_ROWS : (r + 1) * PROJ_ROWS, pl.ds(at, 128)]
        out_ref[j, 0:PROJ_ROWS, :] = block.astype(BF16)
        at = pl.multiple_of(half * 128, 128)
        block = gram_ref[j * GRAM_ROWS : (j + 1) * GRAM_ROWS, pl.ds(at, 128)]
        out_ref[j, PROJ_ROWS:SUM_ROWS, :] = block.astype(BF16)
        out_ref[j, SUM_ROWS:PART_ROWS, :] = squares


def move(base, own_ref, got_ref):
    grad = own_ref[...].astype(F32) + got_ref[...].astype(F32)
    moved = (base - ETA * grad).astype(BF16)
    wide = moved.astype(F32)
    return moved, jnp.sum(wide * wide, axis=0, keepdims=True)


def most_kernel(at_ref, m_ref, xa_ref, xb_ref, za_ref, zb_ref, *refs):
    *refs, base_ref, moved_ref, proj_ref, gram_ref, squares_ref = refs
    halos = (xa_ref, xb_ref, za_ref, zb_ref)
    count = len(refs) // 3
    owns, gots, xs = refs[:count], refs[count : 2 * count], refs[2 * count :]
    squares = None
    for level in range(count):
        moved, part = move(base_of(level, at_ref[0], m_ref, *halos), owns[level], gots[level])
        squares = part if level == 0 else squares + part
        moved_ref[level * moved.shape[0] : (level + 1) * moved.shape[0], :] = moved
        turned = moved.T
        gram = jnp.dot(turned, moved, preferred_element_type=F32)
        gram_ref[...] = gram if level == 0 else gram_ref[...] + gram
        for e in range(proj_ref.shape[0]):
            x = xs[level][e] if len(xs[level].shape) == 3 else xs[level][e, 0]
            proj = jnp.dot(turned, x, preferred_element_type=F32)
            proj_ref[e] = proj if level == 0 else proj_ref[e] + proj
    squares_ref[...] = squares
    base_ref[...] = base_of(count, at_ref[0], m_ref, *halos)


def last_kernel(at_ref, base_ref, own_ref, got_ref, x_ref, proj_in, gram_in, squares_in, *refs):
    moved_ref, keep_ref, send_ref, proj_ref, gram_ref = refs
    moved, squares = move(base_ref[...], own_ref, got_ref)
    moved_ref[...] = moved
    squares = squares + squares_in[...]
    turned = moved.T
    gram_ref[...] = gram_in[...] + jnp.dot(turned, moved, preferred_element_type=F32)
    for e in range(proj_ref.shape[0]):
        proj = jnp.dot(turned, x_ref[e, x_ref.shape[1] - 1], preferred_element_type=F32)
        proj_ref[e] = proj_in[e] + proj
    core = core_of(at_ref[0])
    pair = jnp.concatenate([squares[:, 0:128], squares[:, 128:256]], axis=0)
    packed = split_squares(pair, 8).astype(BF16)
    emit(send_ref, 1 - core, proj_ref, gram_ref, packed)
    emit(keep_ref, core, proj_ref, gram_ref, packed)


def step_cost(members, cells, frames, width):
    return pl.CostEstimate(
        flops=2 * cells * width * (width + members * frames),
        bytes_accessed=2 * cells * (4 * width + members * frames),
        transcendentals=0,
    )


def steps(place, modes, halos, owns, gots, series):
    members, frames = series[0].shape[0], series[0].shape[-1]
    cells, width = owns[0].shape
    most = len(owns) - 1
    sums = [
        jax.ShapeDtypeStruct((members, width, frames), F32),
        jax.ShapeDtypeStruct((width, width), F32),
        jax.ShapeDtypeStruct((1, width), F32),
    ]
    args = [modes, *halos, *owns[:most], *gots[:most], *series[:most]]
    base, moved, *carry = pl.pallas_call(
        most_kernel,
        in_specs=[SM] + [VM] * len(args),
        out_specs=[VM] * 5,
        out_shape=[
            jax.ShapeDtypeStruct((cells, width), F32),
            jax.ShapeDtypeStruct((most * cells, width), BF16),
            *sums,
        ],
        compiler_params=PARAMS,
        cost_estimate=step_cost(members, most * cells, frames, width),
    )(place, *args)
    args = [base, owns[most], gots[most], series[most], *carry]
    tail, keep, send = pl.pallas_call(
        last_kernel,
        in_specs=[SM] + [VM] * len(args),
        out_specs=[VM] * 3,
        out_shape=[jax.ShapeDtypeStruct((cells, width), BF16)]
        + [jax.ShapeDtypeStruct((PARTS, PART_ROWS, 128), BF16)] * 2,
        scratch_shapes=[pltpu.VMEM(s.shape, F32) for s in sums[:2]],
        compiler_params=PARAMS,
        cost_estimate=step_cost(members, cells, frames, width),
    )(place, *args)
    return [moved, tail], keep, send


def whole_squares(part):
    return part[SUM_ROWS : SUM_ROWS + 2, :] + part[SUM_ROWS + 2 : SUM_ROWS + 4, :]


def packed_squares(total):
    return split_squares(whole_squares(total), 8).astype(BF16)


def join_kernel(keep_ref, got_ref, out_ref):
    out_ref[:, 0:SUM_ROWS, :] = (
        keep_ref[:, 0:SUM_ROWS, :].astype(F32) + got_ref[:, 0:SUM_ROWS, :].astype(F32)
    ).astype(BF16)
    tail = keep_ref[0].astype(F32) + got_ref[0].astype(F32)
    packed = packed_squares(tail)
    for j in range(PARTS):
        out_ref[j, SUM_ROWS:PART_ROWS, :] = packed


def group_kernel(in_ref, out_ref):
    total = in_ref[0].astype(F32)
    for j in range(1, PARTS):
        total = total + in_ref[j].astype(F32)
    out_ref[0:SUM_ROWS, :] = total[0:SUM_ROWS, :].astype(BF16)
    out_ref[SUM_ROWS:PART_ROWS, :] = packed_squares(total)


def add_kernel(own_ref, got_ref, out_ref):
    total = own_ref[...].astype(F32) + got_ref[...].astype(F32)
    out_ref[0:SUM_ROWS, :] = total[0:SUM_ROWS, :].astype(BF16)
    out_ref[SUM_ROWS:PART_ROWS, :] = packed_squares(total)


def reduce_kernel(total_cells, at_ref, own_ref, got_ref, out_ref, shrink_ref, column_ref):
    core, part = core_of(at_ref[0]), part_of(at_ref[0])
    total = own_ref[...].astype(F32) + got_ref[...].astype(F32)
    squares = whole_squares(total)
    shrink = jnp.maximum(0.0, 1.0 - TAU / jnp.sqrt(squares / total_cells + 1e-06))
    shrink_ref[...] = shrink
    for k in range(2):
        column_ref[k * 128 : (k + 1) * 128, :] = jnp.broadcast_to(shrink[k : k + 1, :], (128, 128)).T
    at = pl.multiple_of((part & 3) * PROJ_ROWS, PROJ_ROWS)
    proj = column_ref[pl.ds(at, PROJ_ROWS), :] * total[0:PROJ_ROWS, :] * (1.0 / math.sqrt(total_cells))
    at = pl.multiple_of(part * GRAM_ROWS, GRAM_ROWS)
    lanes = jnp.where(core == 0, shrink[0:1, :], shrink[1:2, :])
    gram = column_ref[pl.ds(at, GRAM_ROWS), :] * total[PROJ_ROWS:SUM_ROWS, :] * lanes * (1.0 / total_cells)
    mine = jnp.concatenate([proj, gram], axis=0).astype(BF16)
    for j in range(PARTS):
        out_ref[j] = mine


def scale_kernel(shrink_ref, *refs):
    out_ref = refs[-1]
    at = 0
    for m_ref in refs[:-1]:
        rows = slice(at, at + m_ref.shape[0])
        at = rows.stop
        for k in range(2):
            lanes = slice(k * 128, (k + 1) * 128)
            out_ref[rows, lanes] = (m_ref[:, lanes].astype(F32) * shrink_ref[k : k + 1, :]).astype(BF16)


def final_kernel(at_ref, own_ref, got_ref, proj_ref, gram_ref):
    core = core_of(at_ref[0])
    members = proj_ref.shape[0]
    for ref, half in ((own_ref, core), (got_ref, 1 - core)):
        for j in range(PARTS):
            tb, m, r = j // 8, (j // 4) % members, j % 4
            at = pl.multiple_of((half * 2 + tb) * 128, 128)
            rows = slice(r * PROJ_ROWS, (r + 1) * PROJ_ROWS)
            proj_ref[m, rows, pl.ds(at, 128)] = ref[j, 0:PROJ_ROWS, :].astype(F32)
            at = pl.multiple_of(half * 128, 128)
            gram_ref[j * GRAM_ROWS : (j + 1) * GRAM_ROWS, pl.ds(at, 128)] = (
                ref[j, PROJ_ROWS:SUM_ROWS, :].astype(F32)
            )


def both_ways(pairs):
    return [p for i, j in pairs for p in ((i, j), (j, i))]


def local(snapshots, coefficients, modes):
    members, levels, rows_x, rows_y, frames = snapshots.shape
    width = modes.shape[3]
    cells = rows_x * rows_y
    local_cells = levels * cells
    n_sx, n_z = lax.axis_size(SX), lax.axis_size(SY)
    total_cells = local_cells * n_sx * n_z
    core = lax.axis_index("c").astype(jnp.int32)
    parity = lax.axis_index("zl").astype(jnp.int32)
    part = lax.axis_index(GROUP).astype(jnp.int32)
    x_at, z_at = lax.axis_index(SX), lax.axis_index(SY)
    place = core + 2 * parity + 4 * part
    for i, end in enumerate((x_at == 0, x_at == n_sx - 1, z_at == 0, z_at == n_z - 1)):
        place = place + end.astype(jnp.int32) * (64 << i)
    place = place.reshape(1)
    series = snapshots.reshape(members, levels, cells, frames)
    swap = [(0, 1), (1, 0)]

    g0, coefficients, x0, edge_b = first_grad(place, modes, coefficients, series)
    got0 = lax.ppermute(g0, "ens", swap)
    xb = lax.ppermute(edge_b, SX, both_ways([(i, (i + 1) % n_sx) for i in range(1, n_sx, 2)]))
    g1, x1 = second_grad(modes, coefficients, series, 1)
    g1, xb = lax.optimization_barrier((g1, xb))
    got1 = lax.ppermute(g1, "ens", swap)
    coefficients, got0, _ = lax.optimization_barrier((coefficients, got0, g1))
    g2, g3, modes, series, edge_a, row_a, row_b = rest_grad(place, modes, coefficients, series, 2)
    got2 = lax.ppermute(g2, "ens", swap)
    got3 = lax.ppermute(g3, "ens", swap)
    got0, row_a, row_b = lax.optimization_barrier((got0, row_a, row_b))
    za = lax.ppermute(row_a, SY, both_ways([(i, i + 1) for i in range(0, n_z, 2)]))
    zb = lax.ppermute(row_b, SY, both_ways([(i, (i + 1) % n_z) for i in range(1, n_z, 2)]))
    got1, edge_a, za, zb = lax.optimization_barrier((got1, edge_a, za, zb))
    xa = lax.ppermute(edge_a, "c", swap)
    moved, keep, send = steps(
        place,
        modes,
        (xa, xb, za, zb),
        (g0, g1, g2, g3),
        (got0, got1, got2, got3),
        (x0, x1, series, series),
    )

    part_shape = jax.ShapeDtypeStruct((PARTS, PART_ROWS, 128), BF16)
    other = lax.ppermute(send, "c", swap)
    joined = pl.pallas_call(
        join_kernel, in_specs=[VM, VM], out_specs=VM, out_shape=part_shape, compiler_params=PARAMS
    )(keep, other)
    parts = lax.all_to_all(joined, GROUP, 0, 0)
    line_shape = jax.ShapeDtypeStruct((PART_ROWS, 128), BF16)
    line = pl.pallas_call(
        group_kernel, in_specs=[VM], out_specs=VM, out_shape=line_shape, compiler_params=PARAMS
    )(parts)
    pairs = lax.axis_size("zh")
    near = lax.ppermute(line, "zh", [(i, i ^ 1) for i in range(pairs)])
    line = pl.pallas_call(
        add_kernel, in_specs=[VM, VM], out_specs=VM, out_shape=line_shape, compiler_params=PARAMS
    )(line, near)
    near = lax.ppermute(line, "zh", [(i, i ^ 3) for i in range(pairs)])
    spread, shrink = pl.pallas_call(
        functools.partial(reduce_kernel, total_cells),
        in_specs=[SM, VM, VM],
        out_specs=[VM, VM],
        out_shape=[
            jax.ShapeDtypeStruct((PARTS, SUM_ROWS, 128), BF16),
            jax.ShapeDtypeStruct((2, 128), F32),
        ],
        scratch_shapes=[pltpu.VMEM((width, 128), F32)],
        compiler_params=PARAMS,
    )(place, line, near)
    half = lax.all_to_all(spread, GROUP, 0, 0)
    new_modes = pl.pallas_call(
        scale_kernel,
        in_specs=[VM] * (1 + len(moved)),
        out_specs=VM,
        out_shape=jax.ShapeDtypeStruct((local_cells, width), BF16),
        compiler_params=PARAMS,
    )(shrink, *moved)
    half, new_modes = lax.optimization_barrier((half, new_modes))
    other_half = lax.ppermute(half, "c", swap)
    projected, gram = pl.pallas_call(
        final_kernel,
        in_specs=[SM, VM, VM],
        out_specs=[VM, VM],
        out_shape=[
            jax.ShapeDtypeStruct((members, width, frames), F32),
            jax.ShapeDtypeStruct((width, width), F32),
        ],
        compiler_params=PARAMS,
    )(place, half, other_half)
    return (new_modes.reshape(levels, rows_x, rows_y, width), gram, projected)


def solution(mesh):
    ens, n_sx, n_sy = (mesh.shape[a] for a in ("ens", "sx", "sy"))
    fine = Mesh(mesh.devices.reshape(ens, 2, n_sx // 4, 2, n_sy // 2, 2), ("ens", *SX, *SY))
    in_specs = (P("ens", None, SX, SY, None), P("ens", None, None), P(None, SX, SY, None))
    out_specs = (P(None, SX, SY, None), P(), P("ens", None, None))
    return jax.shard_map(local, mesh=fine, in_specs=in_specs, out_specs=out_specs, check_vma=False)
```

```python
import functools
import math

import jax
import jax.numpy as jnp
from jax import lax
from jax.experimental import pallas as pl
from jax.experimental.pallas import tpu as pltpu
from jax.sharding import Mesh, PartitionSpec as P

ETA = 0.25
LAM = 0.5
TAU = 0.4

F32 = jnp.float32
BF16 = jnp.bfloat16
VMEM_LIMIT = 40 * 1024 * 1024
PARAMS = pltpu.CompilerParams(vmem_limit_bytes=VMEM_LIMIT)

SX = ("xh", "y", "c")
SY = ("zh", "zl")
GROUP = ("xh", "y", "zl")
PARTS = 16
PROJ_ROWS = 64
GRAM_ROWS = 16
SUM_ROWS = PROJ_ROWS + GRAM_ROWS
PART_ROWS = SUM_ROWS + 8

VM = pl.BlockSpec(memory_space=pltpu.VMEM)
SM = pl.BlockSpec(memory_space=pltpu.SMEM)
HBM = pl.BlockSpec(memory_space=pltpu.HBM)


def core_of(place):
    return place & 1


def parity_of(place):
    return (place >> 1) & 1


def part_of(place):
    return (place >> 2) & 15


def at_end(place, which):
    return ((place >> (6 + which)) & 1) == 1


def gradient(m, coefficients, series):
    acc = None
    for e in range(len(coefficients)):
        c = coefficients[e]()
        fitted = jnp.dot(m, c, preferred_element_type=F32)
        misfit = (fitted - series[e]().astype(F32)).astype(BF16)
        term = lax.dot_general(misfit, c, (((1,), (1,)), ((), ())), preferred_element_type=F32)
        acc = term if acc is None else acc + term
    return acc.astype(BF16)


def start_all(copies, sems):
    copies = [pltpu.make_async_copy(s, d, sems.at[i]) for i, (s, d) in enumerate(copies)]
    for copy in copies:
        copy.start()
    return copies


def after(copy, ref, *at):
    def load():
        copy.wait()
        return ref[at].reshape(-1, ref.shape[-1])

    return load


def first_grad_kernel(at_ref, m_hbm, c_hbm, x_hbm, g_ref, c_ref, x_ref, xb_ref, m_ref, sems):
    members = c_hbm.shape[0]
    last = m_hbm.shape[1] - 1
    copies = [(m_hbm.at[0], m_ref)]
    for e in range(members):
        copies.append((c_hbm.at[e], c_ref.at[e]))
        copies.append((x_hbm.at[e, 0], x_ref.at[e]))
    copies.append((m_hbm.at[:, last * core_of(at_ref[0])], xb_ref))
    copies = start_all(copies, sems)
    copies[0].wait()
    g_ref[...] = gradient(
        m_ref[...].reshape(g_ref.shape),
        [after(copies[1 + 2 * e], c_ref, e) for e in range(members)],
        [after(copies[2 + 2 * e], x_ref, e) for e in range(members)],
    )
    copies[-1].wait()


def second_grad_kernel(level, m_hbm, c_ref, x_hbm, g_ref, x_ref, m_ref, sems):
    members = c_ref.shape[0]
    copies = [(m_hbm.at[level], m_ref)]
    for e in range(members):
        copies.append((x_hbm.at[e, level], x_ref.at[e]))
    copies = start_all(copies, sems)
    copies[0].wait()
    g_ref[...] = gradient(
        m_ref[...].reshape(g_ref.shape),
        [functools.partial(c_ref.__getitem__, e) for e in range(members)],
        [after(copies[1 + e], x_ref, e) for e in range(members)],
    )


def rest_grad_kernel(begin, at_ref, m_hbm, c_ref, x_hbm, *refs):
    *g_refs, m_ref, x_ref, xa_ref, za_ref, zb_ref, tmp_ref, sems = refs
    members, levels, cells, _ = x_hbm.shape
    _, rows_x, rows_y, width = m_ref.shape
    copies = [(m_hbm, m_ref)]
    for level in range(begin, levels):
        for e in range(members):
            copies.append((x_hbm.at[e, level], x_ref.at[e, level - begin]))
    copies = start_all(copies, sems)
    copies[0].wait()
    core, even = core_of(at_ref[0]), parity_of(at_ref[0]) == 0
    xa_ref[...] = m_ref[:, (rows_x - 1) * (1 - core)]
    tmp_ref[0] = m_ref[:, :, 0:8, :].reshape(levels * rows_x, 8, width).astype(F32)
    tmp_ref[1] = m_ref[:, :, rows_y - 8 : rows_y, :].reshape(levels * rows_x, 8, width).astype(F32)
    lo, hi = tmp_ref[0, :, 0, :], tmp_ref[1, :, 7, :]
    za_ref[...] = jnp.where(even, hi, lo).astype(BF16)
    zb_ref[...] = jnp.where(even, lo, hi).astype(BF16)
    for i, g_ref in enumerate(g_refs):
        g_ref[...] = gradient(
            m_ref[begin + i].reshape(g_ref.shape),
            [functools.partial(c_ref.__getitem__, e) for e in range(members)],
            [after(copies[1 + i * members + e], x_ref, e, i) for e in range(members)],
        )


def grad_cost(members, cells, frames, width):
    return pl.CostEstimate(
        flops=4 * members * cells * frames * width,
        bytes_accessed=2 * cells * (2 * width + members * frames) + 2 * members * width * frames,
        transcendentals=0,
    )


def in_hbm(array):
    return pltpu.with_memory_space_constraint(array, pltpu.HBM)


def first_grad(place, modes, coefficients, series):
    members, _, cells, frames = series.shape
    levels, rows_x, rows_y, width = modes.shape
    outs = [
        jax.ShapeDtypeStruct((cells, width), BF16),
        pltpu.VMEM(coefficients.shape, BF16),
        pltpu.VMEM((members, cells, frames), BF16),
        jax.ShapeDtypeStruct((levels, rows_y, width), BF16),
    ]
    return pl.pallas_call(
        first_grad_kernel,
        in_specs=[SM] + [HBM] * 3,
        out_specs=[VM] * len(outs),
        out_shape=outs,
        scratch_shapes=[
            pltpu.VMEM((rows_x, rows_y, width), BF16),
            pltpu.SemaphoreType.DMA((2 + 2 * members,)),
        ],
        compiler_params=PARAMS,
        cost_estimate=grad_cost(members, cells, frames, width),
    )(place, in_hbm(modes), in_hbm(coefficients), in_hbm(series))


def second_grad(modes, coefficients, series, level):
    members, _, cells, frames = series.shape
    _, rows_x, rows_y, width = modes.shape
    outs = [jax.ShapeDtypeStruct((cells, width), BF16), pltpu.VMEM((members, cells, frames), BF16)]
    return pl.pallas_call(
        functools.partial(second_grad_kernel, level),
        in_specs=[HBM, VM, HBM],
        out_specs=[VM] * len(outs),
        out_shape=outs,
        scratch_shapes=[
            pltpu.VMEM((rows_x, rows_y, width), BF16),
            pltpu.SemaphoreType.DMA((1 + members,)),
        ],
        compiler_params=PARAMS,
        cost_estimate=grad_cost(members, cells, frames, width),
    )(in_hbm(modes), coefficients, in_hbm(series))


def rest_grad(place, modes, coefficients, series, begin):
    members, levels, cells, frames = series.shape
    _, rows_x, rows_y, width = modes.shape
    count = levels - begin
    outs = [jax.ShapeDtypeStruct((cells, width), BF16)] * count
    outs += [
        pltpu.VMEM(modes.shape, BF16),
        pltpu.VMEM((members, count, cells, frames), BF16),
        jax.ShapeDtypeStruct((levels, rows_y, width), BF16),
        jax.ShapeDtypeStruct((levels * rows_x, width), BF16),
        jax.ShapeDtypeStruct((levels * rows_x, width), BF16),
    ]
    return pl.pallas_call(
        functools.partial(rest_grad_kernel, begin),
        in_specs=[SM, HBM, VM, HBM],
        out_specs=[VM] * len(outs),
        out_shape=outs,
        scratch_shapes=[
            pltpu.VMEM((2, levels * rows_x, 8, width), F32),
            pltpu.SemaphoreType.DMA((1 + members * count,)),
        ],
        compiler_params=PARAMS,
        cost_estimate=grad_cost(members, count * cells, frames, width),
    )(place, in_hbm(modes), coefficients, in_hbm(series))


def base_of(level, place, m_ref, xa_ref, xb_ref, za_ref, zb_ref):
    _, rows_x, rows_y, width = m_ref.shape
    lower, even = core_of(place) == 0, parity_of(place) == 0
    shape = (rows_x, rows_y, width)
    f = m_ref[level].astype(F32)
    xa, xb = xa_ref[level : level + 1].astype(F32), xb_ref[level : level + 1].astype(F32)
    rows = slice(level * rows_x, (level + 1) * rows_x)
    za, zb = za_ref[rows, :].astype(F32), zb_ref[rows, :].astype(F32)
    xlo = jnp.where(at_end(place, 0), 0.0, jnp.where(lower, xb, xa))
    xhi = jnp.where(at_end(place, 1), 0.0, jnp.where(lower, xa, xb))
    zlo = jnp.where(at_end(place, 2), 0.0, jnp.where(even, zb, za))
    zhi = jnp.where(at_end(place, 3), 0.0, jnp.where(even, za, zb))
    up = jnp.concatenate([xlo, f[:-1]], axis=0)
    down = jnp.concatenate([f[1:], xhi], axis=0)
    at = lax.broadcasted_iota(jnp.int32, shape, 1)
    left = jnp.where(at == 0, jnp.broadcast_to(zlo[:, None, :], shape), pltpu.roll(f, 1, 1))
    right = jnp.where(
        at == rows_y - 1, jnp.broadcast_to(zhi[:, None, :], shape), pltpu.roll(f, rows_y - 1, 1)
    )
    bent = 4.0 * f - (down + up + right + left)
    return (f - (ETA * LAM) * bent).reshape(rows_x * rows_y, width)


def split_squares(squares, rows):
    high = squares.astype(BF16).astype(F32)
    return jnp.concatenate([high, squares - high, jnp.zeros((rows - 4, 128), F32)], axis=0)


def emit(out_ref, half, proj_ref, gram_ref, squares):
    members = proj_ref.shape[0]
    for j in range(PARTS):
        tb, m, r = j // 8, (j // 4) % members, j % 4
        at = pl.multiple_of((half * 2 + tb) * 128, 128)
        block = proj_ref[m, r * PROJ_ROWS : (r + 1) * PROJ_ROWS, pl.ds(at, 128)]
        out_ref[j, 0:PROJ_ROWS, :] = block.astype(BF16)
        at = pl.multiple_of(half * 128, 128)
        block = gram_ref[j * GRAM_ROWS : (j + 1) * GRAM_ROWS, pl.ds(at, 128)]
        out_ref[j, PROJ_ROWS:SUM_ROWS, :] = block.astype(BF16)
        out_ref[j, SUM_ROWS:PART_ROWS, :] = squares


def move(base, own_ref, got_ref):
    grad = own_ref[...].astype(F32) + got_ref[...].astype(F32)
    moved = (base - ETA * grad).astype(BF16)
    wide = moved.astype(F32)
    return moved, jnp.sum(wide * wide, axis=0, keepdims=True)


def most_kernel(at_ref, m_ref, xa_ref, xb_ref, za_ref, zb_ref, *refs):
    *refs, base_ref, moved_ref, proj_ref, gram_ref, squares_ref = refs
    halos = (xa_ref, xb_ref, za_ref, zb_ref)
    count = len(refs) // 3
    owns, gots, xs = refs[:count], refs[count : 2 * count], refs[2 * count :]
    squares = None
    for level in range(count):
        moved, part = move(base_of(level, at_ref[0], m_ref, *halos), owns[level], gots[level])
        squares = part if level == 0 else squares + part
        moved_ref[level * moved.shape[0] : (level + 1) * moved.shape[0], :] = moved
        turned = moved.T
        gram = jnp.dot(turned, moved, preferred_element_type=F32)
        gram_ref[...] = gram if level == 0 else gram_ref[...] + gram
        for e in range(proj_ref.shape[0]):
            x = xs[level][e] if len(xs[level].shape) == 3 else xs[level][e, 0]
            proj = jnp.dot(turned, x, preferred_element_type=F32)
            proj_ref[e] = proj if level == 0 else proj_ref[e] + proj
    squares_ref[...] = squares
    base_ref[...] = base_of(count, at_ref[0], m_ref, *halos)


def last_kernel(at_ref, base_ref, own_ref, got_ref, x_ref, proj_in, gram_in, squares_in, *refs):
    moved_ref, keep_ref, send_ref, proj_ref, gram_ref = refs
    moved, squares = move(base_ref[...], own_ref, got_ref)
    moved_ref[...] = moved
    squares = squares + squares_in[...]
    turned = moved.T
    gram_ref[...] = gram_in[...] + jnp.dot(turned, moved, preferred_element_type=F32)
    for e in range(proj_ref.shape[0]):
        proj = jnp.dot(turned, x_ref[e, x_ref.shape[1] - 1], preferred_element_type=F32)
        proj_ref[e] = proj_in[e] + proj
    core = core_of(at_ref[0])
    pair = jnp.concatenate([squares[:, 0:128], squares[:, 128:256]], axis=0)
    packed = split_squares(pair, 8).astype(BF16)
    emit(send_ref, 1 - core, proj_ref, gram_ref, packed)
    emit(keep_ref, core, proj_ref, gram_ref, packed)


def step_cost(members, cells, frames, width):
    return pl.CostEstimate(
        flops=2 * cells * width * (width + members * frames),
        bytes_accessed=2 * cells * (4 * width + members * frames),
        transcendentals=0,
    )


def steps(place, modes, halos, owns, gots, series):
    members, frames = series[0].shape[0], series[0].shape[-1]
    cells, width = owns[0].shape
    most = len(owns) - 1
    sums = [
        jax.ShapeDtypeStruct((members, width, frames), F32),
        jax.ShapeDtypeStruct((width, width), F32),
        jax.ShapeDtypeStruct((1, width), F32),
    ]
    args = [modes, *halos, *owns[:most], *gots[:most], *series[:most]]
    base, moved, *carry = pl.pallas_call(
        most_kernel,
        in_specs=[SM] + [VM] * len(args),
        out_specs=[VM] * 5,
        out_shape=[
            jax.ShapeDtypeStruct((cells, width), F32),
            jax.ShapeDtypeStruct((most * cells, width), BF16),
            *sums,
        ],
        compiler_params=PARAMS,
        cost_estimate=step_cost(members, most * cells, frames, width),
    )(place, *args)
    args = [base, owns[most], gots[most], series[most], *carry]
    tail, keep, send = pl.pallas_call(
        last_kernel,
        in_specs=[SM] + [VM] * len(args),
        out_specs=[VM] * 3,
        out_shape=[jax.ShapeDtypeStruct((cells, width), BF16)]
        + [jax.ShapeDtypeStruct((PARTS, PART_ROWS, 128), BF16)] * 2,
        scratch_shapes=[pltpu.VMEM(s.shape, F32) for s in sums[:2]],
        compiler_params=PARAMS,
        cost_estimate=step_cost(members, cells, frames, width),
    )(place, *args)
    return [moved, tail], keep, send


def whole_squares(part):
    return part[SUM_ROWS : SUM_ROWS + 2, :] + part[SUM_ROWS + 2 : SUM_ROWS + 4, :]


def packed_squares(total):
    return split_squares(whole_squares(total), 8).astype(BF16)


def join_kernel(keep_ref, got_ref, out_ref):
    out_ref[:, 0:SUM_ROWS, :] = (
        keep_ref[:, 0:SUM_ROWS, :].astype(F32) + got_ref[:, 0:SUM_ROWS, :].astype(F32)
    ).astype(BF16)
    tail = keep_ref[0].astype(F32) + got_ref[0].astype(F32)
    packed = packed_squares(tail)
    for j in range(PARTS):
        out_ref[j, SUM_ROWS:PART_ROWS, :] = packed


def group_kernel(in_ref, out_ref):
    total = in_ref[0].astype(F32)
    for j in range(1, PARTS):
        total = total + in_ref[j].astype(F32)
    out_ref[0:SUM_ROWS, :] = total[0:SUM_ROWS, :].astype(BF16)
    out_ref[SUM_ROWS:PART_ROWS, :] = packed_squares(total)


def add_kernel(own_ref, got_ref, out_ref):
    total = own_ref[...].astype(F32) + got_ref[...].astype(F32)
    out_ref[0:SUM_ROWS, :] = total[0:SUM_ROWS, :].astype(BF16)
    out_ref[SUM_ROWS:PART_ROWS, :] = packed_squares(total)


def reduce_kernel(total_cells, at_ref, own_ref, got_ref, out_ref, shrink_ref, column_ref):
    core, part = core_of(at_ref[0]), part_of(at_ref[0])
    total = own_ref[...].astype(F32) + got_ref[...].astype(F32)
    squares = whole_squares(total)
    shrink = jnp.maximum(0.0, 1.0 - TAU / jnp.sqrt(squares / total_cells + 1e-06))
    shrink_ref[...] = shrink
    for k in range(2):
        column_ref[k * 128 : (k + 1) * 128, :] = jnp.broadcast_to(shrink[k : k + 1, :], (128, 128)).T
    at = pl.multiple_of((part & 3) * PROJ_ROWS, PROJ_ROWS)
    proj = column_ref[pl.ds(at, PROJ_ROWS), :] * total[0:PROJ_ROWS, :] * (1.0 / math.sqrt(total_cells))
    at = pl.multiple_of(part * GRAM_ROWS, GRAM_ROWS)
    lanes = jnp.where(core == 0, shrink[0:1, :], shrink[1:2, :])
    gram = column_ref[pl.ds(at, GRAM_ROWS), :] * total[PROJ_ROWS:SUM_ROWS, :] * lanes * (1.0 / total_cells)
    mine = jnp.concatenate([proj, gram], axis=0).astype(BF16)
    for j in range(PARTS):
        out_ref[j] = mine


def scale_kernel(shrink_ref, *refs):
    out_ref = refs[-1]
    at = 0
    for m_ref in refs[:-1]:
        rows = slice(at, at + m_ref.shape[0])
        at = rows.stop
        for k in range(2):
            lanes = slice(k * 128, (k + 1) * 128)
            out_ref[rows, lanes] = (m_ref[:, lanes].astype(F32) * shrink_ref[k : k + 1, :]).astype(BF16)


def final_kernel(at_ref, own_ref, got_ref, proj_ref, gram_ref):
    core = core_of(at_ref[0])
    members = proj_ref.shape[0]
    for ref, half in ((own_ref, core), (got_ref, 1 - core)):
        for j in range(PARTS):
            tb, m, r = j // 8, (j // 4) % members, j % 4
            at = pl.multiple_of((half * 2 + tb) * 128, 128)
            rows = slice(r * PROJ_ROWS, (r + 1) * PROJ_ROWS)
            proj_ref[m, rows, pl.ds(at, 128)] = ref[j, 0:PROJ_ROWS, :].astype(F32)
            at = pl.multiple_of(half * 128, 128)
            gram_ref[j * GRAM_ROWS : (j + 1) * GRAM_ROWS, pl.ds(at, 128)] = (
                ref[j, PROJ_ROWS:SUM_ROWS, :].astype(F32)
            )


def both_ways(pairs):
    return [p for i, j in pairs for p in ((i, j), (j, i))]


def local(snapshots, coefficients, modes):
    members, levels, rows_x, rows_y, frames = snapshots.shape
    width = modes.shape[3]
    cells = rows_x * rows_y
    local_cells = levels * cells
    n_sx, n_z = lax.axis_size(SX), lax.axis_size(SY)
    total_cells = local_cells * n_sx * n_z
    core = lax.axis_index("c").astype(jnp.int32)
    parity = lax.axis_index("zl").astype(jnp.int32)
    part = lax.axis_index(GROUP).astype(jnp.int32)
    x_at, z_at = lax.axis_index(SX), lax.axis_index(SY)
    place = core + 2 * parity + 4 * part
    for i, end in enumerate((x_at == 0, x_at == n_sx - 1, z_at == 0, z_at == n_z - 1)):
        place = place + end.astype(jnp.int32) * (64 << i)
    place = place.reshape(1)
    series = snapshots.reshape(members, levels, cells, frames)
    swap = [(0, 1), (1, 0)]

    g0, coefficients, x0, edge_b = first_grad(place, modes, coefficients, series)
    got0 = lax.ppermute(g0, "ens", swap)
    xb = lax.ppermute(edge_b, SX, both_ways([(i, (i + 1) % n_sx) for i in range(1, n_sx, 2)]))
    g1, x1 = second_grad(modes, coefficients, series, 1)
    got1 = lax.ppermute(g1, "ens", swap)
    coefficients, _ = lax.optimization_barrier((coefficients, g1))
    g2, g3, modes, series, edge_a, row_a, row_b = rest_grad(place, modes, coefficients, series, 2)
    got2 = lax.ppermute(g2, "ens", swap)
    got3 = lax.ppermute(g3, "ens", swap)
    got0, xb, row_a, row_b = lax.optimization_barrier((got0, xb, row_a, row_b))
    za = lax.ppermute(row_a, SY, both_ways([(i, i + 1) for i in range(0, n_z, 2)]))
    zb = lax.ppermute(row_b, SY, both_ways([(i, (i + 1) % n_z) for i in range(1, n_z, 2)]))
    got1, edge_a, za, zb = lax.optimization_barrier((got1, edge_a, za, zb))
    xa = lax.ppermute(edge_a, "c", swap)
    moved, keep, send = steps(
        place,
        modes,
        (xa, xb, za, zb),
        (g0, g1, g2, g3),
        (got0, got1, got2, got3),
        (x0, x1, series, series),
    )

    part_shape = jax.ShapeDtypeStruct((PARTS, PART_ROWS, 128), BF16)
    other = lax.ppermute(send, "c", swap)
    joined = pl.pallas_call(
        join_kernel, in_specs=[VM, VM], out_specs=VM, out_shape=part_shape, compiler_params=PARAMS
    )(keep, other)
    parts = lax.all_to_all(joined, GROUP, 0, 0)
    line_shape = jax.ShapeDtypeStruct((PART_ROWS, 128), BF16)
    line = pl.pallas_call(
        group_kernel, in_specs=[VM], out_specs=VM, out_shape=line_shape, compiler_params=PARAMS
    )(parts)
    pairs = lax.axis_size("zh")
    near = lax.ppermute(line, "zh", [(i, i ^ 1) for i in range(pairs)])
    line = pl.pallas_call(
        add_kernel, in_specs=[VM, VM], out_specs=VM, out_shape=line_shape, compiler_params=PARAMS
    )(line, near)
    near = lax.ppermute(line, "zh", [(i, i ^ 3) for i in range(pairs)])
    spread, shrink = pl.pallas_call(
        functools.partial(reduce_kernel, total_cells),
        in_specs=[SM, VM, VM],
        out_specs=[VM, VM],
        out_shape=[
            jax.ShapeDtypeStruct((PARTS, SUM_ROWS, 128), BF16),
            jax.ShapeDtypeStruct((2, 128), F32),
        ],
        scratch_shapes=[pltpu.VMEM((width, 128), F32)],
        compiler_params=PARAMS,
    )(place, line, near)
    half = lax.all_to_all(spread, GROUP, 0, 0)
    new_modes = pl.pallas_call(
        scale_kernel,
        in_specs=[VM] * (1 + len(moved)),
        out_specs=VM,
        out_shape=jax.ShapeDtypeStruct((local_cells, width), BF16),
        compiler_params=PARAMS,
    )(shrink, *moved)
    half, new_modes = lax.optimization_barrier((half, new_modes))
    other_half = lax.ppermute(half, "c", swap)
    projected, gram = pl.pallas_call(
        final_kernel,
        in_specs=[SM, VM, VM],
        out_specs=[VM, VM],
        out_shape=[
            jax.ShapeDtypeStruct((members, width, frames), F32),
            jax.ShapeDtypeStruct((width, width), F32),
        ],
        compiler_params=PARAMS,
    )(place, half, other_half)
    return (new_modes.reshape(levels, rows_x, rows_y, width), gram, projected)


def solution(mesh):
    ens, n_sx, n_sy = (mesh.shape[a] for a in ("ens", "sx", "sy"))
    fine = Mesh(mesh.devices.reshape(ens, 2, n_sx // 4, 2, n_sy // 2, 2), ("ens", *SX, *SY))
    in_specs = (P("ens", None, SX, SY, None), P("ens", None, None), P(None, SX, SY, None))
    out_specs = (P(None, SX, SY, None), P(), P("ens", None, None))
    return jax.shard_map(local, mesh=fine, in_specs=in_specs, out_specs=out_specs, check_vma=False)
```

```python
import functools
import math

import jax
import jax.numpy as jnp
from jax import lax
from jax.experimental import pallas as pl
from jax.experimental.pallas import tpu as pltpu
from jax.sharding import Mesh, PartitionSpec as P

ETA = 0.25
LAM = 0.5
TAU = 0.4

F32 = jnp.float32
BF16 = jnp.bfloat16
VMEM_LIMIT = 40 * 1024 * 1024
PARAMS = pltpu.CompilerParams(vmem_limit_bytes=VMEM_LIMIT)

SX = ("xh", "y", "c")
SY = ("zh", "zl")
GROUP = ("xh", "y", "zl")
PARTS = 16
PROJ_ROWS = 64
GRAM_ROWS = 16
SUM_ROWS = PROJ_ROWS + GRAM_ROWS
PART_ROWS = SUM_ROWS + 8

VM = pl.BlockSpec(memory_space=pltpu.VMEM)
SM = pl.BlockSpec(memory_space=pltpu.SMEM)
HBM = pl.BlockSpec(memory_space=pltpu.HBM)


def core_of(place):
    return place & 1


def parity_of(place):
    return (place >> 1) & 1


def part_of(place):
    return (place >> 2) & 15


def at_end(place, which):
    return ((place >> (6 + which)) & 1) == 1


def gradient(m, coefficients, series):
    acc = None
    for e in range(len(coefficients)):
        c = coefficients[e]()
        fitted = jnp.dot(m, c, preferred_element_type=F32)
        misfit = (fitted - series[e]().astype(F32)).astype(BF16)
        term = lax.dot_general(misfit, c, (((1,), (1,)), ((), ())), preferred_element_type=F32)
        acc = term if acc is None else acc + term
    return acc.astype(BF16)


def start_all(copies, sems):
    copies = [pltpu.make_async_copy(s, d, sems.at[i]) for i, (s, d) in enumerate(copies)]
    for copy in copies:
        copy.start()
    return copies


def after(copy, ref, *at):
    def load():
        copy.wait()
        return ref[at].reshape(-1, ref.shape[-1])

    return load


def first_grad_kernel(at_ref, m_hbm, c_hbm, x_hbm, g_ref, c_ref, x_ref, xb_ref, m_ref, sems):
    members = c_hbm.shape[0]
    last = m_hbm.shape[1] - 1
    copies = [(m_hbm.at[0], m_ref)]
    for e in range(members):
        copies.append((c_hbm.at[e], c_ref.at[e]))
        copies.append((x_hbm.at[e, 0], x_ref.at[e]))
    copies.append((m_hbm.at[:, last * core_of(at_ref[0])], xb_ref))
    copies = start_all(copies, sems)
    copies[0].wait()
    g_ref[...] = gradient(
        m_ref[...].reshape(g_ref.shape),
        [after(copies[1 + 2 * e], c_ref, e) for e in range(members)],
        [after(copies[2 + 2 * e], x_ref, e) for e in range(members)],
    )
    copies[-1].wait()


def second_grad_kernel(level, m_hbm, c_ref, x_hbm, g_ref, x_ref, m_ref, sems):
    members = c_ref.shape[0]
    copies = [(m_hbm.at[level], m_ref)]
    for e in range(members):
        copies.append((x_hbm.at[e, level], x_ref.at[e]))
    copies = start_all(copies, sems)
    copies[0].wait()
    g_ref[...] = gradient(
        m_ref[...].reshape(g_ref.shape),
        [functools.partial(c_ref.__getitem__, e) for e in range(members)],
        [after(copies[1 + e], x_ref, e) for e in range(members)],
    )


def rest_grad_kernel(begin, at_ref, m_hbm, c_ref, x_hbm, *refs):
    *g_refs, m_ref, x_ref, xa_ref, za_ref, zb_ref, tmp_ref, sems = refs
    members, levels, cells, _ = x_hbm.shape
    _, rows_x, rows_y, width = m_ref.shape
    copies = [(m_hbm, m_ref)]
    for level in range(begin, levels):
        for e in range(members):
            copies.append((x_hbm.at[e, level], x_ref.at[e, level - begin]))
    copies = start_all(copies, sems)
    copies[0].wait()
    core, even = core_of(at_ref[0]), parity_of(at_ref[0]) == 0
    xa_ref[...] = m_ref[:, (rows_x - 1) * (1 - core)]
    tmp_ref[0] = m_ref[:, :, 0:8, :].reshape(levels * rows_x, 8, width).astype(F32)
    tmp_ref[1] = m_ref[:, :, rows_y - 8 : rows_y, :].reshape(levels * rows_x, 8, width).astype(F32)
    lo, hi = tmp_ref[0, :, 0, :], tmp_ref[1, :, 7, :]
    za_ref[...] = jnp.where(even, hi, lo).astype(BF16)
    zb_ref[...] = jnp.where(even, lo, hi).astype(BF16)
    for i, g_ref in enumerate(g_refs):
        g_ref[...] = gradient(
            m_ref[begin + i].reshape(g_ref.shape),
            [functools.partial(c_ref.__getitem__, e) for e in range(members)],
            [after(copies[1 + i * members + e], x_ref, e, i) for e in range(members)],
        )


def grad_cost(members, cells, frames, width):
    return pl.CostEstimate(
        flops=4 * members * cells * frames * width,
        bytes_accessed=2 * cells * (2 * width + members * frames) + 2 * members * width * frames,
        transcendentals=0,
    )


def in_hbm(array):
    return pltpu.with_memory_space_constraint(array, pltpu.HBM)


def first_grad(place, modes, coefficients, series):
    members, _, cells, frames = series.shape
    levels, rows_x, rows_y, width = modes.shape
    outs = [
        jax.ShapeDtypeStruct((cells, width), BF16),
        pltpu.VMEM(coefficients.shape, BF16),
        pltpu.VMEM((members, cells, frames), BF16),
        jax.ShapeDtypeStruct((levels, rows_y, width), BF16),
    ]
    return pl.pallas_call(
        first_grad_kernel,
        in_specs=[SM] + [HBM] * 3,
        out_specs=[VM] * len(outs),
        out_shape=outs,
        scratch_shapes=[
            pltpu.VMEM((rows_x, rows_y, width), BF16),
            pltpu.SemaphoreType.DMA((2 + 2 * members,)),
        ],
        compiler_params=PARAMS,
        cost_estimate=grad_cost(members, cells, frames, width),
    )(place, in_hbm(modes), in_hbm(coefficients), in_hbm(series))


def second_grad(modes, coefficients, series, level):
    members, _, cells, frames = series.shape
    _, rows_x, rows_y, width = modes.shape
    outs = [jax.ShapeDtypeStruct((cells, width), BF16), pltpu.VMEM((members, cells, frames), BF16)]
    return pl.pallas_call(
        functools.partial(second_grad_kernel, level),
        in_specs=[HBM, VM, HBM],
        out_specs=[VM] * len(outs),
        out_shape=outs,
        scratch_shapes=[
            pltpu.VMEM((rows_x, rows_y, width), BF16),
            pltpu.SemaphoreType.DMA((1 + members,)),
        ],
        compiler_params=PARAMS,
        cost_estimate=grad_cost(members, cells, frames, width),
    )(in_hbm(modes), coefficients, in_hbm(series))


def rest_grad(place, modes, coefficients, series, begin):
    members, levels, cells, frames = series.shape
    _, rows_x, rows_y, width = modes.shape
    count = levels - begin
    outs = [jax.ShapeDtypeStruct((cells, width), BF16)] * count
    outs += [
        pltpu.VMEM(modes.shape, BF16),
        pltpu.VMEM((members, count, cells, frames), BF16),
        jax.ShapeDtypeStruct((levels, rows_y, width), BF16),
        jax.ShapeDtypeStruct((levels * rows_x, width), BF16),
        jax.ShapeDtypeStruct((levels * rows_x, width), BF16),
    ]
    return pl.pallas_call(
        functools.partial(rest_grad_kernel, begin),
        in_specs=[SM, HBM, VM, HBM],
        out_specs=[VM] * len(outs),
        out_shape=outs,
        scratch_shapes=[
            pltpu.VMEM((2, levels * rows_x, 8, width), F32),
            pltpu.SemaphoreType.DMA((1 + members * count,)),
        ],
        compiler_params=PARAMS,
        cost_estimate=grad_cost(members, count * cells, frames, width),
    )(place, in_hbm(modes), coefficients, in_hbm(series))


def base_of(level, place, m_ref, xa_ref, xb_ref, za_ref, zb_ref):
    _, rows_x, rows_y, width = m_ref.shape
    lower, even = core_of(place) == 0, parity_of(place) == 0
    shape = (rows_x, rows_y, width)
    f = m_ref[level].astype(F32)
    xa, xb = xa_ref[level : level + 1].astype(F32), xb_ref[level : level + 1].astype(F32)
    rows = slice(level * rows_x, (level + 1) * rows_x)
    za, zb = za_ref[rows, :].astype(F32), zb_ref[rows, :].astype(F32)
    xlo = jnp.where(at_end(place, 0), 0.0, jnp.where(lower, xb, xa))
    xhi = jnp.where(at_end(place, 1), 0.0, jnp.where(lower, xa, xb))
    zlo = jnp.where(at_end(place, 2), 0.0, jnp.where(even, zb, za))
    zhi = jnp.where(at_end(place, 3), 0.0, jnp.where(even, za, zb))
    up = jnp.concatenate([xlo, f[:-1]], axis=0)
    down = jnp.concatenate([f[1:], xhi], axis=0)
    at = lax.broadcasted_iota(jnp.int32, shape, 1)
    left = jnp.where(at == 0, jnp.broadcast_to(zlo[:, None, :], shape), pltpu.roll(f, 1, 1))
    right = jnp.where(
        at == rows_y - 1, jnp.broadcast_to(zhi[:, None, :], shape), pltpu.roll(f, rows_y - 1, 1)
    )
    bent = 4.0 * f - (down + up + right + left)
    return (f - (ETA * LAM) * bent).reshape(rows_x * rows_y, width)


def split_squares(squares, rows):
    high = squares.astype(BF16).astype(F32)
    return jnp.concatenate([high, squares - high, jnp.zeros((rows - 4, 128), F32)], axis=0)


def emit(out_ref, half, proj_ref, gram_ref, squares):
    members = proj_ref.shape[0]
    for j in range(PARTS):
        tb, m, r = j // 8, (j // 4) % members, j % 4
        at = pl.multiple_of((half * 2 + tb) * 128, 128)
        block = proj_ref[m, r * PROJ_ROWS : (r + 1) * PROJ_ROWS, pl.ds(at, 128)]
        out_ref[j, 0:PROJ_ROWS, :] = block.astype(BF16)
        at = pl.multiple_of(half * 128, 128)
        block = gram_ref[j * GRAM_ROWS : (j + 1) * GRAM_ROWS, pl.ds(at, 128)]
        out_ref[j, PROJ_ROWS:SUM_ROWS, :] = block.astype(BF16)
        out_ref[j, SUM_ROWS:PART_ROWS, :] = squares


def move(base, own_ref, got_ref):
    grad = own_ref[...].astype(F32) + got_ref[...].astype(F32)
    moved = (base - ETA * grad).astype(BF16)
    wide = moved.astype(F32)
    return moved, jnp.sum(wide * wide, axis=0, keepdims=True)


def most_kernel(at_ref, m_ref, xa_ref, xb_ref, za_ref, zb_ref, *refs):
    *refs, base_ref, moved_ref, proj_ref, gram_ref, squares_ref = refs
    halos = (xa_ref, xb_ref, za_ref, zb_ref)
    count = len(refs) // 3
    owns, gots, xs = refs[:count], refs[count : 2 * count], refs[2 * count :]
    squares = None
    for level in range(count):
        moved, part = move(base_of(level, at_ref[0], m_ref, *halos), owns[level], gots[level])
        squares = part if level == 0 else squares + part
        moved_ref[level * moved.shape[0] : (level + 1) * moved.shape[0], :] = moved
        turned = moved.T
        gram = jnp.dot(turned, moved, preferred_element_type=F32)
        gram_ref[...] = gram if level == 0 else gram_ref[...] + gram
        for e in range(proj_ref.shape[0]):
            x = xs[level][e] if len(xs[level].shape) == 3 else xs[level][e, 0]
            proj = jnp.dot(turned, x, preferred_element_type=F32)
            proj_ref[e] = proj if level == 0 else proj_ref[e] + proj
    squares_ref[...] = squares
    base_ref[...] = base_of(count, at_ref[0], m_ref, *halos)


def last_kernel(at_ref, base_ref, own_ref, got_ref, x_ref, proj_in, gram_in, squares_in, *refs):
    moved_ref, keep_ref, send_ref, proj_ref, gram_ref = refs
    moved, squares = move(base_ref[...], own_ref, got_ref)
    moved_ref[...] = moved
    squares = squares + squares_in[...]
    turned = moved.T
    gram_ref[...] = gram_in[...] + jnp.dot(turned, moved, preferred_element_type=F32)
    for e in range(proj_ref.shape[0]):
        proj = jnp.dot(turned, x_ref[e, x_ref.shape[1] - 1], preferred_element_type=F32)
        proj_ref[e] = proj_in[e] + proj
    core = core_of(at_ref[0])
    pair = jnp.concatenate([squares[:, 0:128], squares[:, 128:256]], axis=0)
    packed = split_squares(pair, 8).astype(BF16)
    emit(send_ref, 1 - core, proj_ref, gram_ref, packed)
    emit(keep_ref, core, proj_ref, gram_ref, packed)


def step_cost(members, cells, frames, width):
    return pl.CostEstimate(
        flops=2 * cells * width * (width + members * frames),
        bytes_accessed=2 * cells * (4 * width + members * frames),
        transcendentals=0,
    )


def steps(place, modes, halos, owns, gots, series):
    members, frames = series[0].shape[0], series[0].shape[-1]
    cells, width = owns[0].shape
    most = len(owns) - 1
    sums = [
        jax.ShapeDtypeStruct((members, width, frames), F32),
        jax.ShapeDtypeStruct((width, width), F32),
        jax.ShapeDtypeStruct((1, width), F32),
    ]
    args = [modes, *halos, *owns[:most], *gots[:most], *series[:most]]
    base, moved, *carry = pl.pallas_call(
        most_kernel,
        in_specs=[SM] + [VM] * len(args),
        out_specs=[VM] * 5,
        out_shape=[
            jax.ShapeDtypeStruct((cells, width), F32),
            jax.ShapeDtypeStruct((most * cells, width), BF16),
            *sums,
        ],
        compiler_params=PARAMS,
        cost_estimate=step_cost(members, most * cells, frames, width),
    )(place, *args)
    args = [base, owns[most], gots[most], series[most], *carry]
    tail, keep, send = pl.pallas_call(
        last_kernel,
        in_specs=[SM] + [VM] * len(args),
        out_specs=[VM] * 3,
        out_shape=[jax.ShapeDtypeStruct((cells, width), BF16)]
        + [jax.ShapeDtypeStruct((PARTS, PART_ROWS, 128), BF16)] * 2,
        scratch_shapes=[pltpu.VMEM(s.shape, F32) for s in sums[:2]],
        compiler_params=PARAMS,
        cost_estimate=step_cost(members, cells, frames, width),
    )(place, *args)
    return [moved, tail], keep, send


def whole_squares(part):
    return part[SUM_ROWS : SUM_ROWS + 2, :] + part[SUM_ROWS + 2 : SUM_ROWS + 4, :]


def packed_squares(total):
    return split_squares(whole_squares(total), 8).astype(BF16)


def join_kernel(keep_ref, got_ref, out_ref):
    out_ref[:, 0:SUM_ROWS, :] = (
        keep_ref[:, 0:SUM_ROWS, :].astype(F32) + got_ref[:, 0:SUM_ROWS, :].astype(F32)
    ).astype(BF16)
    tail = keep_ref[0].astype(F32) + got_ref[0].astype(F32)
    packed = packed_squares(tail)
    for j in range(PARTS):
        out_ref[j, SUM_ROWS:PART_ROWS, :] = packed


def group_kernel(in_ref, out_ref):
    total = in_ref[0].astype(F32)
    for j in range(1, PARTS):
        total = total + in_ref[j].astype(F32)
    out_ref[0:SUM_ROWS, :] = total[0:SUM_ROWS, :].astype(BF16)
    out_ref[SUM_ROWS:PART_ROWS, :] = packed_squares(total)


def add_kernel(own_ref, got_ref, out_ref):
    total = own_ref[...].astype(F32) + got_ref[...].astype(F32)
    out_ref[0:SUM_ROWS, :] = total[0:SUM_ROWS, :].astype(BF16)
    out_ref[SUM_ROWS:PART_ROWS, :] = packed_squares(total)


def reduce_kernel(total_cells, at_ref, own_ref, got_ref, out_ref, shrink_ref, column_ref):
    core, part = core_of(at_ref[0]), part_of(at_ref[0])
    total = own_ref[...].astype(F32) + got_ref[...].astype(F32)
    squares = whole_squares(total)
    shrink = jnp.maximum(0.0, 1.0 - TAU / jnp.sqrt(squares / total_cells + 1e-06))
    shrink_ref[...] = shrink
    for k in range(2):
        column_ref[k * 128 : (k + 1) * 128, :] = jnp.broadcast_to(shrink[k : k + 1, :], (128, 128)).T
    at = pl.multiple_of((part & 3) * PROJ_ROWS, PROJ_ROWS)
    proj = column_ref[pl.ds(at, PROJ_ROWS), :] * total[0:PROJ_ROWS, :] * (1.0 / math.sqrt(total_cells))
    at = pl.multiple_of(part * GRAM_ROWS, GRAM_ROWS)
    lanes = jnp.where(core == 0, shrink[0:1, :], shrink[1:2, :])
    gram = column_ref[pl.ds(at, GRAM_ROWS), :] * total[PROJ_ROWS:SUM_ROWS, :] * lanes * (1.0 / total_cells)
    mine = jnp.concatenate([proj, gram], axis=0).astype(BF16)
    for j in range(PARTS):
        out_ref[j] = mine


def scale_kernel(shrink_ref, *refs):
    out_ref = refs[-1]
    at = 0
    for m_ref in refs[:-1]:
        rows = slice(at, at + m_ref.shape[0])
        at = rows.stop
        for k in range(2):
            lanes = slice(k * 128, (k + 1) * 128)
            out_ref[rows, lanes] = (m_ref[:, lanes].astype(F32) * shrink_ref[k : k + 1, :]).astype(BF16)


def final_kernel(at_ref, own_ref, got_ref, proj_ref, gram_ref):
    core = core_of(at_ref[0])
    members = proj_ref.shape[0]
    for ref, half in ((own_ref, core), (got_ref, 1 - core)):
        for j in range(PARTS):
            tb, m, r = j // 8, (j // 4) % members, j % 4
            at = pl.multiple_of((half * 2 + tb) * 128, 128)
            rows = slice(r * PROJ_ROWS, (r + 1) * PROJ_ROWS)
            proj_ref[m, rows, pl.ds(at, 128)] = ref[j, 0:PROJ_ROWS, :].astype(F32)
            at = pl.multiple_of(half * 128, 128)
            gram_ref[j * GRAM_ROWS : (j + 1) * GRAM_ROWS, pl.ds(at, 128)] = (
                ref[j, PROJ_ROWS:SUM_ROWS, :].astype(F32)
            )


def both_ways(pairs):
    return [p for i, j in pairs for p in ((i, j), (j, i))]


def local(snapshots, coefficients, modes):
    members, levels, rows_x, rows_y, frames = snapshots.shape
    width = modes.shape[3]
    cells = rows_x * rows_y
    local_cells = levels * cells
    n_sx, n_z = lax.axis_size(SX), lax.axis_size(SY)
    total_cells = local_cells * n_sx * n_z
    core = lax.axis_index("c").astype(jnp.int32)
    parity = lax.axis_index("zl").astype(jnp.int32)
    part = lax.axis_index(GROUP).astype(jnp.int32)
    x_at, z_at = lax.axis_index(SX), lax.axis_index(SY)
    place = core + 2 * parity + 4 * part
    for i, end in enumerate((x_at == 0, x_at == n_sx - 1, z_at == 0, z_at == n_z - 1)):
        place = place + end.astype(jnp.int32) * (64 << i)
    place = place.reshape(1)
    series = snapshots.reshape(members, levels, cells, frames)
    swap = [(0, 1), (1, 0)]

    g0, coefficients, x0, edge_b = first_grad(place, modes, coefficients, series)
    got0 = lax.ppermute(g0, "ens", swap)
    xb = lax.ppermute(edge_b, SX, both_ways([(i, (i + 1) % n_sx) for i in range(1, n_sx, 2)]))
    g1, x1 = second_grad(modes, coefficients, series, 1)
    got1 = lax.ppermute(g1, "ens", swap)
    coefficients, _ = lax.optimization_barrier((coefficients, g1))
    g2, g3, modes, series, edge_a, row_a, row_b = rest_grad(place, modes, coefficients, series, 2)
    got2 = lax.ppermute(g2, "ens", swap)
    got3 = lax.ppermute(g3, "ens", swap)
    got0, got1, row_a, row_b = lax.optimization_barrier((got0, got1, row_a, row_b))
    za = lax.ppermute(row_a, SY, both_ways([(i, i + 1) for i in range(0, n_z, 2)]))
    zb = lax.ppermute(row_b, SY, both_ways([(i, (i + 1) % n_z) for i in range(1, n_z, 2)]))
    xb, edge_a, za, zb = lax.optimization_barrier((xb, edge_a, za, zb))
    xa = lax.ppermute(edge_a, "c", swap)
    moved, keep, send = steps(
        place,
        modes,
        (xa, xb, za, zb),
        (g0, g1, g2, g3),
        (got0, got1, got2, got3),
        (x0, x1, series, series),
    )

    part_shape = jax.ShapeDtypeStruct((PARTS, PART_ROWS, 128), BF16)
    other = lax.ppermute(send, "c", swap)
    joined = pl.pallas_call(
        join_kernel, in_specs=[VM, VM], out_specs=VM, out_shape=part_shape, compiler_params=PARAMS
    )(keep, other)
    parts = lax.all_to_all(joined, GROUP, 0, 0)
    line_shape = jax.ShapeDtypeStruct((PART_ROWS, 128), BF16)
    line = pl.pallas_call(
        group_kernel, in_specs=[VM], out_specs=VM, out_shape=line_shape, compiler_params=PARAMS
    )(parts)
    pairs = lax.axis_size("zh")
    near = lax.ppermute(line, "zh", [(i, i ^ 1) for i in range(pairs)])
    line = pl.pallas_call(
        add_kernel, in_specs=[VM, VM], out_specs=VM, out_shape=line_shape, compiler_params=PARAMS
    )(line, near)
    near = lax.ppermute(line, "zh", [(i, i ^ 3) for i in range(pairs)])
    spread, shrink = pl.pallas_call(
        functools.partial(reduce_kernel, total_cells),
        in_specs=[SM, VM, VM],
        out_specs=[VM, VM],
        out_shape=[
            jax.ShapeDtypeStruct((PARTS, SUM_ROWS, 128), BF16),
            jax.ShapeDtypeStruct((2, 128), F32),
        ],
        scratch_shapes=[pltpu.VMEM((width, 128), F32)],
        compiler_params=PARAMS,
    )(place, line, near)
    half = lax.all_to_all(spread, GROUP, 0, 0)
    new_modes = pl.pallas_call(
        scale_kernel,
        in_specs=[VM] * (1 + len(moved)),
        out_specs=VM,
        out_shape=jax.ShapeDtypeStruct((local_cells, width), BF16),
        compiler_params=PARAMS,
    )(shrink, *moved)
    half, new_modes = lax.optimization_barrier((half, new_modes))
    other_half = lax.ppermute(half, "c", swap)
    projected, gram = pl.pallas_call(
        final_kernel,
        in_specs=[SM, VM, VM],
        out_specs=[VM, VM],
        out_shape=[
            jax.ShapeDtypeStruct((members, width, frames), F32),
            jax.ShapeDtypeStruct((width, width), F32),
        ],
        compiler_params=PARAMS,
    )(place, half, other_half)
    return (new_modes.reshape(levels, rows_x, rows_y, width), gram, projected)


def solution(mesh):
    ens, n_sx, n_sy = (mesh.shape[a] for a in ("ens", "sx", "sy"))
    fine = Mesh(mesh.devices.reshape(ens, 2, n_sx // 4, 2, n_sy // 2, 2), ("ens", *SX, *SY))
    in_specs = (P("ens", None, SX, SY, None), P("ens", None, None), P(None, SX, SY, None))
    out_specs = (P(None, SX, SY, None), P(), P("ens", None, None))
    return jax.shard_map(local, mesh=fine, in_specs=in_specs, out_specs=out_specs, check_vma=False)
```

```python
import functools
import math

import jax
import jax.numpy as jnp
from jax import lax
from jax.experimental import pallas as pl
from jax.experimental.pallas import tpu as pltpu
from jax.sharding import Mesh, PartitionSpec as P

ETA = 0.25
LAM = 0.5
TAU = 0.4

F32 = jnp.float32
BF16 = jnp.bfloat16
VMEM_LIMIT = 40 * 1024 * 1024
PARAMS = pltpu.CompilerParams(vmem_limit_bytes=VMEM_LIMIT)

SX = ("xh", "y", "c")
SY = ("zh", "zl")
GROUP = ("y", "xh", "zl")
PARTS = 16
PROJ_ROWS = 64
GRAM_ROWS = 16
SUM_ROWS = PROJ_ROWS + GRAM_ROWS
PART_ROWS = SUM_ROWS + 8

VM = pl.BlockSpec(memory_space=pltpu.VMEM)
SM = pl.BlockSpec(memory_space=pltpu.SMEM)
HBM = pl.BlockSpec(memory_space=pltpu.HBM)


def core_of(place):
    return place & 1


def parity_of(place):
    return (place >> 1) & 1


def part_of(place):
    return (place >> 2) & 15


def at_end(place, which):
    return ((place >> (6 + which)) & 1) == 1


def gradient(m, coefficients, series):
    acc = None
    for e in range(len(coefficients)):
        c = coefficients[e]()
        fitted = jnp.dot(m, c, preferred_element_type=F32)
        misfit = (fitted - series[e]().astype(F32)).astype(BF16)
        term = lax.dot_general(misfit, c, (((1,), (1,)), ((), ())), preferred_element_type=F32)
        acc = term if acc is None else acc + term
    return acc.astype(BF16)


def start_all(copies, sems):
    copies = [pltpu.make_async_copy(s, d, sems.at[i]) for i, (s, d) in enumerate(copies)]
    for copy in copies:
        copy.start()
    return copies


def after(copy, ref, *at):
    def load():
        copy.wait()
        return ref[at].reshape(-1, ref.shape[-1])

    return load


def first_grad_kernel(at_ref, m_hbm, c_hbm, x_hbm, g_ref, c_ref, x_ref, xb_ref, m_ref, sems):
    members = c_hbm.shape[0]
    last = m_hbm.shape[1] - 1
    copies = [(m_hbm.at[0], m_ref)]
    for e in range(members):
        copies.append((c_hbm.at[e], c_ref.at[e]))
        copies.append((x_hbm.at[e, 0], x_ref.at[e]))
    copies.append((m_hbm.at[:, last * core_of(at_ref[0])], xb_ref))
    copies = start_all(copies, sems)
    copies[0].wait()
    g_ref[...] = gradient(
        m_ref[...].reshape(g_ref.shape),
        [after(copies[1 + 2 * e], c_ref, e) for e in range(members)],
        [after(copies[2 + 2 * e], x_ref, e) for e in range(members)],
    )
    copies[-1].wait()


def second_grad_kernel(level, m_hbm, c_ref, x_hbm, g_ref, x_ref, m_ref, sems):
    members = c_ref.shape[0]
    copies = [(m_hbm.at[level], m_ref)]
    for e in range(members):
        copies.append((x_hbm.at[e, level], x_ref.at[e]))
    copies = start_all(copies, sems)
    copies[0].wait()
    g_ref[...] = gradient(
        m_ref[...].reshape(g_ref.shape),
        [functools.partial(c_ref.__getitem__, e) for e in range(members)],
        [after(copies[1 + e], x_ref, e) for e in range(members)],
    )


def rest_grad_kernel(begin, at_ref, m_hbm, c_ref, x_hbm, *refs):
    *g_refs, m_ref, x_ref, xa_ref, za_ref, zb_ref, tmp_ref, sems = refs
    members, levels, cells, _ = x_hbm.shape
    _, rows_x, rows_y, width = m_ref.shape
    copies = [(m_hbm, m_ref)]
    for level in range(begin, levels):
        for e in range(members):
            copies.append((x_hbm.at[e, level], x_ref.at[e, level - begin]))
    copies = start_all(copies, sems)
    copies[0].wait()
    core, even = core_of(at_ref[0]), parity_of(at_ref[0]) == 0
    xa_ref[...] = m_ref[:, (rows_x - 1) * (1 - core)]
    tmp_ref[0] = m_ref[:, :, 0:8, :].reshape(levels * rows_x, 8, width).astype(F32)
    tmp_ref[1] = m_ref[:, :, rows_y - 8 : rows_y, :].reshape(levels * rows_x, 8, width).astype(F32)
    lo, hi = tmp_ref[0, :, 0, :], tmp_ref[1, :, 7, :]
    za_ref[...] = jnp.where(even, hi, lo).astype(BF16)
    zb_ref[...] = jnp.where(even, lo, hi).astype(BF16)
    for i, g_ref in enumerate(g_refs):
        g_ref[...] = gradient(
            m_ref[begin + i].reshape(g_ref.shape),
            [functools.partial(c_ref.__getitem__, e) for e in range(members)],
            [after(copies[1 + i * members + e], x_ref, e, i) for e in range(members)],
        )


def grad_cost(members, cells, frames, width):
    return pl.CostEstimate(
        flops=4 * members * cells * frames * width,
        bytes_accessed=2 * cells * (2 * width + members * frames) + 2 * members * width * frames,
        transcendentals=0,
    )


def in_hbm(array):
    return pltpu.with_memory_space_constraint(array, pltpu.HBM)


def first_grad(place, modes, coefficients, series):
    members, _, cells, frames = series.shape
    levels, rows_x, rows_y, width = modes.shape
    outs = [
        jax.ShapeDtypeStruct((cells, width), BF16),
        pltpu.VMEM(coefficients.shape, BF16),
        pltpu.VMEM((members, cells, frames), BF16),
        jax.ShapeDtypeStruct((levels, rows_y, width), BF16),
    ]
    return pl.pallas_call(
        first_grad_kernel,
        in_specs=[SM] + [HBM] * 3,
        out_specs=[VM] * len(outs),
        out_shape=outs,
        scratch_shapes=[
            pltpu.VMEM((rows_x, rows_y, width), BF16),
            pltpu.SemaphoreType.DMA((2 + 2 * members,)),
        ],
        compiler_params=PARAMS,
        cost_estimate=grad_cost(members, cells, frames, width),
    )(place, in_hbm(modes), in_hbm(coefficients), in_hbm(series))


def second_grad(modes, coefficients, series, level):
    members, _, cells, frames = series.shape
    _, rows_x, rows_y, width = modes.shape
    outs = [jax.ShapeDtypeStruct((cells, width), BF16), pltpu.VMEM((members, cells, frames), BF16)]
    return pl.pallas_call(
        functools.partial(second_grad_kernel, level),
        in_specs=[HBM, VM, HBM],
        out_specs=[VM] * len(outs),
        out_shape=outs,
        scratch_shapes=[
            pltpu.VMEM((rows_x, rows_y, width), BF16),
            pltpu.SemaphoreType.DMA((1 + members,)),
        ],
        compiler_params=PARAMS,
        cost_estimate=grad_cost(members, cells, frames, width),
    )(in_hbm(modes), coefficients, in_hbm(series))


def rest_grad(place, modes, coefficients, series, begin):
    members, levels, cells, frames = series.shape
    _, rows_x, rows_y, width = modes.shape
    count = levels - begin
    outs = [jax.ShapeDtypeStruct((cells, width), BF16)] * count
    outs += [
        pltpu.VMEM(modes.shape, BF16),
        pltpu.VMEM((members, count, cells, frames), BF16),
        jax.ShapeDtypeStruct((levels, rows_y, width), BF16),
        jax.ShapeDtypeStruct((levels * rows_x, width), BF16),
        jax.ShapeDtypeStruct((levels * rows_x, width), BF16),
    ]
    return pl.pallas_call(
        functools.partial(rest_grad_kernel, begin),
        in_specs=[SM, HBM, VM, HBM],
        out_specs=[VM] * len(outs),
        out_shape=outs,
        scratch_shapes=[
            pltpu.VMEM((2, levels * rows_x, 8, width), F32),
            pltpu.SemaphoreType.DMA((1 + members * count,)),
        ],
        compiler_params=PARAMS,
        cost_estimate=grad_cost(members, count * cells, frames, width),
    )(place, in_hbm(modes), coefficients, in_hbm(series))


def base_of(level, place, m_ref, xa_ref, xb_ref, za_ref, zb_ref):
    _, rows_x, rows_y, width = m_ref.shape
    lower, even = core_of(place) == 0, parity_of(place) == 0
    shape = (rows_x, rows_y, width)
    f = m_ref[level].astype(F32)
    xa, xb = xa_ref[level : level + 1].astype(F32), xb_ref[level : level + 1].astype(F32)
    rows = slice(level * rows_x, (level + 1) * rows_x)
    za, zb = za_ref[rows, :].astype(F32), zb_ref[rows, :].astype(F32)
    xlo = jnp.where(at_end(place, 0), 0.0, jnp.where(lower, xb, xa))
    xhi = jnp.where(at_end(place, 1), 0.0, jnp.where(lower, xa, xb))
    zlo = jnp.where(at_end(place, 2), 0.0, jnp.where(even, zb, za))
    zhi = jnp.where(at_end(place, 3), 0.0, jnp.where(even, za, zb))
    up = jnp.concatenate([xlo, f[:-1]], axis=0)
    down = jnp.concatenate([f[1:], xhi], axis=0)
    at = lax.broadcasted_iota(jnp.int32, shape, 1)
    left = jnp.where(at == 0, jnp.broadcast_to(zlo[:, None, :], shape), pltpu.roll(f, 1, 1))
    right = jnp.where(
        at == rows_y - 1, jnp.broadcast_to(zhi[:, None, :], shape), pltpu.roll(f, rows_y - 1, 1)
    )
    bent = 4.0 * f - (down + up + right + left)
    return (f - (ETA * LAM) * bent).reshape(rows_x * rows_y, width)


def split_squares(squares, rows):
    high = squares.astype(BF16).astype(F32)
    return jnp.concatenate([high, squares - high, jnp.zeros((rows - 4, 128), F32)], axis=0)


def emit(out_ref, half, proj_ref, gram_ref, squares):
    members = proj_ref.shape[0]
    for j in range(PARTS):
        tb, m, r = j // 8, (j // 4) % members, j % 4
        at = pl.multiple_of((half * 2 + tb) * 128, 128)
        block = proj_ref[m, r * PROJ_ROWS : (r + 1) * PROJ_ROWS, pl.ds(at, 128)]
        out_ref[j, 0:PROJ_ROWS, :] = block.astype(BF16)
        at = pl.multiple_of(half * 128, 128)
        block = gram_ref[j * GRAM_ROWS : (j + 1) * GRAM_ROWS, pl.ds(at, 128)]
        out_ref[j, PROJ_ROWS:SUM_ROWS, :] = block.astype(BF16)
        out_ref[j, SUM_ROWS:PART_ROWS, :] = squares


def move(base, own_ref, got_ref):
    grad = own_ref[...].astype(F32) + got_ref[...].astype(F32)
    moved = (base - ETA * grad).astype(BF16)
    wide = moved.astype(F32)
    return moved, jnp.sum(wide * wide, axis=0, keepdims=True)


def most_kernel(at_ref, m_ref, xa_ref, xb_ref, za_ref, zb_ref, *refs):
    *refs, base_ref, moved_ref, proj_ref, gram_ref, squares_ref = refs
    halos = (xa_ref, xb_ref, za_ref, zb_ref)
    count = len(refs) // 3
    owns, gots, xs = refs[:count], refs[count : 2 * count], refs[2 * count :]
    squares = None
    for level in range(count):
        moved, part = move(base_of(level, at_ref[0], m_ref, *halos), owns[level], gots[level])
        squares = part if level == 0 else squares + part
        moved_ref[level * moved.shape[0] : (level + 1) * moved.shape[0], :] = moved
        turned = moved.T
        gram = jnp.dot(turned, moved, preferred_element_type=F32)
        gram_ref[...] = gram if level == 0 else gram_ref[...] + gram
        for e in range(proj_ref.shape[0]):
            x = xs[level][e] if len(xs[level].shape) == 3 else xs[level][e, 0]
            proj = jnp.dot(turned, x, preferred_element_type=F32)
            proj_ref[e] = proj if level == 0 else proj_ref[e] + proj
    squares_ref[...] = squares
    base_ref[...] = base_of(count, at_ref[0], m_ref, *halos)


def last_kernel(at_ref, base_ref, own_ref, got_ref, x_ref, proj_in, gram_in, squares_in, *refs):
    moved_ref, keep_ref, send_ref, proj_ref, gram_ref = refs
    moved, squares = move(base_ref[...], own_ref, got_ref)
    moved_ref[...] = moved
    squares = squares + squares_in[...]
    turned = moved.T
    gram_ref[...] = gram_in[...] + jnp.dot(turned, moved, preferred_element_type=F32)
    for e in range(proj_ref.shape[0]):
        proj = jnp.dot(turned, x_ref[e, x_ref.shape[1] - 1], preferred_element_type=F32)
        proj_ref[e] = proj_in[e] + proj
    core = core_of(at_ref[0])
    pair = jnp.concatenate([squares[:, 0:128], squares[:, 128:256]], axis=0)
    packed = split_squares(pair, 8).astype(BF16)
    emit(send_ref, 1 - core, proj_ref, gram_ref, packed)
    emit(keep_ref, core, proj_ref, gram_ref, packed)


def step_cost(members, cells, frames, width):
    return pl.CostEstimate(
        flops=2 * cells * width * (width + members * frames),
        bytes_accessed=2 * cells * (4 * width + members * frames),
        transcendentals=0,
    )


def steps(place, modes, halos, owns, gots, series):
    members, frames = series[0].shape[0], series[0].shape[-1]
    cells, width = owns[0].shape
    most = len(owns) - 1
    sums = [
        jax.ShapeDtypeStruct((members, width, frames), F32),
        jax.ShapeDtypeStruct((width, width), F32),
        jax.ShapeDtypeStruct((1, width), F32),
    ]
    args = [modes, *halos, *owns[:most], *gots[:most], *series[:most]]
    base, moved, *carry = pl.pallas_call(
        most_kernel,
        in_specs=[SM] + [VM] * len(args),
        out_specs=[VM] * 5,
        out_shape=[
            jax.ShapeDtypeStruct((cells, width), F32),
            jax.ShapeDtypeStruct((most * cells, width), BF16),
            *sums,
        ],
        compiler_params=PARAMS,
        cost_estimate=step_cost(members, most * cells, frames, width),
    )(place, *args)
    args = [base, owns[most], gots[most], series[most], *carry]
    tail, keep, send = pl.pallas_call(
        last_kernel,
        in_specs=[SM] + [VM] * len(args),
        out_specs=[VM] * 3,
        out_shape=[jax.ShapeDtypeStruct((cells, width), BF16)]
        + [jax.ShapeDtypeStruct((PARTS, PART_ROWS, 128), BF16)] * 2,
        scratch_shapes=[pltpu.VMEM(s.shape, F32) for s in sums[:2]],
        compiler_params=PARAMS,
        cost_estimate=step_cost(members, cells, frames, width),
    )(place, *args)
    return [moved, tail], keep, send


def whole_squares(part):
    return part[SUM_ROWS : SUM_ROWS + 2, :] + part[SUM_ROWS + 2 : SUM_ROWS + 4, :]


def packed_squares(total):
    return split_squares(whole_squares(total), 8).astype(BF16)


def join_kernel(keep_ref, got_ref, out_ref):
    out_ref[:, 0:SUM_ROWS, :] = (
        keep_ref[:, 0:SUM_ROWS, :].astype(F32) + got_ref[:, 0:SUM_ROWS, :].astype(F32)
    ).astype(BF16)
    tail = keep_ref[0].astype(F32) + got_ref[0].astype(F32)
    packed = packed_squares(tail)
    for j in range(PARTS):
        out_ref[j, SUM_ROWS:PART_ROWS, :] = packed


def group_kernel(in_ref, out_ref):
    total = in_ref[0].astype(F32)
    for j in range(1, PARTS):
        total = total + in_ref[j].astype(F32)
    out_ref[0:SUM_ROWS, :] = total[0:SUM_ROWS, :].astype(BF16)
    out_ref[SUM_ROWS:PART_ROWS, :] = packed_squares(total)


def add_kernel(own_ref, got_ref, out_ref):
    total = own_ref[...].astype(F32) + got_ref[...].astype(F32)
    out_ref[0:SUM_ROWS, :] = total[0:SUM_ROWS, :].astype(BF16)
    out_ref[SUM_ROWS:PART_ROWS, :] = packed_squares(total)


def reduce_kernel(total_cells, at_ref, own_ref, got_ref, out_ref, shrink_ref, column_ref):
    core, part = core_of(at_ref[0]), part_of(at_ref[0])
    total = own_ref[...].astype(F32) + got_ref[...].astype(F32)
    squares = whole_squares(total)
    shrink = jnp.maximum(0.0, 1.0 - TAU / jnp.sqrt(squares / total_cells + 1e-06))
    shrink_ref[...] = shrink
    for k in range(2):
        column_ref[k * 128 : (k + 1) * 128, :] = jnp.broadcast_to(shrink[k : k + 1, :], (128, 128)).T
    at = pl.multiple_of((part & 3) * PROJ_ROWS, PROJ_ROWS)
    proj = column_ref[pl.ds(at, PROJ_ROWS), :] * total[0:PROJ_ROWS, :] * (1.0 / math.sqrt(total_cells))
    at = pl.multiple_of(part * GRAM_ROWS, GRAM_ROWS)
    lanes = jnp.where(core == 0, shrink[0:1, :], shrink[1:2, :])
    gram = column_ref[pl.ds(at, GRAM_ROWS), :] * total[PROJ_ROWS:SUM_ROWS, :] * lanes * (1.0 / total_cells)
    mine = jnp.concatenate([proj, gram], axis=0).astype(BF16)
    for j in range(PARTS):
        out_ref[j] = mine


def scale_kernel(shrink_ref, *refs):
    out_ref = refs[-1]
    at = 0
    for m_ref in refs[:-1]:
        rows = slice(at, at + m_ref.shape[0])
        at = rows.stop
        for k in range(2):
            lanes = slice(k * 128, (k + 1) * 128)
            out_ref[rows, lanes] = (m_ref[:, lanes].astype(F32) * shrink_ref[k : k + 1, :]).astype(BF16)


def final_kernel(at_ref, own_ref, got_ref, proj_ref, gram_ref):
    core = core_of(at_ref[0])
    members = proj_ref.shape[0]
    for ref, half in ((own_ref, core), (got_ref, 1 - core)):
        for j in range(PARTS):
            tb, m, r = j // 8, (j // 4) % members, j % 4
            at = pl.multiple_of((half * 2 + tb) * 128, 128)
            rows = slice(r * PROJ_ROWS, (r + 1) * PROJ_ROWS)
            proj_ref[m, rows, pl.ds(at, 128)] = ref[j, 0:PROJ_ROWS, :].astype(F32)
            at = pl.multiple_of(half * 128, 128)
            gram_ref[j * GRAM_ROWS : (j + 1) * GRAM_ROWS, pl.ds(at, 128)] = (
                ref[j, PROJ_ROWS:SUM_ROWS, :].astype(F32)
            )


def both_ways(pairs):
    return [p for i, j in pairs for p in ((i, j), (j, i))]


def local(snapshots, coefficients, modes):
    members, levels, rows_x, rows_y, frames = snapshots.shape
    width = modes.shape[3]
    cells = rows_x * rows_y
    local_cells = levels * cells
    n_sx, n_z = lax.axis_size(SX), lax.axis_size(SY)
    total_cells = local_cells * n_sx * n_z
    core = lax.axis_index("c").astype(jnp.int32)
    parity = lax.axis_index("zl").astype(jnp.int32)
    part = lax.axis_index(GROUP).astype(jnp.int32)
    x_at, z_at = lax.axis_index(SX), lax.axis_index(SY)
    place = core + 2 * parity + 4 * part
    for i, end in enumerate((x_at == 0, x_at == n_sx - 1, z_at == 0, z_at == n_z - 1)):
        place = place + end.astype(jnp.int32) * (64 << i)
    place = place.reshape(1)
    series = snapshots.reshape(members, levels, cells, frames)
    swap = [(0, 1), (1, 0)]

    g0, coefficients, x0, edge_b = first_grad(place, modes, coefficients, series)
    got0 = lax.ppermute(g0, "ens", swap)
    xb = lax.ppermute(edge_b, SX, both_ways([(i, (i + 1) % n_sx) for i in range(1, n_sx, 2)]))
    g1, x1 = second_grad(modes, coefficients, series, 1)
    got1 = lax.ppermute(g1, "ens", swap)
    coefficients, _ = lax.optimization_barrier((coefficients, g1))
    g2, g3, modes, series, edge_a, row_a, row_b = rest_grad(place, modes, coefficients, series, 2)
    got2 = lax.ppermute(g2, "ens", swap)
    got3 = lax.ppermute(g3, "ens", swap)
    got0, got1, row_a, row_b = lax.optimization_barrier((got0, got1, row_a, row_b))
    za = lax.ppermute(row_a, SY, both_ways([(i, i + 1) for i in range(0, n_z, 2)]))
    zb = lax.ppermute(row_b, SY, both_ways([(i, (i + 1) % n_z) for i in range(1, n_z, 2)]))
    xb, edge_a, za, zb = lax.optimization_barrier((xb, edge_a, za, zb))
    xa = lax.ppermute(edge_a, "c", swap)
    moved, keep, send = steps(
        place,
        modes,
        (xa, xb, za, zb),
        (g0, g1, g2, g3),
        (got0, got1, got2, got3),
        (x0, x1, series, series),
    )

    part_shape = jax.ShapeDtypeStruct((PARTS, PART_ROWS, 128), BF16)
    other = lax.ppermute(send, "c", swap)
    joined = pl.pallas_call(
        join_kernel, in_specs=[VM, VM], out_specs=VM, out_shape=part_shape, compiler_params=PARAMS
    )(keep, other)
    parts = lax.all_to_all(joined, GROUP, 0, 0)
    line_shape = jax.ShapeDtypeStruct((PART_ROWS, 128), BF16)
    line = pl.pallas_call(
        group_kernel, in_specs=[VM], out_specs=VM, out_shape=line_shape, compiler_params=PARAMS
    )(parts)
    pairs = lax.axis_size("zh")
    near = lax.ppermute(line, "zh", [(i, i ^ 1) for i in range(pairs)])
    line = pl.pallas_call(
        add_kernel, in_specs=[VM, VM], out_specs=VM, out_shape=line_shape, compiler_params=PARAMS
    )(line, near)
    near = lax.ppermute(line, "zh", [(i, i ^ 3) for i in range(pairs)])
    spread, shrink = pl.pallas_call(
        functools.partial(reduce_kernel, total_cells),
        in_specs=[SM, VM, VM],
        out_specs=[VM, VM],
        out_shape=[
            jax.ShapeDtypeStruct((PARTS, SUM_ROWS, 128), BF16),
            jax.ShapeDtypeStruct((2, 128), F32),
        ],
        scratch_shapes=[pltpu.VMEM((width, 128), F32)],
        compiler_params=PARAMS,
    )(place, line, near)
    half = lax.all_to_all(spread, GROUP, 0, 0)
    new_modes = pl.pallas_call(
        scale_kernel,
        in_specs=[VM] * (1 + len(moved)),
        out_specs=VM,
        out_shape=jax.ShapeDtypeStruct((local_cells, width), BF16),
        compiler_params=PARAMS,
    )(shrink, *moved)
    half, new_modes = lax.optimization_barrier((half, new_modes))
    other_half = lax.ppermute(half, "c", swap)
    projected, gram = pl.pallas_call(
        final_kernel,
        in_specs=[SM, VM, VM],
        out_specs=[VM, VM],
        out_shape=[
            jax.ShapeDtypeStruct((members, width, frames), F32),
            jax.ShapeDtypeStruct((width, width), F32),
        ],
        compiler_params=PARAMS,
    )(place, half, other_half)
    return (new_modes.reshape(levels, rows_x, rows_y, width), gram, projected)


def solution(mesh):
    ens, n_sx, n_sy = (mesh.shape[a] for a in ("ens", "sx", "sy"))
    fine = Mesh(mesh.devices.reshape(ens, 2, n_sx // 4, 2, n_sy // 2, 2), ("ens", *SX, *SY))
    in_specs = (P("ens", None, SX, SY, None), P("ens", None, None), P(None, SX, SY, None))
    out_specs = (P(None, SX, SY, None), P(), P("ens", None, None))
    return jax.shard_map(local, mesh=fine, in_specs=in_specs, out_specs=out_specs, check_vma=False)
```

```python
import functools
import math

import jax
import jax.numpy as jnp
from jax import lax
from jax.experimental import pallas as pl
from jax.experimental.pallas import tpu as pltpu
from jax.sharding import Mesh, PartitionSpec as P

ETA = 0.25
LAM = 0.5
TAU = 0.4

F32 = jnp.float32
BF16 = jnp.bfloat16
VMEM_LIMIT = 40 * 1024 * 1024
PARAMS = pltpu.CompilerParams(vmem_limit_bytes=VMEM_LIMIT)

SX = ("xh", "y", "c")
SY = ("zh", "zl")
GROUP = ("xh", "y", "zl")
PARTS = 16
PROJ_ROWS = 64
GRAM_ROWS = 16
SUM_ROWS = PROJ_ROWS + GRAM_ROWS
PART_ROWS = SUM_ROWS + 8

VM = pl.BlockSpec(memory_space=pltpu.VMEM)
SM = pl.BlockSpec(memory_space=pltpu.SMEM)
HBM = pl.BlockSpec(memory_space=pltpu.HBM)


def core_of(place):
    return place & 1


def parity_of(place):
    return (place >> 1) & 1


def part_of(place):
    return (place >> 2) & 15


def at_end(place, which):
    return ((place >> (6 + which)) & 1) == 1


def gradient(m, coefficients, series):
    acc = None
    for e in range(len(coefficients)):
        c = coefficients[e]()
        fitted = jnp.dot(m, c, preferred_element_type=F32)
        misfit = (fitted - series[e]().astype(F32)).astype(BF16)
        term = lax.dot_general(misfit, c, (((1,), (1,)), ((), ())), preferred_element_type=F32)
        acc = term if acc is None else acc + term
    return acc.astype(BF16)


def start_all(copies, sems):
    copies = [pltpu.make_async_copy(s, d, sems.at[i]) for i, (s, d) in enumerate(copies)]
    for copy in copies:
        copy.start()
    return copies


def after(copy, ref, *at):
    def load():
        copy.wait()
        return ref[at].reshape(-1, ref.shape[-1])

    return load


def first_grad_kernel(at_ref, m_hbm, c_hbm, x_hbm, g_ref, c_ref, x_ref, xb_ref, m_ref, sems):
    members = c_hbm.shape[0]
    last = m_hbm.shape[1] - 1
    copies = [(m_hbm.at[0], m_ref)]
    for e in range(members):
        copies.append((c_hbm.at[e], c_ref.at[e]))
        copies.append((x_hbm.at[e, 0], x_ref.at[e]))
    copies.append((m_hbm.at[:, last * core_of(at_ref[0])], xb_ref))
    copies = start_all(copies, sems)
    copies[0].wait()
    g_ref[...] = gradient(
        m_ref[...].reshape(g_ref.shape),
        [after(copies[1 + 2 * e], c_ref, e) for e in range(members)],
        [after(copies[2 + 2 * e], x_ref, e) for e in range(members)],
    )
    copies[-1].wait()


def second_grad_kernel(level, m_hbm, c_ref, x_hbm, g_ref, x_ref, m_ref, sems):
    members = c_ref.shape[0]
    copies = [(m_hbm.at[level], m_ref)]
    for e in range(members):
        copies.append((x_hbm.at[e, level], x_ref.at[e]))
    copies = start_all(copies, sems)
    copies[0].wait()
    g_ref[...] = gradient(
        m_ref[...].reshape(g_ref.shape),
        [functools.partial(c_ref.__getitem__, e) for e in range(members)],
        [after(copies[1 + e], x_ref, e) for e in range(members)],
    )


def rest_grad_kernel(begin, at_ref, m_hbm, c_ref, x_hbm, *refs):
    *g_refs, m_ref, x_ref, xa_ref, za_ref, zb_ref, tmp_ref, sems = refs
    members, levels, cells, _ = x_hbm.shape
    _, rows_x, rows_y, width = m_ref.shape
    copies = [(m_hbm, m_ref)]
    for level in range(begin, levels):
        for e in range(members):
            copies.append((x_hbm.at[e, level], x_ref.at[e, level - begin]))
    copies = start_all(copies, sems)
    copies[0].wait()
    core, even = core_of(at_ref[0]), parity_of(at_ref[0]) == 0
    xa_ref[...] = m_ref[:, (rows_x - 1) * (1 - core)]
    tmp_ref[0] = m_ref[:, :, 0:8, :].reshape(levels * rows_x, 8, width).astype(F32)
    tmp_ref[1] = m_ref[:, :, rows_y - 8 : rows_y, :].reshape(levels * rows_x, 8, width).astype(F32)
    lo, hi = tmp_ref[0, :, 0, :], tmp_ref[1, :, 7, :]
    za_ref[...] = jnp.where(even, hi, lo).astype(BF16)
    zb_ref[...] = jnp.where(even, lo, hi).astype(BF16)
    for i, g_ref in enumerate(g_refs):
        g_ref[...] = gradient(
            m_ref[begin + i].reshape(g_ref.shape),
            [functools.partial(c_ref.__getitem__, e) for e in range(members)],
            [after(copies[1 + i * members + e], x_ref, e, i) for e in range(members)],
        )


def grad_cost(members, cells, frames, width):
    return pl.CostEstimate(
        flops=4 * members * cells * frames * width,
        bytes_accessed=2 * cells * (2 * width + members * frames) + 2 * members * width * frames,
        transcendentals=0,
    )


def in_hbm(array):
    return pltpu.with_memory_space_constraint(array, pltpu.HBM)


def first_grad(place, modes, coefficients, series):
    members, _, cells, frames = series.shape
    levels, rows_x, rows_y, width = modes.shape
    outs = [
        jax.ShapeDtypeStruct((cells, width), BF16),
        pltpu.VMEM(coefficients.shape, BF16),
        pltpu.VMEM((members, cells, frames), BF16),
        jax.ShapeDtypeStruct((levels, rows_y, width), BF16),
    ]
    return pl.pallas_call(
        first_grad_kernel,
        in_specs=[SM] + [HBM] * 3,
        out_specs=[VM] * len(outs),
        out_shape=outs,
        scratch_shapes=[
            pltpu.VMEM((rows_x, rows_y, width), BF16),
            pltpu.SemaphoreType.DMA((2 + 2 * members,)),
        ],
        compiler_params=PARAMS,
        cost_estimate=grad_cost(members, cells, frames, width),
    )(place, in_hbm(modes), in_hbm(coefficients), in_hbm(series))


def second_grad(modes, coefficients, series, level):
    members, _, cells, frames = series.shape
    _, rows_x, rows_y, width = modes.shape
    outs = [jax.ShapeDtypeStruct((cells, width), BF16), pltpu.VMEM((members, cells, frames), BF16)]
    return pl.pallas_call(
        functools.partial(second_grad_kernel, level),
        in_specs=[HBM, VM, HBM],
        out_specs=[VM] * len(outs),
        out_shape=outs,
        scratch_shapes=[
            pltpu.VMEM((rows_x, rows_y, width), BF16),
            pltpu.SemaphoreType.DMA((1 + members,)),
        ],
        compiler_params=PARAMS,
        cost_estimate=grad_cost(members, cells, frames, width),
    )(in_hbm(modes), coefficients, in_hbm(series))


def rest_grad(place, modes, coefficients, series, begin):
    members, levels, cells, frames = series.shape
    _, rows_x, rows_y, width = modes.shape
    count = levels - begin
    outs = [jax.ShapeDtypeStruct((cells, width), BF16)] * count
    outs += [
        pltpu.VMEM(modes.shape, BF16),
        pltpu.VMEM((members, count, cells, frames), BF16),
        jax.ShapeDtypeStruct((levels, rows_y, width), BF16),
        jax.ShapeDtypeStruct((levels * rows_x, width), BF16),
        jax.ShapeDtypeStruct((levels * rows_x, width), BF16),
    ]
    return pl.pallas_call(
        functools.partial(rest_grad_kernel, begin),
        in_specs=[SM, HBM, VM, HBM],
        out_specs=[VM] * len(outs),
        out_shape=outs,
        scratch_shapes=[
            pltpu.VMEM((2, levels * rows_x, 8, width), F32),
            pltpu.SemaphoreType.DMA((1 + members * count,)),
        ],
        compiler_params=PARAMS,
        cost_estimate=grad_cost(members, count * cells, frames, width),
    )(place, in_hbm(modes), coefficients, in_hbm(series))


def base_of(level, place, m_ref, xa_ref, xb_ref, za_ref, zb_ref):
    _, rows_x, rows_y, width = m_ref.shape
    lower, even = core_of(place) == 0, parity_of(place) == 0
    shape = (rows_x, rows_y, width)
    f = m_ref[level].astype(F32)
    xa, xb = xa_ref[level : level + 1].astype(F32), xb_ref[level : level + 1].astype(F32)
    rows = slice(level * rows_x, (level + 1) * rows_x)
    za, zb = za_ref[rows, :].astype(F32), zb_ref[rows, :].astype(F32)
    xlo = jnp.where(at_end(place, 0), 0.0, jnp.where(lower, xb, xa))
    xhi = jnp.where(at_end(place, 1), 0.0, jnp.where(lower, xa, xb))
    zlo = jnp.where(at_end(place, 2), 0.0, jnp.where(even, zb, za))
    zhi = jnp.where(at_end(place, 3), 0.0, jnp.where(even, za, zb))
    up = jnp.concatenate([xlo, f[:-1]], axis=0)
    down = jnp.concatenate([f[1:], xhi], axis=0)
    at = lax.broadcasted_iota(jnp.int32, shape, 1)
    left = jnp.where(at == 0, jnp.broadcast_to(zlo[:, None, :], shape), pltpu.roll(f, 1, 1))
    right = jnp.where(
        at == rows_y - 1, jnp.broadcast_to(zhi[:, None, :], shape), pltpu.roll(f, rows_y - 1, 1)
    )
    bent = 4.0 * f - (down + up + right + left)
    return (f - (ETA * LAM) * bent).reshape(rows_x * rows_y, width)


def split_squares(squares, rows):
    high = squares.astype(BF16).astype(F32)
    return jnp.concatenate([high, squares - high, jnp.zeros((rows - 4, 128), F32)], axis=0)


def emit(out_ref, half, proj_ref, gram_ref, squares):
    members = proj_ref.shape[0]
    for j in range(PARTS):
        tb, m, r = j // 8, (j // 4) % members, j % 4
        at = pl.multiple_of((half * 2 + tb) * 128, 128)
        block = proj_ref[m, r * PROJ_ROWS : (r + 1) * PROJ_ROWS, pl.ds(at, 128)]
        out_ref[j, 0:PROJ_ROWS, :] = block.astype(BF16)
        at = pl.multiple_of(half * 128, 128)
        block = gram_ref[j * GRAM_ROWS : (j + 1) * GRAM_ROWS, pl.ds(at, 128)]
        out_ref[j, PROJ_ROWS:SUM_ROWS, :] = block.astype(BF16)
        out_ref[j, SUM_ROWS:PART_ROWS, :] = squares


def move(base, own_ref, got_ref):
    grad = own_ref[...].astype(F32) + got_ref[...].astype(F32)
    moved = (base - ETA * grad).astype(BF16)
    wide = moved.astype(F32)
    return moved, jnp.sum(wide * wide, axis=0, keepdims=True)


def most_kernel(at_ref, m_ref, xa_ref, xb_ref, za_ref, zb_ref, *refs):
    *refs, base_ref, moved_ref, proj_ref, gram_ref, squares_ref = refs
    halos = (xa_ref, xb_ref, za_ref, zb_ref)
    count = len(refs) // 3
    owns, gots, xs = refs[:count], refs[count : 2 * count], refs[2 * count :]
    squares = None
    for level in range(count):
        moved, part = move(base_of(level, at_ref[0], m_ref, *halos), owns[level], gots[level])
        squares = part if level == 0 else squares + part
        moved_ref[level * moved.shape[0] : (level + 1) * moved.shape[0], :] = moved
        turned = moved.T
        gram = jnp.dot(turned, moved, preferred_element_type=F32)
        gram_ref[...] = gram if level == 0 else gram_ref[...] + gram
        for e in range(proj_ref.shape[0]):
            x = xs[level][e] if len(xs[level].shape) == 3 else xs[level][e, 0]
            proj = jnp.dot(turned, x, preferred_element_type=F32)
            proj_ref[e] = proj if level == 0 else proj_ref[e] + proj
    squares_ref[...] = squares
    base_ref[...] = base_of(count, at_ref[0], m_ref, *halos)


def last_kernel(at_ref, base_ref, own_ref, got_ref, x_ref, proj_in, gram_in, squares_in, *refs):
    moved_ref, keep_ref, send_ref, proj_ref, gram_ref = refs
    moved, squares = move(base_ref[...], own_ref, got_ref)
    moved_ref[...] = moved
    squares = squares + squares_in[...]
    turned = moved.T
    gram_ref[...] = gram_in[...] + jnp.dot(turned, moved, preferred_element_type=F32)
    for e in range(proj_ref.shape[0]):
        proj = jnp.dot(turned, x_ref[e, x_ref.shape[1] - 1], preferred_element_type=F32)
        proj_ref[e] = proj_in[e] + proj
    core = core_of(at_ref[0])
    pair = jnp.concatenate([squares[:, 0:128], squares[:, 128:256]], axis=0)
    packed = split_squares(pair, 8).astype(BF16)
    emit(send_ref, 1 - core, proj_ref, gram_ref, packed)
    emit(keep_ref, core, proj_ref, gram_ref, packed)


def step_cost(members, cells, frames, width):
    return pl.CostEstimate(
        flops=2 * cells * width * (width + members * frames),
        bytes_accessed=2 * cells * (4 * width + members * frames),
        transcendentals=0,
    )


def steps(place, modes, halos, owns, gots, series):
    members, frames = series[0].shape[0], series[0].shape[-1]
    cells, width = owns[0].shape
    most = len(owns) - 1
    sums = [
        jax.ShapeDtypeStruct((members, width, frames), F32),
        jax.ShapeDtypeStruct((width, width), F32),
        jax.ShapeDtypeStruct((1, width), F32),
    ]
    args = [modes, *halos, *owns[:most], *gots[:most], *series[:most]]
    base, moved, *carry = pl.pallas_call(
        most_kernel,
        in_specs=[SM] + [VM] * len(args),
        out_specs=[VM] * 5,
        out_shape=[
            jax.ShapeDtypeStruct((cells, width), F32),
            jax.ShapeDtypeStruct((most * cells, width), BF16),
            *sums,
        ],
        compiler_params=PARAMS,
        cost_estimate=step_cost(members, most * cells, frames, width),
    )(place, *args)
    args = [base, owns[most], gots[most], series[most], *carry]
    tail, keep, send = pl.pallas_call(
        last_kernel,
        in_specs=[SM] + [VM] * len(args),
        out_specs=[VM] * 3,
        out_shape=[jax.ShapeDtypeStruct((cells, width), BF16)]
        + [jax.ShapeDtypeStruct((PARTS, PART_ROWS, 128), BF16)] * 2,
        scratch_shapes=[pltpu.VMEM(s.shape, F32) for s in sums[:2]],
        compiler_params=PARAMS,
        cost_estimate=step_cost(members, cells, frames, width),
    )(place, *args)
    return [moved, tail], keep, send


def whole_squares(part):
    return part[SUM_ROWS : SUM_ROWS + 2, :] + part[SUM_ROWS + 2 : SUM_ROWS + 4, :]


def packed_squares(total):
    return split_squares(whole_squares(total), 8).astype(BF16)


def join_kernel(keep_ref, got_ref, out_ref):
    out_ref[:, 0:SUM_ROWS, :] = (
        keep_ref[:, 0:SUM_ROWS, :].astype(F32) + got_ref[:, 0:SUM_ROWS, :].astype(F32)
    ).astype(BF16)
    tail = keep_ref[0].astype(F32) + got_ref[0].astype(F32)
    packed = packed_squares(tail)
    for j in range(PARTS):
        out_ref[j, SUM_ROWS:PART_ROWS, :] = packed


def group_kernel(in_ref, out_ref):
    total = in_ref[0].astype(F32)
    for j in range(1, PARTS):
        total = total + in_ref[j].astype(F32)
    out_ref[0:SUM_ROWS, :] = total[0:SUM_ROWS, :].astype(BF16)
    out_ref[SUM_ROWS:PART_ROWS, :] = packed_squares(total)


def add_kernel(own_ref, got_ref, out_ref):
    total = own_ref[...].astype(F32) + got_ref[...].astype(F32)
    out_ref[0:SUM_ROWS, :] = total[0:SUM_ROWS, :].astype(BF16)
    out_ref[SUM_ROWS:PART_ROWS, :] = packed_squares(total)


def reduce_kernel(total_cells, at_ref, own_ref, got_ref, out_ref, shrink_ref, column_ref):
    core, part = core_of(at_ref[0]), part_of(at_ref[0])
    total = own_ref[...].astype(F32) + got_ref[...].astype(F32)
    squares = whole_squares(total)
    shrink = jnp.maximum(0.0, 1.0 - TAU / jnp.sqrt(squares / total_cells + 1e-06))
    shrink_ref[...] = shrink
    for k in range(2):
        column_ref[k * 128 : (k + 1) * 128, :] = jnp.broadcast_to(shrink[k : k + 1, :], (128, 128)).T
    at = pl.multiple_of((part & 3) * PROJ_ROWS, PROJ_ROWS)
    proj = column_ref[pl.ds(at, PROJ_ROWS), :] * total[0:PROJ_ROWS, :] * (1.0 / math.sqrt(total_cells))
    at = pl.multiple_of(part * GRAM_ROWS, GRAM_ROWS)
    lanes = jnp.where(core == 0, shrink[0:1, :], shrink[1:2, :])
    gram = column_ref[pl.ds(at, GRAM_ROWS), :] * total[PROJ_ROWS:SUM_ROWS, :] * lanes * (1.0 / total_cells)
    mine = jnp.concatenate([proj, gram], axis=0).astype(BF16)
    for j in range(PARTS):
        out_ref[j] = mine


def scale_kernel(shrink_ref, *refs):
    out_ref = refs[-1]
    at = 0
    for m_ref in refs[:-1]:
        rows = slice(at, at + m_ref.shape[0])
        at = rows.stop
        for k in range(2):
            lanes = slice(k * 128, (k + 1) * 128)
            out_ref[rows, lanes] = (m_ref[:, lanes].astype(F32) * shrink_ref[k : k + 1, :]).astype(BF16)


def final_kernel(at_ref, own_ref, got_ref, proj_ref, gram_ref):
    core = core_of(at_ref[0])
    members = proj_ref.shape[0]
    for ref, half in ((own_ref, core), (got_ref, 1 - core)):
        for j in range(PARTS):
            tb, m, r = j // 8, (j // 4) % members, j % 4
            at = pl.multiple_of((half * 2 + tb) * 128, 128)
            rows = slice(r * PROJ_ROWS, (r + 1) * PROJ_ROWS)
            proj_ref[m, rows, pl.ds(at, 128)] = ref[j, 0:PROJ_ROWS, :].astype(F32)
            at = pl.multiple_of(half * 128, 128)
            gram_ref[j * GRAM_ROWS : (j + 1) * GRAM_ROWS, pl.ds(at, 128)] = (
                ref[j, PROJ_ROWS:SUM_ROWS, :].astype(F32)
            )


def both_ways(pairs):
    return [p for i, j in pairs for p in ((i, j), (j, i))]


def local(snapshots, coefficients, modes):
    members, levels, rows_x, rows_y, frames = snapshots.shape
    width = modes.shape[3]
    cells = rows_x * rows_y
    local_cells = levels * cells
    n_sx, n_z = lax.axis_size(SX), lax.axis_size(SY)
    total_cells = local_cells * n_sx * n_z
    core = lax.axis_index("c").astype(jnp.int32)
    parity = lax.axis_index("zl").astype(jnp.int32)
    part = lax.axis_index(GROUP).astype(jnp.int32)
    x_at, z_at = lax.axis_index(SX), lax.axis_index(SY)
    place = core + 2 * parity + 4 * part
    for i, end in enumerate((x_at == 0, x_at == n_sx - 1, z_at == 0, z_at == n_z - 1)):
        place = place + end.astype(jnp.int32) * (64 << i)
    place = place.reshape(1)
    series = snapshots.reshape(members, levels, cells, frames)
    swap = [(0, 1), (1, 0)]

    g0, coefficients, x0, edge_b = first_grad(place, modes, coefficients, series)
    got0 = lax.ppermute(g0, "ens", swap)
    xb = lax.ppermute(edge_b, SX, both_ways([(i, (i + 1) % n_sx) for i in range(1, n_sx, 2)]))
    g1, x1 = second_grad(modes, coefficients, series, 1)
    got1 = lax.ppermute(g1, "ens", swap)
    coefficients, _ = lax.optimization_barrier((coefficients, g1))
    g2, g3, modes, series, edge_a, row_a, row_b = rest_grad(place, modes, coefficients, series, 2)
    got2 = lax.ppermute(g2, "ens", swap)
    got3 = lax.ppermute(g3, "ens", swap)
    got0, got1, row_a, row_b = lax.optimization_barrier((got0, got1, row_a, row_b))
    za = lax.ppermute(row_a, SY, both_ways([(i, i + 1) for i in range(0, n_z, 2)]))
    zb = lax.ppermute(row_b, SY, both_ways([(i, (i + 1) % n_z) for i in range(1, n_z, 2)]))
    xb, edge_a, za, zb = lax.optimization_barrier((xb, edge_a, za, zb))
    xa = lax.ppermute(edge_a, "c", swap)
    moved, keep, send = steps(
        place,
        modes,
        (xa, xb, za, zb),
        (g0, g1, g2, g3),
        (got0, got1, got2, got3),
        (x0, x1, series, series),
    )

    part_shape = jax.ShapeDtypeStruct((PARTS, PART_ROWS, 128), BF16)
    other = lax.ppermute(send, "c", swap)
    joined = pl.pallas_call(
        join_kernel, in_specs=[VM, VM], out_specs=VM, out_shape=part_shape, compiler_params=PARAMS
    )(keep, other)
    parts = lax.all_to_all(joined, GROUP, 0, 0)
    line_shape = jax.ShapeDtypeStruct((PART_ROWS, 128), BF16)
    line = pl.pallas_call(
        group_kernel, in_specs=[VM], out_specs=VM, out_shape=line_shape, compiler_params=PARAMS
    )(parts)
    pairs = lax.axis_size("zh")
    near = lax.ppermute(line, "zh", [(i, i ^ 1) for i in range(pairs)])
    line = pl.pallas_call(
        add_kernel, in_specs=[VM, VM], out_specs=VM, out_shape=line_shape, compiler_params=PARAMS
    )(line, near)
    near = lax.ppermute(line, "zh", [(i, i ^ 3) for i in range(pairs)])
    spread, shrink = pl.pallas_call(
        functools.partial(reduce_kernel, total_cells),
        in_specs=[SM, VM, VM],
        out_specs=[VM, VM],
        out_shape=[
            jax.ShapeDtypeStruct((PARTS, SUM_ROWS, 128), BF16),
            jax.ShapeDtypeStruct((2, 128), F32),
        ],
        scratch_shapes=[pltpu.VMEM((width, 128), F32)],
        compiler_params=PARAMS,
    )(place, line, near)
    half = lax.all_to_all(spread, GROUP, 0, 0)
    new_modes = pl.pallas_call(
        scale_kernel,
        in_specs=[VM] * (1 + len(moved)),
        out_specs=VM,
        out_shape=jax.ShapeDtypeStruct((local_cells, width), BF16),
        compiler_params=PARAMS,
    )(shrink, *moved)
    other_half = lax.ppermute(half, "c", swap)
    projected, gram = pl.pallas_call(
        final_kernel,
        in_specs=[SM, VM, VM],
        out_specs=[VM, VM],
        out_shape=[
            jax.ShapeDtypeStruct((members, width, frames), F32),
            jax.ShapeDtypeStruct((width, width), F32),
        ],
        compiler_params=PARAMS,
    )(place, half, other_half)
    return (new_modes.reshape(levels, rows_x, rows_y, width), gram, projected)


def solution(mesh):
    ens, n_sx, n_sy = (mesh.shape[a] for a in ("ens", "sx", "sy"))
    fine = Mesh(mesh.devices.reshape(ens, 2, n_sx // 4, 2, n_sy // 2, 2), ("ens", *SX, *SY))
    in_specs = (P("ens", None, SX, SY, None), P("ens", None, None), P(None, SX, SY, None))
    out_specs = (P(None, SX, SY, None), P(), P("ens", None, None))
    return jax.shard_map(local, mesh=fine, in_specs=in_specs, out_specs=out_specs, check_vma=False)
```

```python
import functools
import math

import jax
import jax.numpy as jnp
from jax import lax
from jax.experimental import pallas as pl
from jax.experimental.pallas import tpu as pltpu
from jax.sharding import Mesh, PartitionSpec as P

ETA = 0.25
LAM = 0.5
TAU = 0.4

F32 = jnp.float32
BF16 = jnp.bfloat16
VMEM_LIMIT = 40 * 1024 * 1024
PARAMS = pltpu.CompilerParams(vmem_limit_bytes=VMEM_LIMIT)

SX = ("xh", "y", "c")
SY = ("zh", "zl")
GROUP = ("xh", "y", "zl")
PARTS = 16
PROJ_ROWS = 64
GRAM_ROWS = 16
SUM_ROWS = PROJ_ROWS + GRAM_ROWS
PART_ROWS = SUM_ROWS + 8

VM = pl.BlockSpec(memory_space=pltpu.VMEM)
SM = pl.BlockSpec(memory_space=pltpu.SMEM)
HBM = pl.BlockSpec(memory_space=pltpu.HBM)


def core_of(place):
    return place & 1


def parity_of(place):
    return (place >> 1) & 1


def part_of(place):
    return (place >> 2) & 15


def at_end(place, which):
    return ((place >> (6 + which)) & 1) == 1


def gradient(m, coefficients, series):
    acc = None
    for e in range(len(coefficients)):
        c = coefficients[e]()
        fitted = jnp.dot(m, c, preferred_element_type=F32)
        misfit = (fitted - series[e]().astype(F32)).astype(BF16)
        term = lax.dot_general(misfit, c, (((1,), (1,)), ((), ())), preferred_element_type=F32)
        acc = term if acc is None else acc + term
    return acc.astype(BF16)


def start_all(copies, sems):
    copies = [pltpu.make_async_copy(s, d, sems.at[i]) for i, (s, d) in enumerate(copies)]
    for copy in copies:
        copy.start()
    return copies


def after(copy, ref, *at):
    def load():
        copy.wait()
        return ref[at].reshape(-1, ref.shape[-1])

    return load


def first_grad_kernel(at_ref, m_hbm, c_hbm, x_hbm, g_ref, c_ref, x_ref, xb_ref, m_ref, sems):
    members = c_hbm.shape[0]
    last = m_hbm.shape[1] - 1
    copies = [(m_hbm.at[0], m_ref)]
    for e in range(members):
        copies.append((c_hbm.at[e], c_ref.at[e]))
        copies.append((x_hbm.at[e, 0], x_ref.at[e]))
    copies.append((m_hbm.at[:, last * core_of(at_ref[0])], xb_ref))
    copies = start_all(copies, sems)
    copies[0].wait()
    g_ref[...] = gradient(
        m_ref[...].reshape(g_ref.shape),
        [after(copies[1 + 2 * e], c_ref, e) for e in range(members)],
        [after(copies[2 + 2 * e], x_ref, e) for e in range(members)],
    )
    copies[-1].wait()


def second_grad_kernel(level, m_hbm, c_ref, x_hbm, g_ref, x_ref, m_ref, sems):
    members = c_ref.shape[0]
    copies = [(m_hbm.at[level], m_ref)]
    for e in range(members):
        copies.append((x_hbm.at[e, level], x_ref.at[e]))
    copies = start_all(copies, sems)
    copies[0].wait()
    g_ref[...] = gradient(
        m_ref[...].reshape(g_ref.shape),
        [functools.partial(c_ref.__getitem__, e) for e in range(members)],
        [after(copies[1 + e], x_ref, e) for e in range(members)],
    )


def rest_grad_kernel(begin, at_ref, m_hbm, c_ref, x_hbm, *refs):
    *g_refs, m_ref, x_ref, xa_ref, za_ref, zb_ref, tmp_ref, sems = refs
    members, levels, cells, _ = x_hbm.shape
    _, rows_x, rows_y, width = m_ref.shape
    copies = [(m_hbm, m_ref)]
    for level in range(begin, levels):
        for e in range(members):
            copies.append((x_hbm.at[e, level], x_ref.at[e, level - begin]))
    copies = start_all(copies, sems)
    copies[0].wait()
    core, even = core_of(at_ref[0]), parity_of(at_ref[0]) == 0
    xa_ref[...] = m_ref[:, (rows_x - 1) * (1 - core)]
    tmp_ref[0] = m_ref[:, :, 0:8, :].reshape(levels * rows_x, 8, width).astype(F32)
    tmp_ref[1] = m_ref[:, :, rows_y - 8 : rows_y, :].reshape(levels * rows_x, 8, width).astype(F32)
    lo, hi = tmp_ref[0, :, 0, :], tmp_ref[1, :, 7, :]
    za_ref[...] = jnp.where(even, hi, lo).astype(BF16)
    zb_ref[...] = jnp.where(even, lo, hi).astype(BF16)
    for i, g_ref in enumerate(g_refs):
        g_ref[...] = gradient(
            m_ref[begin + i].reshape(g_ref.shape),
            [functools.partial(c_ref.__getitem__, e) for e in range(members)],
            [after(copies[1 + i * members + e], x_ref, e, i) for e in range(members)],
        )


def grad_cost(members, cells, frames, width):
    return pl.CostEstimate(
        flops=4 * members * cells * frames * width,
        bytes_accessed=2 * cells * (2 * width + members * frames) + 2 * members * width * frames,
        transcendentals=0,
    )


def in_hbm(array):
    return pltpu.with_memory_space_constraint(array, pltpu.HBM)


def first_grad(place, modes, coefficients, series):
    members, _, cells, frames = series.shape
    levels, rows_x, rows_y, width = modes.shape
    outs = [
        jax.ShapeDtypeStruct((cells, width), BF16),
        pltpu.VMEM(coefficients.shape, BF16),
        pltpu.VMEM((members, cells, frames), BF16),
        jax.ShapeDtypeStruct((levels, rows_y, width), BF16),
    ]
    return pl.pallas_call(
        first_grad_kernel,
        in_specs=[SM] + [HBM] * 3,
        out_specs=[VM] * len(outs),
        out_shape=outs,
        scratch_shapes=[
            pltpu.VMEM((rows_x, rows_y, width), BF16),
            pltpu.SemaphoreType.DMA((2 + 2 * members,)),
        ],
        compiler_params=PARAMS,
        cost_estimate=grad_cost(members, cells, frames, width),
    )(place, in_hbm(modes), in_hbm(coefficients), in_hbm(series))


def second_grad(modes, coefficients, series, level):
    members, _, cells, frames = series.shape
    _, rows_x, rows_y, width = modes.shape
    outs = [jax.ShapeDtypeStruct((cells, width), BF16), pltpu.VMEM((members, cells, frames), BF16)]
    return pl.pallas_call(
        functools.partial(second_grad_kernel, level),
        in_specs=[HBM, VM, HBM],
        out_specs=[VM] * len(outs),
        out_shape=outs,
        scratch_shapes=[
            pltpu.VMEM((rows_x, rows_y, width), BF16),
            pltpu.SemaphoreType.DMA((1 + members,)),
        ],
        compiler_params=PARAMS,
        cost_estimate=grad_cost(members, cells, frames, width),
    )(in_hbm(modes), coefficients, in_hbm(series))


def rest_grad(place, modes, coefficients, series, begin):
    members, levels, cells, frames = series.shape
    _, rows_x, rows_y, width = modes.shape
    count = levels - begin
    outs = [jax.ShapeDtypeStruct((cells, width), BF16)] * count
    outs += [
        pltpu.VMEM(modes.shape, BF16),
        pltpu.VMEM((members, count, cells, frames), BF16),
        jax.ShapeDtypeStruct((levels, rows_y, width), BF16),
        jax.ShapeDtypeStruct((levels * rows_x, width), BF16),
        jax.ShapeDtypeStruct((levels * rows_x, width), BF16),
    ]
    return pl.pallas_call(
        functools.partial(rest_grad_kernel, begin),
        in_specs=[SM, HBM, VM, HBM],
        out_specs=[VM] * len(outs),
        out_shape=outs,
        scratch_shapes=[
            pltpu.VMEM((2, levels * rows_x, 8, width), F32),
            pltpu.SemaphoreType.DMA((1 + members * count,)),
        ],
        compiler_params=PARAMS,
        cost_estimate=grad_cost(members, count * cells, frames, width),
    )(place, in_hbm(modes), coefficients, in_hbm(series))


def base_of(level, place, m_ref, xa_ref, xb_ref, za_ref, zb_ref):
    _, rows_x, rows_y, width = m_ref.shape
    lower, even = core_of(place) == 0, parity_of(place) == 0
    shape = (rows_x, rows_y, width)
    f = m_ref[level].astype(F32)
    xa, xb = xa_ref[level : level + 1].astype(F32), xb_ref[level : level + 1].astype(F32)
    rows = slice(level * rows_x, (level + 1) * rows_x)
    za, zb = za_ref[rows, :].astype(F32), zb_ref[rows, :].astype(F32)
    xlo = jnp.where(at_end(place, 0), 0.0, jnp.where(lower, xb, xa))
    xhi = jnp.where(at_end(place, 1), 0.0, jnp.where(lower, xa, xb))
    zlo = jnp.where(at_end(place, 2), 0.0, jnp.where(even, zb, za))
    zhi = jnp.where(at_end(place, 3), 0.0, jnp.where(even, za, zb))
    up = jnp.concatenate([xlo, f[:-1]], axis=0)
    down = jnp.concatenate([f[1:], xhi], axis=0)
    at = lax.broadcasted_iota(jnp.int32, shape, 1)
    left = jnp.where(at == 0, jnp.broadcast_to(zlo[:, None, :], shape), pltpu.roll(f, 1, 1))
    right = jnp.where(
        at == rows_y - 1, jnp.broadcast_to(zhi[:, None, :], shape), pltpu.roll(f, rows_y - 1, 1)
    )
    bent = 4.0 * f - (down + up + right + left)
    return (f - (ETA * LAM) * bent).reshape(rows_x * rows_y, width)


def split_squares(squares, rows):
    high = squares.astype(BF16).astype(F32)
    return jnp.concatenate([high, squares - high, jnp.zeros((rows - 4, 128), F32)], axis=0)


def emit(out_ref, half, proj_ref, gram_ref, squares):
    members = proj_ref.shape[0]
    for j in range(PARTS):
        tb, m, r = j // 8, (j // 4) % members, j % 4
        at = pl.multiple_of((half * 2 + tb) * 128, 128)
        block = proj_ref[m, r * PROJ_ROWS : (r + 1) * PROJ_ROWS, pl.ds(at, 128)]
        out_ref[j, 0:PROJ_ROWS, :] = block.astype(BF16)
        at = pl.multiple_of(half * 128, 128)
        block = gram_ref[j * GRAM_ROWS : (j + 1) * GRAM_ROWS, pl.ds(at, 128)]
        out_ref[j, PROJ_ROWS:SUM_ROWS, :] = block.astype(BF16)
        out_ref[j, SUM_ROWS:PART_ROWS, :] = squares


def move(base, own_ref, got_ref):
    grad = own_ref[...].astype(F32) + got_ref[...].astype(F32)
    moved = (base - ETA * grad).astype(BF16)
    wide = moved.astype(F32)
    return moved, jnp.sum(wide * wide, axis=0, keepdims=True)


def most_kernel(at_ref, m_ref, xa_ref, xb_ref, za_ref, zb_ref, *refs):
    *refs, base_ref, moved_ref, proj_ref, gram_ref, squares_ref = refs
    halos = (xa_ref, xb_ref, za_ref, zb_ref)
    count = len(refs) // 3
    owns, gots, xs = refs[:count], refs[count : 2 * count], refs[2 * count :]
    squares = None
    for level in range(count):
        moved, part = move(base_of(level, at_ref[0], m_ref, *halos), owns[level], gots[level])
        squares = part if level == 0 else squares + part
        moved_ref[level * moved.shape[0] : (level + 1) * moved.shape[0], :] = moved
        turned = moved.T
        gram = jnp.dot(turned, moved, preferred_element_type=F32)
        gram_ref[...] = gram if level == 0 else gram_ref[...] + gram
        for e in range(proj_ref.shape[0]):
            x = xs[level][e] if len(xs[level].shape) == 3 else xs[level][e, 0]
            proj = jnp.dot(turned, x, preferred_element_type=F32)
            proj_ref[e] = proj if level == 0 else proj_ref[e] + proj
    squares_ref[...] = squares
    base_ref[...] = base_of(count, at_ref[0], m_ref, *halos)


def last_kernel(at_ref, base_ref, own_ref, got_ref, x_ref, proj_in, gram_in, squares_in, *refs):
    moved_ref, send_ref, proj_ref, gram_ref, squares_ref = refs
    moved, squares = move(base_ref[...], own_ref, got_ref)
    moved_ref[...] = moved
    squares = squares + squares_in[...]
    turned = moved.T
    gram_ref[...] = gram_in[...] + jnp.dot(turned, moved, preferred_element_type=F32)
    for e in range(proj_ref.shape[0]):
        proj = jnp.dot(turned, x_ref[e, x_ref.shape[1] - 1], preferred_element_type=F32)
        proj_ref[e] = proj_in[e] + proj
    core = core_of(at_ref[0])
    pair = jnp.concatenate([squares[:, 0:128], squares[:, 128:256]], axis=0)
    packed = split_squares(pair, 8).astype(BF16)
    emit(send_ref, 1 - core, proj_ref, gram_ref, packed)
    squares_ref[...] = squares


def step_cost(members, cells, frames, width):
    return pl.CostEstimate(
        flops=2 * cells * width * (width + members * frames),
        bytes_accessed=2 * cells * (4 * width + members * frames),
        transcendentals=0,
    )


def steps(place, modes, halos, owns, gots, series):
    members, frames = series[0].shape[0], series[0].shape[-1]
    cells, width = owns[0].shape
    most = len(owns) - 1
    sums = [
        jax.ShapeDtypeStruct((members, width, frames), F32),
        jax.ShapeDtypeStruct((width, width), F32),
        jax.ShapeDtypeStruct((1, width), F32),
    ]
    args = [modes, *halos, *owns[:most], *gots[:most], *series[:most]]
    base, moved, *carry = pl.pallas_call(
        most_kernel,
        in_specs=[SM] + [VM] * len(args),
        out_specs=[VM] * 5,
        out_shape=[
            jax.ShapeDtypeStruct((cells, width), F32),
            jax.ShapeDtypeStruct((most * cells, width), BF16),
            *sums,
        ],
        compiler_params=PARAMS,
        cost_estimate=step_cost(members, most * cells, frames, width),
    )(place, *args)
    args = [base, owns[most], gots[most], series[most], *carry]
    tail, send, *sums = pl.pallas_call(
        last_kernel,
        in_specs=[SM] + [VM] * len(args),
        out_specs=[VM] * 5,
        out_shape=[jax.ShapeDtypeStruct((cells, width), BF16)]
        + [jax.ShapeDtypeStruct((PARTS, PART_ROWS, 128), BF16), *sums],
        input_output_aliases={5: 2, 6: 3, 7: 4},
        compiler_params=PARAMS,
        cost_estimate=step_cost(members, cells, frames, width),
    )(place, *args)
    return [moved, tail], sums, send


def whole_squares(part):
    return part[SUM_ROWS : SUM_ROWS + 2, :] + part[SUM_ROWS + 2 : SUM_ROWS + 4, :]


def packed_squares(total):
    return split_squares(whole_squares(total), 8).astype(BF16)


def join_kernel(at_ref, proj_ref, gram_ref, squares_ref, got_ref, out_ref):
    core = core_of(at_ref[0])
    members, width, _ = proj_ref.shape
    squares = squares_ref[...]
    pair = jnp.concatenate([squares[:, 0:128], squares[:, 128:256]], axis=0)
    packed = split_squares(pair + whole_squares(got_ref[0].astype(F32)), 8).astype(BF16)
    for j in range(PARTS):
        tb, m, r = j // 8, (j // 4) % members, j % 4
        got = got_ref[j].astype(F32)
        at = pl.multiple_of((core * 2 + tb) * 128, 128)
        block = proj_ref[m, r * PROJ_ROWS : (r + 1) * PROJ_ROWS, pl.ds(at, 128)]
        out_ref[j, 0:PROJ_ROWS, :] = (block + got[0:PROJ_ROWS, :]).astype(BF16)
        at = pl.multiple_of(core * 128, 128)
        block = gram_ref[j * GRAM_ROWS : (j + 1) * GRAM_ROWS, pl.ds(at, 128)]
        out_ref[j, PROJ_ROWS:SUM_ROWS, :] = (block + got[PROJ_ROWS:SUM_ROWS, :]).astype(BF16)
        out_ref[j, SUM_ROWS:PART_ROWS, :] = packed


def group_kernel(in_ref, out_ref):
    total = in_ref[0].astype(F32)
    for j in range(1, PARTS):
        total = total + in_ref[j].astype(F32)
    out_ref[0:SUM_ROWS, :] = total[0:SUM_ROWS, :].astype(BF16)
    out_ref[SUM_ROWS:PART_ROWS, :] = packed_squares(total)


def add_kernel(own_ref, got_ref, out_ref):
    total = own_ref[...].astype(F32) + got_ref[...].astype(F32)
    out_ref[0:SUM_ROWS, :] = total[0:SUM_ROWS, :].astype(BF16)
    out_ref[SUM_ROWS:PART_ROWS, :] = packed_squares(total)


def reduce_kernel(total_cells, at_ref, own_ref, got_ref, out_ref, shrink_ref, column_ref):
    core, part = core_of(at_ref[0]), part_of(at_ref[0])
    total = own_ref[...].astype(F32) + got_ref[...].astype(F32)
    squares = whole_squares(total)
    shrink = jnp.maximum(0.0, 1.0 - TAU / jnp.sqrt(squares / total_cells + 1e-06))
    shrink_ref[...] = shrink
    for k in range(2):
        column_ref[k * 128 : (k + 1) * 128, :] = jnp.broadcast_to(shrink[k : k + 1, :], (128, 128)).T
    at = pl.multiple_of((part & 3) * PROJ_ROWS, PROJ_ROWS)
    proj = column_ref[pl.ds(at, PROJ_ROWS), :] * total[0:PROJ_ROWS, :] * (1.0 / math.sqrt(total_cells))
    at = pl.multiple_of(part * GRAM_ROWS, GRAM_ROWS)
    lanes = jnp.where(core == 0, shrink[0:1, :], shrink[1:2, :])
    gram = column_ref[pl.ds(at, GRAM_ROWS), :] * total[PROJ_ROWS:SUM_ROWS, :] * lanes * (1.0 / total_cells)
    mine = jnp.concatenate([proj, gram], axis=0).astype(BF16)
    for j in range(PARTS):
        out_ref[j] = mine


def scale_kernel(shrink_ref, *refs):
    out_ref = refs[-1]
    at = 0
    for m_ref in refs[:-1]:
        rows = slice(at, at + m_ref.shape[0])
        at = rows.stop
        for k in range(2):
            lanes = slice(k * 128, (k + 1) * 128)
            out_ref[rows, lanes] = (m_ref[:, lanes].astype(F32) * shrink_ref[k : k + 1, :]).astype(BF16)


def final_kernel(at_ref, own_ref, got_ref, proj_ref, gram_ref):
    core = core_of(at_ref[0])
    members = proj_ref.shape[0]
    for ref, half in ((own_ref, core), (got_ref, 1 - core)):
        for j in range(PARTS):
            tb, m, r = j // 8, (j // 4) % members, j % 4
            at = pl.multiple_of((half * 2 + tb) * 128, 128)
            rows = slice(r * PROJ_ROWS, (r + 1) * PROJ_ROWS)
            proj_ref[m, rows, pl.ds(at, 128)] = ref[j, 0:PROJ_ROWS, :].astype(F32)
            at = pl.multiple_of(half * 128, 128)
            gram_ref[j * GRAM_ROWS : (j + 1) * GRAM_ROWS, pl.ds(at, 128)] = (
                ref[j, PROJ_ROWS:SUM_ROWS, :].astype(F32)
            )


def both_ways(pairs):
    return [p for i, j in pairs for p in ((i, j), (j, i))]


def local(snapshots, coefficients, modes):
    members, levels, rows_x, rows_y, frames = snapshots.shape
    width = modes.shape[3]
    cells = rows_x * rows_y
    local_cells = levels * cells
    n_sx, n_z = lax.axis_size(SX), lax.axis_size(SY)
    total_cells = local_cells * n_sx * n_z
    core = lax.axis_index("c").astype(jnp.int32)
    parity = lax.axis_index("zl").astype(jnp.int32)
    part = lax.axis_index(GROUP).astype(jnp.int32)
    x_at, z_at = lax.axis_index(SX), lax.axis_index(SY)
    place = core + 2 * parity + 4 * part
    for i, end in enumerate((x_at == 0, x_at == n_sx - 1, z_at == 0, z_at == n_z - 1)):
        place = place + end.astype(jnp.int32) * (64 << i)
    place = place.reshape(1)
    series = snapshots.reshape(members, levels, cells, frames)
    swap = [(0, 1), (1, 0)]

    g0, coefficients, x0, edge_b = first_grad(place, modes, coefficients, series)
    got0 = lax.ppermute(g0, "ens", swap)
    xb = lax.ppermute(edge_b, SX, both_ways([(i, (i + 1) % n_sx) for i in range(1, n_sx, 2)]))
    g1, x1 = second_grad(modes, coefficients, series, 1)
    got1 = lax.ppermute(g1, "ens", swap)
    coefficients, _ = lax.optimization_barrier((coefficients, g1))
    g2, g3, modes, series, edge_a, row_a, row_b = rest_grad(place, modes, coefficients, series, 2)
    got2 = lax.ppermute(g2, "ens", swap)
    got3 = lax.ppermute(g3, "ens", swap)
    got0, got1, row_a, row_b = lax.optimization_barrier((got0, got1, row_a, row_b))
    za = lax.ppermute(row_a, SY, both_ways([(i, i + 1) for i in range(0, n_z, 2)]))
    zb = lax.ppermute(row_b, SY, both_ways([(i, (i + 1) % n_z) for i in range(1, n_z, 2)]))
    xb, edge_a, za, zb = lax.optimization_barrier((xb, edge_a, za, zb))
    xa = lax.ppermute(edge_a, "c", swap)
    moved, sums, send = steps(
        place,
        modes,
        (xa, xb, za, zb),
        (g0, g1, g2, g3),
        (got0, got1, got2, got3),
        (x0, x1, series, series),
    )

    part_shape = jax.ShapeDtypeStruct((PARTS, PART_ROWS, 128), BF16)
    other = lax.ppermute(send, "c", swap)
    joined = pl.pallas_call(
        join_kernel, in_specs=[SM] + [VM] * 4, out_specs=VM, out_shape=part_shape, compiler_params=PARAMS
    )(place, *sums, other)
    parts = lax.all_to_all(joined, GROUP, 0, 0)
    line_shape = jax.ShapeDtypeStruct((PART_ROWS, 128), BF16)
    line = pl.pallas_call(
        group_kernel, in_specs=[VM], out_specs=VM, out_shape=line_shape, compiler_params=PARAMS
    )(parts)
    pairs = lax.axis_size("zh")
    near = lax.ppermute(line, "zh", [(i, i ^ 1) for i in range(pairs)])
    line = pl.pallas_call(
        add_kernel, in_specs=[VM, VM], out_specs=VM, out_shape=line_shape, compiler_params=PARAMS
    )(line, near)
    near = lax.ppermute(line, "zh", [(i, i ^ 3) for i in range(pairs)])
    spread, shrink = pl.pallas_call(
        functools.partial(reduce_kernel, total_cells),
        in_specs=[SM, VM, VM],
        out_specs=[VM, VM],
        out_shape=[
            jax.ShapeDtypeStruct((PARTS, SUM_ROWS, 128), BF16),
            jax.ShapeDtypeStruct((2, 128), F32),
        ],
        scratch_shapes=[pltpu.VMEM((width, 128), F32)],
        compiler_params=PARAMS,
    )(place, line, near)
    half = lax.all_to_all(spread, GROUP, 0, 0)
    new_modes = pl.pallas_call(
        scale_kernel,
        in_specs=[VM] * (1 + len(moved)),
        out_specs=VM,
        out_shape=jax.ShapeDtypeStruct((local_cells, width), BF16),
        compiler_params=PARAMS,
    )(shrink, *moved)
    other_half = lax.ppermute(half, "c", swap)
    projected, gram = pl.pallas_call(
        final_kernel,
        in_specs=[SM, VM, VM],
        out_specs=[VM, VM],
        out_shape=[
            jax.ShapeDtypeStruct((members, width, frames), F32),
            jax.ShapeDtypeStruct((width, width), F32),
        ],
        compiler_params=PARAMS,
    )(place, half, other_half)
    return (new_modes.reshape(levels, rows_x, rows_y, width), gram, projected)


def solution(mesh):
    ens, n_sx, n_sy = (mesh.shape[a] for a in ("ens", "sx", "sy"))
    fine = Mesh(mesh.devices.reshape(ens, 2, n_sx // 4, 2, n_sy // 2, 2), ("ens", *SX, *SY))
    in_specs = (P("ens", None, SX, SY, None), P("ens", None, None), P(None, SX, SY, None))
    out_specs = (P(None, SX, SY, None), P(), P("ens", None, None))
    return jax.shard_map(local, mesh=fine, in_specs=in_specs, out_specs=out_specs, check_vma=False)
```
